128 devices in a mesh: row: 8 (over z_hi, y), col: 16 (over z_lo, x, core).
Axes of the slice: x: 4, y: 4, z: 4 (z_hi: 2, z_lo: 2; z = z_hi * 2 + z_lo), core: 2. Of those that a mesh axis runs over, the one named last changes fastest.
Arguments:
- features: bfloat16 [16, 2048, 4096], P(None, 'row', 'col'), may hold values from -6 to 6
- conv_weight: bfloat16 [3, 16, 3, 3], replicated, may hold values from -0.5 to 0.5
- bias: float32 [3], replicated, may hold values from -3 to 3
- inv_wavelength: float32 [3], replicated, may hold values from 12 to 18
- distance: float32 [1], replicated, may hold values from 16000 to 32000
Outputs:
- propagated: bfloat16 [3, 2, 2048, 4096], P(None, None, ('row', 'col'))
The draws below stay inside these ranges and needn't reach their ends.
All inputs are finite; a program needn't handle non-finite values.
Results may differ from the reference program's by a relative error of at most 0.0025.
Values may be sent and summed in bfloat16 or wider, within the bound.
A program may use at most 128 MiB of HBM per device.

```python
import math
import jax
import jax.numpy as jnp
from jax import lax

CH = 16
COLORS = 3
NX = 2048
NY = 4096


def levels(rng, shape, shards, smallest, top_value):
    factor_of, own = 1.0, jax.random.fold_in(rng, 6)
    for dim, blocks in shards:
        steps = jnp.exp(jax.random.uniform(jax.random.fold_in(own, dim), (blocks,), jnp.float32, smallest / len(shards), top_value / len(shards)))
        factor_of = factor_of * jnp.repeat(steps, shape[dim] // blocks).reshape([-1 if axis == dim else 1 for axis in range(len(shape))])
    return factor_of


def gaussian(stream_key, shape, spread, most, cuts=(), kind=jnp.bfloat16):
    array = spread * jax.random.normal(stream_key, shape, jnp.float32)
    if cuts:
        array = array * levels(stream_key, shape, cuts, -0.22, 0.18)
    return jnp.clip(array, -most, most).astype(kind)


def setup_inputs(seed: int = 0) -> dict:
    key_list = jax.random.split(jax.random.key(seed), 6)
    features = gaussian(key_list[0], (CH, NX, NY), 1.0, 6.0, ((1, 8), (2, 16)))
    conv_weight = gaussian(key_list[1], (COLORS, CH, 3, 3), (CH * 9) ** -0.5, 0.5)
    bias = gaussian(key_list[2], (COLORS,), 0.5, 3.0, (), jnp.float32)
    inv_wavelength = jnp.clip(jnp.exp(jax.random.uniform(key_list[3], (COLORS,), jnp.float32, math.log(12.0), math.log(18.0))), 12.0, 18.0)
    distance = jnp.clip(jax.random.uniform(key_list[4], (1,), jnp.float32, 16000.0, 32000.0), 16000.0, 32000.0)
    return {"features": features, "conv_weight": conv_weight, "bias": bias, "inv_wavelength": inv_wavelength, "distance": distance}


def phase_delay(freq_x, freq_y, grid_height, grid_width, wave_inv, travel):
    signed_x = jnp.where(freq_x < grid_height // 2, freq_x, freq_x - grid_height).astype(jnp.float32) / grid_height
    signed_y = jnp.where(freq_y < grid_width // 2, freq_y, freq_y - grid_width).astype(jnp.float32) / grid_width
    squared = signed_x * signed_x + signed_y * signed_y
    factor = 2.0 * math.pi * travel
    return factor * squared / (wave_inv + jnp.sqrt(wave_inv * wave_inv - squared))

def reference(features, conv_weight, bias, inv_wavelength, distance):
    score = lax.conv_general_dilated(features[None], conv_weight, (1, 1), 'SAME', dimension_numbers=('NCHW', 'OIHW', 'NCHW'), preferred_element_type=jnp.float32)[0]
    phase = math.pi * jnp.tanh(score + bias[:, None, None])
    grid_height = phase.shape[1]
    grid_width = phase.shape[2]
    freq_x = jnp.arange(grid_height, dtype=jnp.int32)[:, None]
    freq_y = jnp.arange(grid_width, dtype=jnp.int32)[None, :]
    results = []
    for color_index in range(phase.shape[0]):
        field = lax.complex(jnp.cos(phase[color_index]), jnp.sin(phase[color_index]))
        delay = phase_delay(freq_x, freq_y, grid_height, grid_width, inv_wavelength[color_index], distance[0])
        transfer = lax.complex(jnp.cos(delay), -jnp.sin(delay))
        propagated_field = jnp.fft.ifft2(jnp.fft.fft2(field) * transfer)
        results.append(jnp.stack((jnp.real(propagated_field), jnp.imag(propagated_field)), 0).astype(jnp.bfloat16))
    return jnp.stack(results, 0)
```

```python
import functools
import math

import jax
import jax.numpy as jnp
import numpy as np
from jax import lax
from jax.experimental import pallas as pl
from jax.experimental.pallas import tpu as pltpu
from jax.sharding import PartitionSpec as P

F32 = jnp.float32
BF16 = jnp.bfloat16
VMEM_LIMIT = 56 * 1024 * 1024


def split_np(table):
    hi = table.astype(np.float32).astype(jnp.bfloat16)
    lo = (table - hi.astype(np.float64)).astype(np.float32).astype(jnp.bfloat16)
    return np.stack([np.asarray(hi), np.asarray(lo)])


def rotation_np(theta):
    return np.array([[np.cos(theta), np.sin(theta)], [-np.sin(theta), np.cos(theta)]])


def tables():
    k2 = np.arange(256)
    b = np.arange(256)
    rot = rotation_np(2.0 * np.pi * ((k2[:, None] * b[None, :]) % 256) / 256.0)
    forward_y = rot.reshape(2, 2, 64, 4, 256).transpose(2, 0, 3, 1, 4).reshape(512, 512)
    inverse_y = forward_y.T
    j = np.arange(16)
    rot16 = rotation_np(2.0 * np.pi * ((j[:, None] * j[None, :]) % 16) / 16.0)
    back16 = np.stack([np.stack([rot16[0, 0], -rot16[0, 1]]), np.stack([-rot16[1, 0], rot16[1, 1]])])
    spread16 = np.einsum("pqjk,rs->pjrqks", back16, np.eye(16)).reshape(512, 512)
    lanes = np.einsum("pqab,cd->qcbpda", rot16, np.eye(8)).reshape(256, 256)
    lanes_back = np.einsum("pqab,cd->qcbpda", back16, np.eye(8)).reshape(256, 256)
    k1 = np.arange(16)
    angle = 2.0 * np.pi * ((k1[:, None] * b[None, :]) % 4096) / 4096.0
    twist_y = np.stack([np.cos(angle), -np.sin(angle)]).astype(np.float32)
    twist_back = np.stack([np.cos(angle.T), np.sin(angle.T)])
    twist_back = np.repeat(twist_back, 16, axis=2).astype(np.float32)
    p = np.arange(128).reshape(64, 2)
    r = np.arange(16)
    angle = 2.0 * np.pi * ((p[:, :, None] * r) % 2048) / 2048.0
    twist_x = np.stack([np.cos(angle), -np.sin(angle)])
    twist_x = np.broadcast_to(twist_x[:, :, :, None, None, :], (2, 64, 2, 4, 8, 16))
    twist_x = twist_x.reshape(2, 64, 8, 128).astype(np.float32)
    return {
        "forward_y": split_np(forward_y * 8.0),
        "inverse_y": split_np(inverse_y * 2.0**-10),
        "spread16": split_np(spread16),
        "lanes": split_np(lanes),
        "lanes_back": split_np(lanes_back * 2.0**-16),
        "twist_y": twist_y,
        "twist_back": twist_back,
        "twist_x": twist_x,
    }


def encode(x):
    x = x * jnp.abs(x)
    x = x * jnp.abs(x)
    x = x * jnp.abs(x)
    return x.astype(BF16)


def decode(y):
    y = y.astype(F32)
    root = jnp.sqrt(jnp.sqrt(jnp.sqrt(jnp.abs(y))))
    return jnp.where(y < 0.0, -root, root)


def split(x):
    hi = x.astype(BF16)
    return hi, (x - hi.astype(F32)).astype(BF16)


def cos_sin_quarters(u):
    n = jnp.round(u)
    f = u - n
    n = n.astype(jnp.int32)
    z = f * f
    s = f * (1.5707963267948966 + z * (-0.6459640975062462 + z * (0.07969262624616703 + z * (-0.004681754135318688 + z * 0.00016044118478735982))))
    c = 1.0 + z * (-1.2337005501361697 + z * (0.253669507901048 + z * (-0.020863480763352960 + z * (0.0009192602748394265 - z * 2.5202042373060605e-05))))
    swap = (n & 1) == 1
    cos = jnp.where(swap, s, c)
    sin = jnp.where(swap, c, s)
    cos = jnp.where(((n + 1) & 2) == 2, -cos, cos)
    sin = jnp.where((n & 2) == 2, -sin, sin)
    return cos, sin


def fft4(x, sign):
    (ar, ai), (br, bi), (cr, ci), (dr, di) = x
    sr, si, tr, ti = ar + cr, ai + ci, ar - cr, ai - ci
    ur, ui, vr, vi = br + dr, bi + di, br - dr, bi - di
    if sign < 0:
        vr, vi = vi, -vr
    else:
        vr, vi = -vi, vr
    return [(sr + ur, si + ui), (tr + vr, ti + vi), (sr - ur, si - ui), (tr - vr, ti - vi)]


def scaled(x, angle):
    turn = angle / (0.5 * math.pi)
    xr, xi = x
    if abs(turn - round(turn)) < 1e-9:
        case = int(round(turn)) % 4
        return [(xr, xi), (-xi, xr), (-xr, -xi), (xi, -xr)][case]
    c, s = math.cos(angle), math.sin(angle)
    eighth = turn * 2
    if abs(eighth - round(eighth)) < 1e-9:
        case = int(round(eighth)) % 8
        h = math.sqrt(0.5)
        if case == 1:
            return ((xr - xi) * h, (xr + xi) * h)
        if case == 3:
            return ((xr + xi) * -h, (xr - xi) * h)
        if case == 5:
            return ((xi - xr) * h, (xr + xi) * -h)
        return ((xr + xi) * h, (xi - xr) * h)
    return (xr * c - xi * s, xr * s + xi * c)


def fft8(x, sign):
    even = fft4(x[0::2], sign)
    odd = fft4(x[1::2], sign)
    odd = [scaled(v, sign * 2.0 * math.pi * k / 8) for k, v in enumerate(odd)]
    first = [(a[0] + b[0], a[1] + b[1]) for a, b in zip(even, odd)]
    return first + [(a[0] - b[0], a[1] - b[1]) for a, b in zip(even, odd)]


def fft16(x, sign):
    inner = [fft4([x[4 * n1 + n2] for n1 in range(4)], sign) for n2 in range(4)]
    out = [None] * 16
    for k1 in range(4):
        column = [scaled(inner[n2][k1], sign * 2.0 * math.pi * n2 * k1 / 16) for n2 in range(4)]
        for k2, v in enumerate(fft4(column, sign)):
            out[k1 + 4 * k2] = v
    return out


def dot3(lhs, rhs, dims):
    one = functools.partial(lax.dot_general, dimension_numbers=(dims, ((), ())), preferred_element_type=F32)
    return one(lhs[0], rhs[0]) + (one(lhs[0], rhs[1]) + one(lhs[1], rhs[0]))


NN = ((1,), (0,))
NT = ((1,), (1,))


def rows_forward_kernel(phase_ref, matrix_ref, twist_ref, out_ref, hi_ref, lo_ref):
    for half in range(2):
        cols = pl.ds(half * 128, 128)
        field = []
        for j in range(16):
            field.append(cos_sin_quarters(2.0 * decode(phase_ref[j, :, cols])))
        spectrum = fft16(field, -1.0)
        for k1 in range(16):
            re, im = spectrum[k1]
            if k1 > 0:
                c = twist_ref[0, pl.ds(k1, 1), cols]
                s = twist_ref[1, pl.ds(k1, 1), cols]
                re, im = re * c - im * s, re * s + im * c
            rows = pl.ds(k1 * 16, 16)
            for part, value in enumerate((re, im)):
                hi, lo = split(value)
                place = pl.ds(part * 256 + half * 128, 128)
                hi_ref[rows, place] = hi
                lo_ref[rows, place] = lo
    result = dot3((matrix_ref[0], matrix_ref[1]), (hi_ref[...], lo_ref[...]), NT)
    for h in range(2):
        out_ref[:, h] = encode(result[:, h * 128 : (h + 1) * 128]).reshape(64, 8, 128)


def columns_kernel(wave_ref, travel_ref, in_ref, matrix_ref, back_ref, twist_ref, out_ref, re_ref, im_ref, hi_ref, lo_ref):
    color = pl.program_id(0)
    position = lax.axis_index("row") * 16 + lax.axis_index("col")
    row = lax.broadcasted_iota(jnp.int32, (8, 128), 0)
    lane = lax.broadcasted_iota(jnp.int32, (8, 128), 1)
    top = row < 4

    def tile(ref, k):
        return ref[k, 0]

    for n2 in range(8):
        column = []
        for n1 in range(8):
            s = 8 * n1 + n2
            a, b = decode(tile(in_ref, s)), decode(tile(in_ref, s + 64))
            total, delta = a + b, a - b
            re = jnp.where(top, total, pltpu.roll(delta, 4, 0))
            im = jnp.where(top, pltpu.roll(total, 4, 0), delta)
            if s > 0:
                angle = 2.0 * math.pi * s / 128
                c = jnp.where(top, 1.0, math.cos(angle))
                w = jnp.where(top, 0.0, math.sin(angle))
                re, im = re * c + im * w, im * c - re * w
            column.append((re, im))
        for m1, v in enumerate(fft8(column, -1.0)):
            re, im = scaled(v, -2.0 * math.pi * n2 * m1 / 64)
            re_ref[m1 * 8 + n2] = re
            im_ref[m1 * 8 + n2] = im
    for m1 in range(8):
        column = [(re_ref[m1 * 8 + n2], im_ref[m1 * 8 + n2]) for n2 in range(8)]
        points = fft8(column, -1.0)
        for pair in range(0, 8, 1):
            place = m1 + 8 * pair
            re, im = points[pair]
            c, w = twist_ref[0, place], twist_ref[1, place]
            re, im = re * c - im * w, re * w + im * c
            hi_re, lo_re = split(re)
            hi_im, lo_im = split(im)
            hi_ref[place, :, :128] = hi_re
            hi_ref[place, :, 128:] = hi_im
            lo_ref[place, :, :128] = lo_re
            lo_ref[place, :, 128:] = lo_im
    data = (hi_ref[...].reshape(512, 256), lo_ref[...].reshape(512, 256))
    spectrum = dot3(data, (matrix_ref[0], matrix_ref[1]), NN).reshape(64, 8, 256)
    wave = wave_ref[color]
    travel = travel_ref[0]
    base_x = (row // 4) + 128 * (lane % 16)
    freq_y = 8 * (position % 2) + lane // 16 + 16 * (4 * (position // 2) + row % 4)
    signed_y = jnp.where(freq_y < 2048, freq_y, freq_y - 4096).astype(F32) * (1.0 / 4096)
    square_y = signed_y * signed_y
    for place in range(64):
        freq_x = base_x + 2 * place
        signed_x = jnp.where(freq_x < 1024, freq_x, freq_x - 2048).astype(F32) * (1.0 / 2048)
        squared = signed_x * signed_x + square_y
        turns = travel * squared / (wave + jnp.sqrt(wave * wave - squared))
        c, w = cos_sin_quarters(4.0 * turns)
        re, im = spectrum[place, :, :128], spectrum[place, :, 128:]
        re, im = re * c + im * w, im * c - re * w
        hi_re, lo_re = split(re)
        hi_im, lo_im = split(im)
        hi_ref[place, :, :128] = hi_re
        hi_ref[place, :, 128:] = hi_im
        lo_ref[place, :, :128] = lo_re
        lo_ref[place, :, 128:] = lo_im
    data = (hi_ref[...].reshape(512, 256), lo_ref[...].reshape(512, 256))
    spectrum = dot3(data, (back_ref[0], back_ref[1]), NN).reshape(64, 8, 256)
    for m1 in range(8):
        column = []
        for m2 in range(8):
            place = m1 + 8 * m2
            re, im = spectrum[place, :, :128], spectrum[place, :, 128:]
            c, w = twist_ref[0, place], twist_ref[1, place]
            column.append((re * c + im * w, im * c - re * w))
        for n2, v in enumerate(fft8(column, 1.0)):
            re, im = scaled(v, 2.0 * math.pi * n2 * m1 / 64)
            re_ref[m1 * 8 + n2] = re
            im_ref[m1 * 8 + n2] = im
    for n2 in range(8):
        column = [(re_ref[m1 * 8 + n2], im_ref[m1 * 8 + n2]) for m1 in range(8)]
        for n1, (re, im) in enumerate(fft8(column, 1.0)):
            s = 8 * n1 + n2
            if s > 0:
                angle = 2.0 * math.pi * s / 128
                c = jnp.where(top, 1.0, math.cos(angle))
                w = jnp.where(top, 0.0, math.sin(angle))
                re, im = re * c - im * w, im * c + re * w
            total = jnp.where(top, re, pltpu.roll(im, 4, 0))
            delta = jnp.where(top, pltpu.roll(re, 4, 0), im)
            out_ref[s, 0] = encode(total + delta)
            out_ref[s + 64, 0] = encode(total - delta)


def rows_inverse_kernel(in_ref, matrix_ref, twist_ref, spread_ref, out_ref):
    left = decode(in_ref[:, 0]).reshape(512, 128)
    right = decode(in_ref[:, 1]).reshape(512, 128)
    data = split(jnp.concatenate([left, right], axis=1))
    value = dot3((matrix_ref[0], matrix_ref[1]), data, NN)
    re, im = value[:256], value[256:]
    c, s = twist_ref[0], twist_ref[1]
    value = jnp.concatenate([re * c - im * s, re * s + im * c], axis=1)
    result = dot3((spread_ref[0], spread_ref[1]), split(value), NT)
    for part in range(2):
        for j in range(16):
            rows = result[part * 256 + j * 16 : part * 256 + j * 16 + 16, :]
            out_ref[part, :, j * 256 : (j + 1) * 256] = rows.astype(BF16)


def whole(array):
    return pl.BlockSpec(array.shape, lambda o: (0,) * array.ndim, pipeline_mode=pl.Buffered(1))


def params():
    return pltpu.CompilerParams(dimension_semantics=("arbitrary",), vmem_limit_bytes=VMEM_LIMIT)


def rows_forward(phase, table):
    colors = phase.shape[1]
    args = (jnp.asarray(table["forward_y"]), jnp.asarray(table["twist_y"]))
    return pl.pallas_call(
        rows_forward_kernel,
        grid=(colors,),
        in_specs=[pl.BlockSpec((16, None, 16, 256), lambda o: (0, o, 0, 0)), whole(args[0]), whole(args[1])],
        out_specs=pl.BlockSpec((64, 2, None, 8, 128), lambda o: (0, 0, o, 0, 0)),
        out_shape=jax.ShapeDtypeStruct((64, 2, colors, 8, 128), BF16),
        scratch_shapes=[pltpu.VMEM((256, 512), BF16), pltpu.VMEM((256, 512), BF16)],
        compiler_params=params(),
        name="rows_forward",
    )(phase, *args)


def columns(spread, wave, travel, table):
    colors = spread.shape[1]
    args = tuple(jnp.asarray(table[k]) for k in ("lanes", "lanes_back", "twist_x"))
    block = pl.BlockSpec((128, 1, 8, 128), lambda o: (0, o, 0, 0))
    smem = pl.BlockSpec(memory_space=pltpu.SMEM)
    return pl.pallas_call(
        columns_kernel,
        grid=(colors,),
        in_specs=[smem, smem, block] + [whole(a) for a in args],
        out_specs=block,
        out_shape=jax.ShapeDtypeStruct((128, colors, 8, 128), BF16),
        scratch_shapes=[
            pltpu.VMEM((64, 8, 128), F32),
            pltpu.VMEM((64, 8, 128), F32),
            pltpu.VMEM((64, 8, 256), BF16),
            pltpu.VMEM((64, 8, 256), BF16),
        ],
        compiler_params=params(),
        name="columns",
    )(wave, travel, spread, *args)


def rows_inverse(returned, table):
    colors = returned.shape[2]
    args = tuple(jnp.asarray(table[k]) for k in ("inverse_y", "twist_back", "spread16"))
    return pl.pallas_call(
        rows_inverse_kernel,
        grid=(colors,),
        in_specs=[pl.BlockSpec((64, 2, None, 8, 128), lambda o: (0, 0, o, 0, 0))] + [whole(a) for a in args],
        out_specs=pl.BlockSpec((None, 2, 16, 4096), lambda o: (o, 0, 0, 0)),
        out_shape=jax.ShapeDtypeStruct((colors, 2, 16, 4096), BF16),
        compiler_params=params(),
        name="rows_inverse",
    )(returned, *args)


def extended(x, sides, width):
    for axis, dim in sides:
        peers, length = (lax.axis_size(axis), x.shape[dim])
        up = [(i, (i + 1) % peers) for i in range(peers - 1)]
        down = [(j, i) for i, j in up]
        last = lax.slice_in_dim(x, length - width, length, axis=dim)
        first = lax.slice_in_dim(x, 0, width, axis=dim)
        before = lax.ppermute(last, axis, up)
        after = lax.ppermute(first, axis, down)
        x = jnp.concatenate([before, x, after], axis=dim)
    return x


def head_conv(padded, conv_weight, tile_rows, tile_cols):
    score = jnp.zeros((conv_weight.shape[0], tile_rows, tile_cols), jnp.float32)
    for shift_u in range(3):
        for shift_v in range(3):
            window = padded[:, shift_u : shift_u + tile_rows, shift_v : shift_v + tile_cols]
            score = score + jnp.einsum(
                "oc,cxy->oxy",
                conv_weight[:, :, shift_u, shift_v],
                window,
                preferred_element_type=jnp.float32,
            )
    return score


def per_device(features, conv_weight, bias, inv_wavelength, distance):
    table = tables()
    tile_rows, tile_cols = features.shape[1:]
    padded = extended(features, (("row", 1), ("col", 2)), 1)
    score = head_conv(padded, conv_weight, tile_rows, tile_cols)
    coded = encode(jnp.tanh(score + bias[:, None, None]))
    coded = coded.reshape(3, 16, 16, 256).transpose(1, 0, 2, 3)
    pencils = lax.all_to_all(coded, "col", split_axis=0, concat_axis=0, tiled=True)
    packets = rows_forward(pencils, table).reshape(128, 3, 8, 128)
    spread = lax.all_to_all(packets, ("row", "col"), split_axis=0, concat_axis=0, tiled=True)
    packets = columns(spread, inv_wavelength, distance, table)
    returned = lax.all_to_all(packets, ("row", "col"), split_axis=0, concat_axis=0, tiled=True)
    return rows_inverse(returned.reshape(64, 2, 3, 8, 128), table)


def solution(mesh):
    in_specs = (P(None, "row", "col"), P(), P(), P(), P())
    out_specs = P(None, None, ("row", "col"), None)
    return jax.shard_map(
        per_device, mesh=mesh, in_specs=in_specs, out_specs=out_specs, check_vma=False
    )
```

```python
import functools
import math

import jax
import jax.numpy as jnp
import numpy as np
from jax import lax
from jax.experimental import pallas as pl
from jax.experimental.pallas import tpu as pltpu
from jax.sharding import PartitionSpec as P

F32 = jnp.float32
BF16 = jnp.bfloat16
VMEM_LIMIT = 56 * 1024 * 1024


def split_np(table):
    hi = table.astype(np.float32).astype(jnp.bfloat16)
    lo = (table - hi.astype(np.float64)).astype(np.float32).astype(jnp.bfloat16)
    return np.stack([np.asarray(hi), np.asarray(lo)])


def rotation_np(theta):
    return np.array([[np.cos(theta), np.sin(theta)], [-np.sin(theta), np.cos(theta)]])


def tables():
    k2 = np.arange(256)
    b = np.arange(256)
    rot = rotation_np(2.0 * np.pi * ((k2[:, None] * b[None, :]) % 256) / 256.0)
    forward_y = rot.reshape(2, 2, 64, 4, 256).transpose(2, 0, 3, 1, 4).reshape(512, 512)
    inverse_y = forward_y.T
    j = np.arange(16)
    rot16 = rotation_np(2.0 * np.pi * ((j[:, None] * j[None, :]) % 16) / 16.0)
    back16 = np.stack([np.stack([rot16[0, 0], -rot16[0, 1]]), np.stack([-rot16[1, 0], rot16[1, 1]])])
    spread16 = np.einsum("pqjk,rs->pjrqks", back16, np.eye(16)).reshape(512, 512)
    lanes = np.einsum("pqab,cd->qcbpda", rot16, np.eye(8)).reshape(256, 256)
    lanes_back = np.einsum("pqab,cd->qcbpda", back16, np.eye(8)).reshape(256, 256)
    k1 = np.arange(16)
    angle = 2.0 * np.pi * ((k1[:, None] * b[None, :]) % 4096) / 4096.0
    twist_y = np.stack([np.cos(angle), -np.sin(angle)]).astype(np.float32)
    twist_back = np.stack([np.cos(angle.T), np.sin(angle.T)])
    twist_back = np.repeat(twist_back, 16, axis=2).astype(np.float32)
    p = np.arange(128).reshape(64, 2)
    r = np.arange(16)
    angle = 2.0 * np.pi * ((p[:, :, None] * r) % 2048) / 2048.0
    twist_x = np.stack([np.cos(angle), -np.sin(angle)])
    twist_x = np.broadcast_to(twist_x[:, :, :, None, None, :], (2, 64, 2, 4, 8, 16))
    twist_x = twist_x.reshape(2, 64, 8, 128).astype(np.float32)
    return {
        "forward_y": split_np(forward_y * 8.0),
        "inverse_y": split_np(inverse_y * 2.0**-10),
        "spread16": split_np(spread16),
        "lanes": split_np(lanes),
        "lanes_back": split_np(lanes_back * 2.0**-16),
        "twist_y": twist_y,
        "twist_back": twist_back,
        "twist_x": twist_x,
    }


def encode(x):
    x = x * jnp.abs(x)
    x = x * jnp.abs(x)
    x = x * jnp.abs(x)
    return x.astype(BF16)


def decode(y):
    y = y.astype(F32)
    root = jnp.sqrt(jnp.sqrt(jnp.sqrt(jnp.abs(y))))
    return jnp.where(y < 0.0, -root, root)


def split(x):
    hi = x.astype(BF16)
    return hi, (x - hi.astype(F32)).astype(BF16)


def cos_sin_quarters(u):
    n = jnp.round(u)
    f = u - n
    n = n.astype(jnp.int32)
    z = f * f
    s = f * (1.5707963267948966 + z * (-0.6459640975062462 + z * (0.07969262624616703 + z * (-0.004681754135318688 + z * 0.00016044118478735982))))
    c = 1.0 + z * (-1.2337005501361697 + z * (0.253669507901048 + z * (-0.020863480763352960 + z * (0.0009192602748394265 - z * 2.5202042373060605e-05))))
    swap = (n & 1) == 1
    cos = jnp.where(swap, s, c)
    sin = jnp.where(swap, c, s)
    cos = jnp.where(((n + 1) & 2) == 2, -cos, cos)
    sin = jnp.where((n & 2) == 2, -sin, sin)
    return cos, sin


def fft4(x, sign):
    (ar, ai), (br, bi), (cr, ci), (dr, di) = x
    sr, si, tr, ti = ar + cr, ai + ci, ar - cr, ai - ci
    ur, ui, vr, vi = br + dr, bi + di, br - dr, bi - di
    if sign < 0:
        vr, vi = vi, -vr
    else:
        vr, vi = -vi, vr
    return [(sr + ur, si + ui), (tr + vr, ti + vi), (sr - ur, si - ui), (tr - vr, ti - vi)]


def scaled(x, angle):
    turn = angle / (0.5 * math.pi)
    xr, xi = x
    if abs(turn - round(turn)) < 1e-9:
        case = int(round(turn)) % 4
        return [(xr, xi), (-xi, xr), (-xr, -xi), (xi, -xr)][case]
    c, s = math.cos(angle), math.sin(angle)
    eighth = turn * 2
    if abs(eighth - round(eighth)) < 1e-9:
        case = int(round(eighth)) % 8
        h = math.sqrt(0.5)
        if case == 1:
            return ((xr - xi) * h, (xr + xi) * h)
        if case == 3:
            return ((xr + xi) * -h, (xr - xi) * h)
        if case == 5:
            return ((xi - xr) * h, (xr + xi) * -h)
        return ((xr + xi) * h, (xi - xr) * h)
    return (xr * c - xi * s, xr * s + xi * c)


def fft8(x, sign):
    even = fft4(x[0::2], sign)
    odd = fft4(x[1::2], sign)
    odd = [scaled(v, sign * 2.0 * math.pi * k / 8) for k, v in enumerate(odd)]
    first = [(a[0] + b[0], a[1] + b[1]) for a, b in zip(even, odd)]
    return first + [(a[0] - b[0], a[1] - b[1]) for a, b in zip(even, odd)]


def fft16(x, sign):
    inner = [fft4([x[4 * n1 + n2] for n1 in range(4)], sign) for n2 in range(4)]
    out = [None] * 16
    for k1 in range(4):
        column = [scaled(inner[n2][k1], sign * 2.0 * math.pi * n2 * k1 / 16) for n2 in range(4)]
        for k2, v in enumerate(fft4(column, sign)):
            out[k1 + 4 * k2] = v
    return out


def dot3(lhs, rhs, dims):
    one = functools.partial(lax.dot_general, dimension_numbers=(dims, ((), ())), preferred_element_type=F32)
    return one(lhs[0], rhs[0]) + (one(lhs[0], rhs[1]) + one(lhs[1], rhs[0]))


NN = ((1,), (0,))
NT = ((1,), (1,))


LOGICAL = pl.DeviceIdType.LOGICAL


def enter(me, free, members):
    barrier = pltpu.get_barrier_semaphore()
    row, col = me // members, me % members
    rows = 128 // members

    def signal(sem, device):
        pl.semaphore_signal(sem, inc=1, device_id=device, device_id_type=LOGICAL)

    def up():
        @pl.when(row > 0)
        def _():
            signal(barrier, col)

    def down():
        @pl.when(row > 0)
        def _():
            pl.semaphore_wait(free, 1)

        @pl.when((row == 0) & (col > 0))
        def _():
            pl.semaphore_wait(barrier, rows - 1)
            signal(barrier, 0)
            pl.semaphore_wait(free, 1)

        @pl.when(me == 0)
        def _():
            pl.semaphore_wait(barrier, rows - 1 + members - 1)

            def tell(k, carry):
                signal(free, k)
                return carry

            lax.fori_loop(1, members, tell, 0)

        @pl.when(row == 0)
        def _():
            def tell(k, carry):
                signal(free, k * members + col)
                return carry

            lax.fori_loop(1, rows, tell, 0)

    return up, down


def send_all(me, block_of, landing, send_sem, recv_sem, local_sem):
    pltpu.make_async_copy(block_of(me), landing.at[me], local_sem).start()

    def step(k, carry):
        peer = (me + k) % 128
        pltpu.make_async_remote_copy(
            src_ref=block_of(peer),
            dst_ref=landing.at[me],
            send_sem=send_sem,
            recv_sem=recv_sem,
            device_id=peer,
            device_id_type=LOGICAL,
        ).start()
        return carry

    lax.fori_loop(1, 128, step, 0)


def wait_all(landing, send_sem, recv_sem, local_sem):
    pltpu.make_async_copy(landing.at[0], landing.at[0], local_sem).wait()
    others = landing.at[pl.ds(0, 127)]
    pltpu.make_async_copy(others, others, send_sem).wait()
    pltpu.make_async_copy(others, others, recv_sem).wait()


def rows_forward(o, phase_ref, matrix_ref, twist_ref, out_ref, hi_ref, lo_ref):
    for half in range(2):
        cols = pl.ds(half * 128, 128)
        field = []
        for j in range(16):
            field.append(cos_sin_quarters(2.0 * decode(phase_ref[j, o, :, cols])))
        spectrum = fft16(field, -1.0)
        for k1 in range(16):
            re, im = spectrum[k1]
            if k1 > 0:
                c = twist_ref[0, pl.ds(k1, 1), cols]
                s = twist_ref[1, pl.ds(k1, 1), cols]
                re, im = re * c - im * s, re * s + im * c
            rows = pl.ds(k1 * 16, 16)
            for part, value in enumerate((re, im)):
                hi, lo = split(value)
                place = pl.ds(part * 256 + half * 128, 128)
                hi_ref[rows, place] = hi
                lo_ref[rows, place] = lo
    result = dot3((matrix_ref[0], matrix_ref[1]), (hi_ref[...], lo_ref[...]), NT)
    for h in range(2):
        out_ref[:, h, o] = encode(result[:, h * 128 : (h + 1) * 128]).reshape(64, 8, 128)


def transfer(o, me, wave, travel, cos_ref, sin_ref):
    row = lax.broadcasted_iota(jnp.int32, (8, 128), 0)
    lane = lax.broadcasted_iota(jnp.int32, (8, 128), 1)
    base_x = (row // 4) + 128 * (lane % 16)
    freq_y = 8 * (me % 2) + lane // 16 + 16 * (4 * (me // 2) + row % 4)
    signed_y = jnp.where(freq_y < 2048, freq_y, freq_y - 4096).astype(F32) * (1.0 / 4096)
    square_y = signed_y * signed_y

    def step(place, carry):
        freq_x = base_x + 2 * place
        signed_x = jnp.where(freq_x < 1024, freq_x, freq_x - 2048).astype(F32) * (1.0 / 2048)
        squared = signed_x * signed_x + square_y
        turns = travel * squared / (wave + jnp.sqrt(wave * wave - squared))
        c, w = cos_sin_quarters(4.0 * turns)
        cos_ref[o, place] = c
        sin_ref[o, place] = w
        return carry

    lax.fori_loop(0, 64, step, 0, unroll=4)


def put_split(place, re, im, hi_ref, lo_ref):
    for part, value in enumerate((re, im)):
        hi, lo = split(value)
        lanes = pl.ds(part * 128, 128)
        hi_ref[place, :, lanes] = hi
        lo_ref[place, :, lanes] = lo


def columns(o, in_ref, matrix_ref, back_ref, twist_ref, cos_ref, sin_ref, out_ref, re_ref, im_ref, hi_ref, lo_ref):
    row = lax.broadcasted_iota(jnp.int32, (8, 128), 0)
    top = row < 4
    for n2 in range(8):
        column = []
        for n1 in range(8):
            s = 8 * n1 + n2
            a, b = decode(in_ref[s, o]), decode(in_ref[s + 64, o])
            total, delta = a + b, a - b
            re = jnp.where(top, total, pltpu.roll(delta, 4, 0))
            im = jnp.where(top, pltpu.roll(total, 4, 0), delta)
            if s > 0:
                angle = 2.0 * math.pi * s / 128
                c = jnp.where(top, 1.0, math.cos(angle))
                w = jnp.where(top, 0.0, math.sin(angle))
                re, im = re * c + im * w, im * c - re * w
            column.append((re, im))
        for m1, v in enumerate(fft8(column, -1.0)):
            re, im = scaled(v, -2.0 * math.pi * n2 * m1 / 64)
            re_ref[m1 * 8 + n2] = re
            im_ref[m1 * 8 + n2] = im
    for m1 in range(8):
        column = [(re_ref[m1 * 8 + n2], im_ref[m1 * 8 + n2]) for n2 in range(8)]
        for m2, (re, im) in enumerate(fft8(column, -1.0)):
            place = m1 + 8 * m2
            c, w = twist_ref[0, place], twist_ref[1, place]
            put_split(place, re * c - im * w, re * w + im * c, hi_ref, lo_ref)
    data = (hi_ref[...].reshape(512, 256), lo_ref[...].reshape(512, 256))
    spectrum = dot3(data, (matrix_ref[0], matrix_ref[1]), NN).reshape(64, 8, 256)
    for place in range(64):
        c, w = cos_ref[o, place], sin_ref[o, place]
        re, im = spectrum[place, :, :128], spectrum[place, :, 128:]
        put_split(place, re * c + im * w, im * c - re * w, hi_ref, lo_ref)
    data = (hi_ref[...].reshape(512, 256), lo_ref[...].reshape(512, 256))
    spectrum = dot3(data, (back_ref[0], back_ref[1]), NN).reshape(64, 8, 256)
    for m1 in range(8):
        column = []
        for m2 in range(8):
            place = m1 + 8 * m2
            re, im = spectrum[place, :, :128], spectrum[place, :, 128:]
            c, w = twist_ref[0, place], twist_ref[1, place]
            column.append((re * c + im * w, im * c - re * w))
        for n2, v in enumerate(fft8(column, 1.0)):
            re, im = scaled(v, 2.0 * math.pi * n2 * m1 / 64)
            re_ref[m1 * 8 + n2] = re
            im_ref[m1 * 8 + n2] = im
    for n2 in range(8):
        column = [(re_ref[m1 * 8 + n2], im_ref[m1 * 8 + n2]) for m1 in range(8)]
        for n1, (re, im) in enumerate(fft8(column, 1.0)):
            s = 8 * n1 + n2
            if s > 0:
                angle = 2.0 * math.pi * s / 128
                c = jnp.where(top, 1.0, math.cos(angle))
                w = jnp.where(top, 0.0, math.sin(angle))
                re, im = re * c - im * w, im * c + re * w
            total = jnp.where(top, re, pltpu.roll(im, 4, 0))
            delta = jnp.where(top, pltpu.roll(re, 4, 0), im)
            out_ref[s, o] = encode(total + delta)
            out_ref[s + 64, o] = encode(total - delta)


def rows_inverse(o, in_ref, matrix_ref, twist_ref, spread_ref, out_ref):
    left = decode(in_ref[:, 0, o]).reshape(512, 128)
    right = decode(in_ref[:, 1, o]).reshape(512, 128)
    data = split(jnp.concatenate([left, right], axis=1))
    value = dot3((matrix_ref[0], matrix_ref[1]), data, NN)
    re, im = value[:256], value[256:]
    c, s = twist_ref[0], twist_ref[1]
    value = jnp.concatenate([re * c - im * s, re * s + im * c], axis=1)
    result = dot3((spread_ref[0], spread_ref[1]), split(value), NT)
    for part in range(2):
        for j in range(16):
            rows = result[part * 256 + j * 16 : part * 256 + j * 16 + 16, :]
            out_ref[o, part, :, j * 256 : (j + 1) * 256] = rows.astype(BF16)


def spectral_kernel(
    wave_ref, travel_ref, phase_ref, forward_ref, inverse_ref, spread_ref, lanes_ref, back_ref, twist_y_ref, twist_back_ref, twist_x_ref,
    out_ref,
    packets_ref, spread_in_ref, filtered_ref, returned_ref, cos_ref, sin_ref, re_ref, im_ref, hi_ref, lo_ref, field_hi_ref, field_lo_ref,
    free_sem, send_sems, recv_sems, local_sems,
):
    colors = phase_ref.shape[1]
    me = lax.axis_index("row") * 16 + lax.axis_index("col")
    up, down = enter(me, free_sem, 16)
    up()

    def each(body):
        def step(o, carry):
            body(o)
            return carry

        lax.fori_loop(0, colors, step, 0)

    by_pair = packets_ref.reshape(64, 2, colors, 8, 128)
    each(lambda o: rows_forward(o, phase_ref, forward_ref, twist_y_ref, by_pair, field_hi_ref, field_lo_ref))
    down()
    first = (send_sems.at[0], recv_sems.at[0], local_sems.at[0])
    second = (send_sems.at[1], recv_sems.at[1], local_sems.at[1])
    send_all(me, lambda d: packets_ref.at[d], spread_in_ref, *first)
    each(lambda o: transfer(o, me, wave_ref[o], travel_ref[0], cos_ref, sin_ref))
    wait_all(spread_in_ref, *first)
    each(lambda o: columns(o, spread_in_ref, lanes_ref, back_ref, twist_x_ref, cos_ref, sin_ref, filtered_ref, re_ref, im_ref, hi_ref, lo_ref))
    send_all(me, lambda d: filtered_ref.at[d], returned_ref, *second)
    wait_all(returned_ref, *second)
    by_pair_back = returned_ref.reshape(64, 2, colors, 8, 128)
    each(lambda o: rows_inverse(o, by_pair_back, inverse_ref, twist_back_ref, spread_ref, out_ref))


def spectral(phase, wave, travel):
    table = tables()
    colors = phase.shape[1]
    names = ("forward_y", "inverse_y", "spread16", "lanes", "lanes_back", "twist_y", "twist_back", "twist_x")
    args = [jnp.asarray(table[k]) for k in names]
    smem = pl.BlockSpec(memory_space=pltpu.SMEM)
    vmem = pl.BlockSpec(memory_space=pltpu.VMEM)
    exchange = pltpu.VMEM((128, colors, 8, 128), BF16)
    return pl.pallas_call(
        spectral_kernel,
        in_specs=[smem, smem] + [vmem] * (1 + len(args)),
        out_specs=vmem,
        out_shape=jax.ShapeDtypeStruct((colors, 2, 16, 4096), BF16),
        scratch_shapes=[
            exchange, exchange, exchange, exchange,
            pltpu.VMEM((colors, 64, 8, 128), F32),
            pltpu.VMEM((colors, 64, 8, 128), F32),
            pltpu.VMEM((64, 8, 128), F32),
            pltpu.VMEM((64, 8, 128), F32),
            pltpu.VMEM((64, 8, 256), BF16),
            pltpu.VMEM((64, 8, 256), BF16),
            pltpu.VMEM((256, 512), BF16),
            pltpu.VMEM((256, 512), BF16),
            pltpu.SemaphoreType.REGULAR,
            pltpu.SemaphoreType.DMA((2,)),
            pltpu.SemaphoreType.DMA((2,)),
            pltpu.SemaphoreType.DMA((2,)),
        ],
        compiler_params=pltpu.CompilerParams(collective_id=0, has_side_effects=True, vmem_limit_bytes=VMEM_LIMIT),
        name="spectral",
    )(wave, travel, phase, *args)


def extended(x, sides, width):
    for axis, dim in sides:
        peers, length = (lax.axis_size(axis), x.shape[dim])
        up = [(i, (i + 1) % peers) for i in range(peers - 1)]
        down = [(j, i) for i, j in up]
        last = lax.slice_in_dim(x, length - width, length, axis=dim)
        first = lax.slice_in_dim(x, 0, width, axis=dim)
        before = lax.ppermute(last, axis, up)
        after = lax.ppermute(first, axis, down)
        x = jnp.concatenate([before, x, after], axis=dim)
    return x


def head_conv(padded, conv_weight, tile_rows, tile_cols):
    score = jnp.zeros((conv_weight.shape[0], tile_rows, tile_cols), jnp.float32)
    for shift_u in range(3):
        for shift_v in range(3):
            window = padded[:, shift_u : shift_u + tile_rows, shift_v : shift_v + tile_cols]
            score = score + jnp.einsum(
                "oc,cxy->oxy",
                conv_weight[:, :, shift_u, shift_v],
                window,
                preferred_element_type=jnp.float32,
            )
    return score


def per_device(features, conv_weight, bias, inv_wavelength, distance):
    tile_rows, tile_cols = features.shape[1:]
    padded = extended(features, (("row", 1), ("col", 2)), 1)
    score = head_conv(padded, conv_weight, tile_rows, tile_cols)
    coded = encode(jnp.tanh(score + bias[:, None, None]))
    coded = coded.reshape(3, 16, 16, 256).transpose(1, 0, 2, 3)
    pencils = lax.all_to_all(coded, "col", split_axis=0, concat_axis=0, tiled=True)
    return spectral(pencils, inv_wavelength, distance)


def solution(mesh):
    in_specs = (P(None, "row", "col"), P(), P(), P(), P())
    out_specs = P(None, None, ("row", "col"), None)
    return jax.shard_map(
        per_device, mesh=mesh, in_specs=in_specs, out_specs=out_specs, check_vma=False
    )
```

```python
import functools
import math

import jax
import jax.numpy as jnp
import numpy as np
from jax import lax
from jax.experimental import pallas as pl
from jax.experimental.pallas import tpu as pltpu
from jax.sharding import PartitionSpec as P

F32 = jnp.float32
BF16 = jnp.bfloat16
VMEM_LIMIT = 56 * 1024 * 1024


def split_np(table):
    hi = table.astype(np.float32).astype(jnp.bfloat16)
    lo = (table - hi.astype(np.float64)).astype(np.float32).astype(jnp.bfloat16)
    return np.stack([np.asarray(hi), np.asarray(lo)])


def rotation_np(theta):
    return np.array([[np.cos(theta), np.sin(theta)], [-np.sin(theta), np.cos(theta)]])


def tables():
    k2 = np.arange(256)
    b = np.arange(256)
    rot = rotation_np(2.0 * np.pi * ((k2[:, None] * b[None, :]) % 256) / 256.0)
    forward_y = rot.reshape(2, 2, 64, 4, 256).transpose(2, 0, 3, 1, 4).reshape(512, 512)
    inverse_y = forward_y.T
    j = np.arange(16)
    rot16 = rotation_np(2.0 * np.pi * ((j[:, None] * j[None, :]) % 16) / 16.0)
    back16 = np.stack([np.stack([rot16[0, 0], -rot16[0, 1]]), np.stack([-rot16[1, 0], rot16[1, 1]])])
    spread16 = np.einsum("pqjk,rs->pjrqks", back16, np.eye(16)).reshape(512, 512)
    lanes = np.einsum("pqab,cd->qcbpda", rot16, np.eye(8)).reshape(256, 256)
    lanes_back = np.einsum("pqab,cd->qcbpda", back16, np.eye(8)).reshape(256, 256)
    k1 = np.arange(16)
    angle = 2.0 * np.pi * ((k1[:, None] * b[None, :]) % 4096) / 4096.0
    twist_y = np.stack([np.cos(angle), -np.sin(angle)]).astype(np.float32)
    twist_back = np.stack([np.cos(angle.T), np.sin(angle.T)])
    twist_back = np.repeat(twist_back, 16, axis=2).astype(np.float32)
    p = np.arange(128).reshape(64, 2)
    r = np.arange(16)
    angle = 2.0 * np.pi * ((p[:, :, None] * r) % 2048) / 2048.0
    twist_x = np.stack([np.cos(angle), -np.sin(angle)])
    twist_x = np.broadcast_to(twist_x[:, :, :, None, None, :], (2, 64, 2, 4, 8, 16))
    twist_x = twist_x.reshape(2, 64, 8, 128).astype(np.float32)
    return {
        "forward_y": split_np(forward_y * 8.0),
        "inverse_y": split_np(inverse_y * 2.0**-10),
        "spread16": split_np(spread16),
        "lanes": split_np(lanes),
        "lanes_back": split_np(lanes_back * 2.0**-16),
        "twist_y": twist_y,
        "twist_back": twist_back,
        "twist_x": twist_x,
    }


def encode(x):
    x = x * jnp.abs(x)
    x = x * jnp.abs(x)
    x = x * jnp.abs(x)
    return x.astype(BF16)


def decode(y):
    y = y.astype(F32)
    root = jnp.sqrt(jnp.sqrt(jnp.sqrt(jnp.abs(y))))
    return jnp.where(y < 0.0, -root, root)


def split(x):
    hi = x.astype(BF16)
    return hi, (x - hi.astype(F32)).astype(BF16)


def cos_sin_quarters(u):
    n = jnp.round(u)
    f = u - n
    n = n.astype(jnp.int32)
    z = f * f
    s = f * (1.5707963267948966 + z * (-0.6459640975062462 + z * (0.07969262624616703 + z * (-0.004681754135318688 + z * 0.00016044118478735982))))
    c = 1.0 + z * (-1.2337005501361697 + z * (0.253669507901048 + z * (-0.020863480763352960 + z * (0.0009192602748394265 - z * 2.5202042373060605e-05))))
    swap = (n & 1) == 1
    cos = jnp.where(swap, s, c)
    sin = jnp.where(swap, c, s)
    cos = jnp.where(((n + 1) & 2) == 2, -cos, cos)
    sin = jnp.where((n & 2) == 2, -sin, sin)
    return cos, sin


def fft4(x, sign):
    (ar, ai), (br, bi), (cr, ci), (dr, di) = x
    sr, si, tr, ti = ar + cr, ai + ci, ar - cr, ai - ci
    ur, ui, vr, vi = br + dr, bi + di, br - dr, bi - di
    if sign < 0:
        vr, vi = vi, -vr
    else:
        vr, vi = -vi, vr
    return [(sr + ur, si + ui), (tr + vr, ti + vi), (sr - ur, si - ui), (tr - vr, ti - vi)]


def scaled(x, angle):
    turn = angle / (0.5 * math.pi)
    xr, xi = x
    if abs(turn - round(turn)) < 1e-9:
        case = int(round(turn)) % 4
        return [(xr, xi), (-xi, xr), (-xr, -xi), (xi, -xr)][case]
    c, s = math.cos(angle), math.sin(angle)
    eighth = turn * 2
    if abs(eighth - round(eighth)) < 1e-9:
        case = int(round(eighth)) % 8
        h = math.sqrt(0.5)
        if case == 1:
            return ((xr - xi) * h, (xr + xi) * h)
        if case == 3:
            return ((xr + xi) * -h, (xr - xi) * h)
        if case == 5:
            return ((xi - xr) * h, (xr + xi) * -h)
        return ((xr + xi) * h, (xi - xr) * h)
    return (xr * c - xi * s, xr * s + xi * c)


def fft8(x, sign):
    even = fft4(x[0::2], sign)
    odd = fft4(x[1::2], sign)
    odd = [scaled(v, sign * 2.0 * math.pi * k / 8) for k, v in enumerate(odd)]
    first = [(a[0] + b[0], a[1] + b[1]) for a, b in zip(even, odd)]
    return first + [(a[0] - b[0], a[1] - b[1]) for a, b in zip(even, odd)]


def fft16(x, sign):
    inner = [fft4([x[4 * n1 + n2] for n1 in range(4)], sign) for n2 in range(4)]
    out = [None] * 16
    for k1 in range(4):
        column = [scaled(inner[n2][k1], sign * 2.0 * math.pi * n2 * k1 / 16) for n2 in range(4)]
        for k2, v in enumerate(fft4(column, sign)):
            out[k1 + 4 * k2] = v
    return out


def dot3(lhs, rhs, dims):
    one = functools.partial(lax.dot_general, dimension_numbers=(dims, ((), ())), preferred_element_type=F32)
    return one(lhs[0], rhs[0]) + (one(lhs[0], rhs[1]) + one(lhs[1], rhs[0]))


NN = ((1,), (0,))
NT = ((1,), (1,))


LOGICAL = pl.DeviceIdType.LOGICAL


def enter(me, free, members):
    barrier = pltpu.get_barrier_semaphore()
    row, col = me // members, me % members
    rows = 128 // members

    def signal(sem, device):
        pl.semaphore_signal(sem, inc=1, device_id=device, device_id_type=LOGICAL)

    def up():
        @pl.when(row > 0)
        def _():
            signal(barrier, col)

    def down():
        @pl.when(row > 0)
        def _():
            pl.semaphore_wait(free, 1)

        @pl.when((row == 0) & (col > 0))
        def _():
            pl.semaphore_wait(barrier, rows - 1)
            signal(barrier, 0)
            pl.semaphore_wait(free, 1)

        @pl.when(me == 0)
        def _():
            pl.semaphore_wait(barrier, rows - 1 + members - 1)

            def tell(k, carry):
                signal(free, k)
                return carry

            lax.fori_loop(1, members, tell, 0)

        @pl.when(row == 0)
        def _():
            def tell(k, carry):
                signal(free, k * members + col)
                return carry

            lax.fori_loop(1, rows, tell, 0)

    return up, down


def send_all(me, block_of, landing, send_sem, recv_sem, local_sem):
    pltpu.make_async_copy(block_of(me), landing.at[me], local_sem).start()

    def step(k, carry):
        peer = (me + k) % 128
        pltpu.make_async_remote_copy(
            src_ref=block_of(peer),
            dst_ref=landing.at[me],
            send_sem=send_sem,
            recv_sem=recv_sem,
            device_id=peer,
            device_id_type=LOGICAL,
        ).start()
        return carry

    lax.fori_loop(1, 128, step, 0)


def wait_all(landing, send_sem, recv_sem, local_sem):
    pltpu.make_async_copy(landing.at[0], landing.at[0], local_sem).wait()
    others = landing.at[pl.ds(0, landing.shape[0] - 1)]
    pltpu.make_async_copy(others, others, send_sem).wait()
    pltpu.make_async_copy(others, others, recv_sem).wait()


def rows_forward(o, phase_ref, matrix_ref, twist_ref, out_ref, hi_ref, lo_ref):
    for half in range(2):
        cols = pl.ds(half * 128, 128)
        field = []
        for j in range(16):
            field.append(cos_sin_quarters(2.0 * decode(phase_ref[j, o, :, cols])))
        spectrum = fft16(field, -1.0)
        for k1 in range(16):
            re, im = spectrum[k1]
            if k1 > 0:
                c = twist_ref[0, pl.ds(k1, 1), cols]
                s = twist_ref[1, pl.ds(k1, 1), cols]
                re, im = re * c - im * s, re * s + im * c
            rows = pl.ds(k1 * 16, 16)
            for part, value in enumerate((re, im)):
                hi, lo = split(value)
                place = pl.ds(part * 256 + half * 128, 128)
                hi_ref[rows, place] = hi
                lo_ref[rows, place] = lo
    result = dot3((matrix_ref[0], matrix_ref[1]), (hi_ref[...], lo_ref[...]), NT)
    for h in range(2):
        out_ref[:, h, o] = encode(result[:, h * 128 : (h + 1) * 128]).reshape(64, 8, 128)


def transfer(o, me, wave, travel, cos_ref, sin_ref):
    row = lax.broadcasted_iota(jnp.int32, (8, 128), 0)
    lane = lax.broadcasted_iota(jnp.int32, (8, 128), 1)
    base_x = (row // 4) + 128 * (lane % 16)
    freq_y = 8 * (me % 2) + lane // 16 + 16 * (4 * (me // 2) + row % 4)
    signed_y = jnp.where(freq_y < 2048, freq_y, freq_y - 4096).astype(F32) * (1.0 / 4096)
    square_y = signed_y * signed_y

    def step(place, carry):
        freq_x = base_x + 2 * place
        signed_x = jnp.where(freq_x < 1024, freq_x, freq_x - 2048).astype(F32) * (1.0 / 2048)
        squared = signed_x * signed_x + square_y
        turns = travel * squared / (wave + jnp.sqrt(wave * wave - squared))
        c, w = cos_sin_quarters(4.0 * turns)
        cos_ref[o, place] = c
        sin_ref[o, place] = w
        return carry

    lax.fori_loop(0, 64, step, 0, unroll=4)


def put_split(place, re, im, hi_ref, lo_ref):
    for part, value in enumerate((re, im)):
        hi, lo = split(value)
        lanes = pl.ds(part * 128, 128)
        hi_ref[place, :, lanes] = hi
        lo_ref[place, :, lanes] = lo


def columns(o, in_ref, matrix_ref, back_ref, twist_ref, cos_ref, sin_ref, out_ref, re_ref, im_ref, hi_ref, lo_ref):
    row = lax.broadcasted_iota(jnp.int32, (8, 128), 0)
    top = row < 4
    for n2 in range(8):
        column = []
        for n1 in range(8):
            s = 8 * n1 + n2
            a, b = decode(in_ref[s, o]), decode(in_ref[s + 64, o])
            total, delta = a + b, a - b
            re = jnp.where(top, total, pltpu.roll(delta, 4, 0))
            im = jnp.where(top, pltpu.roll(total, 4, 0), delta)
            if s > 0:
                angle = 2.0 * math.pi * s / 128
                c = jnp.where(top, 1.0, math.cos(angle))
                w = jnp.where(top, 0.0, math.sin(angle))
                re, im = re * c + im * w, im * c - re * w
            column.append((re, im))
        for m1, v in enumerate(fft8(column, -1.0)):
            re, im = scaled(v, -2.0 * math.pi * n2 * m1 / 64)
            re_ref[m1 * 8 + n2] = re
            im_ref[m1 * 8 + n2] = im
    for m1 in range(8):
        column = [(re_ref[m1 * 8 + n2], im_ref[m1 * 8 + n2]) for n2 in range(8)]
        for m2, (re, im) in enumerate(fft8(column, -1.0)):
            place = m1 + 8 * m2
            c, w = twist_ref[0, place], twist_ref[1, place]
            put_split(place, re * c - im * w, re * w + im * c, hi_ref, lo_ref)
    data = (hi_ref[...].reshape(512, 256), lo_ref[...].reshape(512, 256))
    spectrum = dot3(data, (matrix_ref[0], matrix_ref[1]), NN).reshape(64, 8, 256)
    for place in range(64):
        c, w = cos_ref[o, place], sin_ref[o, place]
        re, im = spectrum[place, :, :128], spectrum[place, :, 128:]
        put_split(place, re * c + im * w, im * c - re * w, hi_ref, lo_ref)
    data = (hi_ref[...].reshape(512, 256), lo_ref[...].reshape(512, 256))
    spectrum = dot3(data, (back_ref[0], back_ref[1]), NN).reshape(64, 8, 256)
    for m1 in range(8):
        column = []
        for m2 in range(8):
            place = m1 + 8 * m2
            re, im = spectrum[place, :, :128], spectrum[place, :, 128:]
            c, w = twist_ref[0, place], twist_ref[1, place]
            column.append((re * c + im * w, im * c - re * w))
        for n2, v in enumerate(fft8(column, 1.0)):
            re, im = scaled(v, 2.0 * math.pi * n2 * m1 / 64)
            re_ref[m1 * 8 + n2] = re
            im_ref[m1 * 8 + n2] = im
    for n2 in range(8):
        column = [(re_ref[m1 * 8 + n2], im_ref[m1 * 8 + n2]) for m1 in range(8)]
        for n1, (re, im) in enumerate(fft8(column, 1.0)):
            s = 8 * n1 + n2
            if s > 0:
                angle = 2.0 * math.pi * s / 128
                c = jnp.where(top, 1.0, math.cos(angle))
                w = jnp.where(top, 0.0, math.sin(angle))
                re, im = re * c - im * w, im * c + re * w
            total = jnp.where(top, re, pltpu.roll(im, 4, 0))
            delta = jnp.where(top, pltpu.roll(re, 4, 0), im)
            out_ref[s, o] = encode(total + delta)
            out_ref[s + 64, o] = encode(total - delta)


def rows_inverse(o, in_ref, matrix_ref, twist_ref, spread_ref, out_ref):
    left = decode(in_ref[:, 0, o]).reshape(512, 128)
    right = decode(in_ref[:, 1, o]).reshape(512, 128)
    data = split(jnp.concatenate([left, right], axis=1))
    value = dot3((matrix_ref[0], matrix_ref[1]), data, NN)
    re, im = value[:256], value[256:]
    c, s = twist_ref[0], twist_ref[1]
    value = jnp.concatenate([re * c - im * s, re * s + im * c], axis=1)
    result = dot3((spread_ref[0], spread_ref[1]), split(value), NT)
    for part in range(2):
        for j in range(16):
            rows = result[part * 256 + j * 16 : part * 256 + j * 16 + 16, :]
            out_ref[o, part, :, j * 256 : (j + 1) * 256] = rows.astype(BF16)


def band(weight_ref, band_ref):
    x = lax.broadcasted_iota(jnp.int32, (32, 128), 0)
    lane = lax.broadcasted_iota(jnp.int32, (32, 128), 1)
    shift = lane % 64 - x - 15
    upper = lane < 64

    def block(vo, carry):
        for pair in range(8):
            value = jnp.zeros((32, 128), F32)
            for u in range(3):
                base = (vo * 16 + 2 * pair) * 3 + u
                both = jnp.where(upper, weight_ref[base], weight_ref[base + 3])
                value = jnp.where(shift == u, both, value)
            band_ref[pl.ds(pl.multiple_of(vo * 32, 32), 32), pair * 128 : (pair + 1) * 128] = value.astype(BF16)
        return carry

    lax.fori_loop(0, 9, block, 0)
    row = lax.broadcasted_iota(jnp.int32, (16, 128), 0)
    lane = lax.broadcasted_iota(jnp.int32, (16, 128), 1)
    upper = lane < 64
    for place, (source, u) in enumerate(((16, 2), (47, 0))):
        here = lane % 64 == source
        for pair in range(8):
            value = jnp.zeros((16, 128), F32)
            for vo in range(9):
                base = (vo * 16 + 2 * pair) * 3 + u
                both = jnp.where(upper, weight_ref[base], weight_ref[base + 3])
                value = jnp.where(here & (row == vo), both, value)
            band_ref[288 + 16 * place : 304 + 16 * place, pair * 128 : (pair + 1) * 128] = value.astype(BF16)


def head(i, j, weight_ref, bias_ref, band_ref, tile_ref, sums_ref, sides_ref, edges_ref, got_sides_ref, got_edges_ref, phase_ref, down, border_sems, send_phase):
    band(weight_ref, band_ref)
    lane = lax.broadcasted_iota(jnp.int32, (32, 128), 1)
    to_right = jnp.zeros((32, 128), F32)
    to_left = jnp.zeros((32, 128), F32)
    for k in range(8):
        window = tile_ref[:, k * 32 : k * 32 + 64, :].reshape(1024, 256)
        count = 320 if k in (0, 7) else 288
        value = jnp.dot(band_ref[:count], window, preferred_element_type=F32)
        sums_ref[k] = value[:288].reshape(9, 32, 256)
        if k == 0:
            edges_ref[0] = value[288:304]
        if k == 7:
            edges_ref[1] = value[304:320]
        for o in range(3):
            to_right = jnp.where(lane == 3 * k + o, value[o * 32 : o * 32 + 32, 255:256], to_right)
            to_left = jnp.where(lane == 3 * k + o, value[192 + o * 32 : 224 + o * 32, 0:1], to_left)
    sides_ref[0] = to_right
    sides_ref[1] = to_left
    down()
    send_sems, recv_sems = border_sems
    copies = []
    for slot, step in enumerate((1, -1)):
        copies.append((sides_ref.at[slot], got_sides_ref.at[slot], i, (j + step + 16) % 16))
    for edge, down_step in enumerate((-1, 1)):
        for side, step in enumerate((-1, 0, 1)):
            copies.append((edges_ref.at[edge], got_edges_ref.at[edge * 3 + 2 - side], (i + down_step + 8) % 8, (j + step + 16) % 16))
    copies = [
        pltpu.make_async_remote_copy(
            src_ref=source, dst_ref=target, send_sem=send_sems.at[n], recv_sem=recv_sems.at[n],
            device_id=row * 16 + col, device_id_type=LOGICAL,
        )
        for n, (source, target, row, col) in enumerate(copies)
    ]
    for copy in copies:
        copy.start()
    for copy in copies:
        copy.wait()
    below, above = i < 7, i > 0
    left, right = j > 0, j < 15
    wide = lax.broadcasted_iota(jnp.int32, (32, 256), 1)
    tall = lax.broadcasted_iota(jnp.int32, (32, 1), 0)

    def rows_beyond(k, vo):
        first = (tall == 0) & (k == 0) & above
        last = (tall == 31) & (k == 7) & below
        top = got_edges_ref[4, vo : vo + 1, :]
        bottom = got_edges_ref[1, vo : vo + 1, :]
        return jnp.where(first, top, jnp.where(last, bottom, 0.0))

    def column_beyond(k, o, side):
        sides = got_sides_ref[side]
        value = jnp.sum(jnp.where(lane == 3 * k + o, sides, 0.0), axis=1, keepdims=True)
        first = (tall == 0) & (k == 0) & above
        last = (tall == 31) & (k == 7) & below
        vo, y = (o, 255) if side == 0 else (6 + o, 0)
        top = got_edges_ref[3 + 2 * side, vo : vo + 1, y : y + 1]
        bottom = got_edges_ref[2 * side, vo : vo + 1, y : y + 1]
        value = value + jnp.where(first, top, jnp.where(last, bottom, 0.0))
        return jnp.where(left if side == 0 else right, value, 0.0)

    def block(step, carry):
        k = (j // 2 + step) % 8
        for o in range(3):
            first = sums_ref[k, o] + rows_beyond(k, o)
            middle = sums_ref[k, 3 + o] + rows_beyond(k, 3 + o)
            last = sums_ref[k, 6 + o] + rows_beyond(k, 6 + o)
            first = jnp.where(wide == 0, column_beyond(k, o, 0), pltpu.roll(first, 1, 1))
            last = jnp.where(wide == 255, column_beyond(k, o, 1), pltpu.roll(last, 255, 1))
            value = encode(jnp.tanh(first + middle + last + bias_ref[o]))
            phase_ref[2 * k, o] = value[:16]
            phase_ref[2 * k + 1, o] = value[16:]
        send_phase(2 * k)
        send_phase(2 * k + 1)
        return carry

    lax.fori_loop(0, 8, block, 0)


def spectral_kernel(
    weight_ref, bias_ref, wave_ref, travel_ref, features_ref,
    forward_ref, inverse_ref, spread_ref, lanes_ref, back_ref, twist_y_ref, twist_back_ref, twist_x_ref,
    out_ref,
    tile_ref, band_ref, sums_ref, sides_ref, edges_ref, got_sides_ref, got_edges_ref, phase_ref, got_phase_ref,
    packets_ref, spread_in_ref, filtered_ref, returned_ref, cos_ref, sin_ref, re_ref, im_ref, hi_ref, lo_ref, field_hi_ref, field_lo_ref,
    free_sem, tile_sem, border_send, border_recv, send_sems, recv_sems, local_sems,
):
    colors = 3
    i, j = lax.axis_index("row"), lax.axis_index("col")
    me = i * 16 + j
    up, down = enter(me, free_sem, 16)
    up()
    load = pltpu.make_async_copy(features_ref, tile_ref.at[:, pl.ds(16, 256), :], tile_sem)
    load.start()
    tile_ref[:, 0:16, :] = jnp.zeros((16, 16, 256), BF16)
    tile_ref[:, 272:288, :] = jnp.zeros((16, 16, 256), BF16)
    load.wait()

    def send_phase(peer):
        @pl.when(peer == j)
        def _():
            pltpu.make_async_copy(phase_ref.at[peer], got_phase_ref.at[j], local_sems.at[2]).start()

        @pl.when(peer != j)
        def _():
            pltpu.make_async_remote_copy(
                src_ref=phase_ref.at[peer], dst_ref=got_phase_ref.at[j], send_sem=send_sems.at[2], recv_sem=recv_sems.at[2],
                device_id=i * 16 + peer, device_id_type=LOGICAL,
            ).start()

    head(
        i, j, weight_ref, bias_ref, band_ref, tile_ref, sums_ref, sides_ref, edges_ref, got_sides_ref, got_edges_ref, phase_ref,
        down, (border_send, border_recv), send_phase,
    )

    def each(body):
        def step(o, carry):
            body(o)
            return carry

        lax.fori_loop(0, colors, step, 0)

    first = (send_sems.at[0], recv_sems.at[0], local_sems.at[0])
    second = (send_sems.at[1], recv_sems.at[1], local_sems.at[1])
    each(lambda o: transfer(o, me, wave_ref[o], travel_ref[0], cos_ref, sin_ref))
    wait_all(got_phase_ref, send_sems.at[2], recv_sems.at[2], local_sems.at[2])
    by_pair = packets_ref.reshape(64, 2, colors, 8, 128)
    each(lambda o: rows_forward(o, got_phase_ref, forward_ref, twist_y_ref, by_pair, field_hi_ref, field_lo_ref))
    send_all(me, lambda d: packets_ref.at[d], spread_in_ref, *first)
    wait_all(spread_in_ref, *first)
    each(lambda o: columns(o, spread_in_ref, lanes_ref, back_ref, twist_x_ref, cos_ref, sin_ref, filtered_ref, re_ref, im_ref, hi_ref, lo_ref))
    send_all(me, lambda d: filtered_ref.at[d], returned_ref, *second)
    wait_all(returned_ref, *second)
    by_pair_back = returned_ref.reshape(64, 2, colors, 8, 128)
    each(lambda o: rows_inverse(o, by_pair_back, inverse_ref, twist_back_ref, spread_ref, out_ref))


def per_device(features, conv_weight, bias, wave, travel):
    table = tables()
    colors = 3
    names = ("forward_y", "inverse_y", "spread16", "lanes", "lanes_back", "twist_y", "twist_back", "twist_x")
    args = [jnp.asarray(table[k]) for k in names]
    weight = conv_weight.astype(F32).transpose(3, 0, 1, 2).reshape(-1)
    smem = pl.BlockSpec(memory_space=pltpu.SMEM)
    vmem = pl.BlockSpec(memory_space=pltpu.VMEM)
    exchange = pltpu.VMEM((128, colors, 8, 128), BF16)
    return pl.pallas_call(
        spectral_kernel,
        in_specs=[smem] * 4 + [pl.BlockSpec(memory_space=pl.ANY)] + [vmem] * len(args),
        out_specs=vmem,
        out_shape=jax.ShapeDtypeStruct((colors, 2, 16, 4096), BF16),
        scratch_shapes=[
            pltpu.VMEM((16, 288, 256), BF16),
            pltpu.VMEM((320, 1024), BF16),
            pltpu.VMEM((8, 9, 32, 256), F32),
            pltpu.VMEM((2, 32, 128), F32),
            pltpu.VMEM((2, 16, 256), F32),
            pltpu.VMEM((2, 32, 128), F32),
            pltpu.VMEM((6, 16, 256), F32),
            pltpu.VMEM((16, colors, 16, 256), BF16),
            pltpu.VMEM((16, colors, 16, 256), BF16),
            exchange, exchange, exchange, exchange,
            pltpu.VMEM((colors, 64, 8, 128), F32),
            pltpu.VMEM((colors, 64, 8, 128), F32),
            pltpu.VMEM((64, 8, 128), F32),
            pltpu.VMEM((64, 8, 128), F32),
            pltpu.VMEM((64, 8, 256), BF16),
            pltpu.VMEM((64, 8, 256), BF16),
            pltpu.VMEM((256, 512), BF16),
            pltpu.VMEM((256, 512), BF16),
            pltpu.SemaphoreType.REGULAR,
            pltpu.SemaphoreType.DMA,
            pltpu.SemaphoreType.DMA((8,)),
            pltpu.SemaphoreType.DMA((8,)),
            pltpu.SemaphoreType.DMA((3,)),
            pltpu.SemaphoreType.DMA((3,)),
            pltpu.SemaphoreType.DMA((3,)),
        ],
        compiler_params=pltpu.CompilerParams(collective_id=0, has_side_effects=True, vmem_limit_bytes=VMEM_LIMIT),
        name="spectral",
    )(weight, bias, wave, travel, features, *args)


def solution(mesh):
    in_specs = (P(None, "row", "col"), P(), P(), P(), P())
    out_specs = P(None, None, ("row", "col"), None)
    return jax.shard_map(
        per_device, mesh=mesh, in_specs=in_specs, out_specs=out_specs, check_vma=False
    )
```

```python
import functools
import math

import jax
import jax.numpy as jnp
import numpy as np
from jax import lax
from jax.experimental import pallas as pl
from jax.experimental.pallas import tpu as pltpu
from jax.sharding import PartitionSpec as P

F32 = jnp.float32
BF16 = jnp.bfloat16
VMEM_LIMIT = 56 * 1024 * 1024


def split_np(table):
    hi = table.astype(np.float32).astype(jnp.bfloat16)
    lo = (table - hi.astype(np.float64)).astype(np.float32).astype(jnp.bfloat16)
    return np.stack([np.asarray(hi), np.asarray(lo)])


def rotation_np(theta):
    return np.array([[np.cos(theta), np.sin(theta)], [-np.sin(theta), np.cos(theta)]])


def tables():
    k2 = np.arange(256)
    b = np.arange(256)
    rot = rotation_np(2.0 * np.pi * ((k2[:, None] * b[None, :]) % 256) / 256.0)
    forward_y = rot.reshape(2, 2, 64, 4, 256).transpose(2, 0, 3, 1, 4).reshape(512, 512)
    j = np.arange(16)
    rot16 = rotation_np(2.0 * np.pi * ((j[:, None] * j[None, :]) % 16) / 16.0)
    back16 = np.stack([np.stack([rot16[0, 0], -rot16[0, 1]]), np.stack([-rot16[1, 0], rot16[1, 1]])])
    lanes = np.einsum("pqab,cd->qcbpda", rot16, np.eye(8)).reshape(256, 256)
    lanes_back = np.einsum("pqab,cd->qcbpda", back16, np.eye(8)).reshape(256, 256)
    k1 = np.arange(16)
    angle = 2.0 * np.pi * ((k1[:, None] * b[None, :]) % 4096) / 4096.0
    twist_y = np.stack([np.cos(angle), -np.sin(angle)]).astype(np.float32)
    p = np.arange(128).reshape(64, 2)
    r = np.arange(16)
    angle = 2.0 * np.pi * ((p[:, :, None] * r) % 2048) / 2048.0
    twist_x = np.stack([np.cos(angle), -np.sin(angle)])
    twist_x = np.broadcast_to(twist_x[:, :, :, None, None, :], (2, 64, 2, 4, 8, 16))
    twist_x = twist_x.reshape(2, 64, 8, 128).astype(np.float32)
    return {
        "forward_y": split_np(forward_y * 8.0),
        "lanes": split_np(lanes),
        "lanes_back": split_np(lanes_back * 2.0**-16),
        "twist_y": twist_y,
        "twist_x": twist_x,
    }


def encode(x):
    x = x * jnp.abs(x)
    x = x * jnp.abs(x)
    x = x * jnp.abs(x)
    return x.astype(BF16)


def decode(y):
    y = y.astype(F32)
    root = jnp.sqrt(jnp.sqrt(jnp.sqrt(jnp.abs(y))))
    return jnp.where(y < 0.0, -root, root)


def split(x):
    hi = x.astype(BF16)
    return hi, (x - hi.astype(F32)).astype(BF16)


def cos_sin_quarters(u):
    n = jnp.round(u)
    f = u - n
    n = n.astype(jnp.int32)
    z = f * f
    s = f * (1.5707963267948966 + z * (-0.6459640975062462 + z * (0.07969262624616703 + z * (-0.004681754135318688 + z * 0.00016044118478735982))))
    c = 1.0 + z * (-1.2337005501361697 + z * (0.253669507901048 + z * (-0.020863480763352960 + z * (0.0009192602748394265 - z * 2.5202042373060605e-05))))
    swap = (n & 1) == 1
    cos = jnp.where(swap, s, c)
    sin = jnp.where(swap, c, s)
    cos = jnp.where(((n + 1) & 2) == 2, -cos, cos)
    sin = jnp.where((n & 2) == 2, -sin, sin)
    return cos, sin


def fft4(x, sign):
    (ar, ai), (br, bi), (cr, ci), (dr, di) = x
    sr, si, tr, ti = ar + cr, ai + ci, ar - cr, ai - ci
    ur, ui, vr, vi = br + dr, bi + di, br - dr, bi - di
    if sign < 0:
        vr, vi = vi, -vr
    else:
        vr, vi = -vi, vr
    return [(sr + ur, si + ui), (tr + vr, ti + vi), (sr - ur, si - ui), (tr - vr, ti - vi)]


def scaled(x, angle):
    turn = angle / (0.5 * math.pi)
    xr, xi = x
    if abs(turn - round(turn)) < 1e-9:
        case = int(round(turn)) % 4
        return [(xr, xi), (-xi, xr), (-xr, -xi), (xi, -xr)][case]
    c, s = math.cos(angle), math.sin(angle)
    eighth = turn * 2
    if abs(eighth - round(eighth)) < 1e-9:
        case = int(round(eighth)) % 8
        h = math.sqrt(0.5)
        if case == 1:
            return ((xr - xi) * h, (xr + xi) * h)
        if case == 3:
            return ((xr + xi) * -h, (xr - xi) * h)
        if case == 5:
            return ((xi - xr) * h, (xr + xi) * -h)
        return ((xr + xi) * h, (xi - xr) * h)
    return (xr * c - xi * s, xr * s + xi * c)


def fft8(x, sign):
    even = fft4(x[0::2], sign)
    odd = fft4(x[1::2], sign)
    odd = [scaled(v, sign * 2.0 * math.pi * k / 8) for k, v in enumerate(odd)]
    first = [(a[0] + b[0], a[1] + b[1]) for a, b in zip(even, odd)]
    return first + [(a[0] - b[0], a[1] - b[1]) for a, b in zip(even, odd)]


def fft16(x, sign):
    inner = [fft4([x[4 * n1 + n2] for n1 in range(4)], sign) for n2 in range(4)]
    out = [None] * 16
    for k1 in range(4):
        column = [scaled(inner[n2][k1], sign * 2.0 * math.pi * n2 * k1 / 16) for n2 in range(4)]
        for k2, v in enumerate(fft4(column, sign)):
            out[k1 + 4 * k2] = v
    return out


def dot3(lhs, rhs, dims):
    one = functools.partial(lax.dot_general, dimension_numbers=(dims, ((), ())), preferred_element_type=F32)
    return one(lhs[0], rhs[0]) + (one(lhs[0], rhs[1]) + one(lhs[1], rhs[0]))


NN = ((1,), (0,))
NT = ((1,), (1,))
TN = ((0,), (0,))


LOGICAL = pl.DeviceIdType.LOGICAL


def enter(i, j):
    barrier = pltpu.get_barrier_semaphore()

    def signal(row, col):
        pl.semaphore_signal(barrier, inc=1, device_id=row * 16 + col, device_id_type=LOGICAL)

    for step in range(1, 16):
        signal(i, (j + step) % 16)
    for step in range(1, 8):
        signal((i + step) % 8, j)
    for row in (7, 1):
        for col in (15, 1):
            signal((i + row) % 8, (j + col) % 16)

    def down():
        pl.semaphore_wait(barrier, 26)

    return down


def send_all(me, block_of, landing, send_sem, recv_sem, local_sem):
    pltpu.make_async_copy(block_of(me), landing.at[me], local_sem).start()

    def one(k):
        peer = (me + k) % 128
        pltpu.make_async_remote_copy(
            src_ref=block_of(peer),
            dst_ref=landing.at[me],
            send_sem=send_sem,
            recv_sem=recv_sem,
            device_id=peer,
            device_id_type=LOGICAL,
        ).start()

    def group(g, carry):
        for k in range(8):
            one(8 * g + k)
        return carry

    for k in range(1, 8):
        one(k)
    lax.fori_loop(1, 16, group, 0)


def wait_all(landing, send_sem, recv_sem, local_sem):
    pltpu.make_async_copy(landing.at[0], landing.at[0], local_sem).wait()
    others = landing.at[pl.ds(0, landing.shape[0] - 1)]
    pltpu.make_async_copy(others, others, send_sem).wait()
    pltpu.make_async_copy(others, others, recv_sem).wait()


def rows_forward(o, phase_ref, matrix_ref, twist_ref, out_ref, hi_ref, lo_ref):
    for half in range(2):
        cols = pl.ds(half * 128, 128)
        field = []
        for j in range(16):
            field.append(cos_sin_quarters(2.0 * decode(phase_ref[j, o, :, cols])))
        spectrum = fft16(field, -1.0)
        for k1 in range(16):
            re, im = spectrum[k1]
            if k1 > 0:
                c = twist_ref[0, pl.ds(k1, 1), cols]
                s = twist_ref[1, pl.ds(k1, 1), cols]
                re, im = re * c - im * s, re * s + im * c
            rows = pl.ds(k1 * 16, 16)
            for part, value in enumerate((re, im)):
                hi, lo = split(value)
                place = pl.ds(part * 256 + half * 128, 128)
                hi_ref[rows, place] = hi
                lo_ref[rows, place] = lo
    result = dot3((matrix_ref[0], matrix_ref[1]), (hi_ref[...], lo_ref[...]), NT)
    for h in range(2):
        out_ref[:, h, o] = encode(result[:, h * 128 : (h + 1) * 128]).reshape(64, 8, 128)


def transfer(o, me, wave, travel, cos_ref, sin_ref):
    row = lax.broadcasted_iota(jnp.int32, (8, 128), 0)
    lane = lax.broadcasted_iota(jnp.int32, (8, 128), 1)
    base_x = (row // 4) + 128 * (lane % 16)
    freq_y = 8 * (me % 2) + lane // 16 + 16 * (4 * (me // 2) + row % 4)
    signed_y = jnp.where(freq_y < 2048, freq_y, freq_y - 4096).astype(F32) * (1.0 / 4096)
    square_y = signed_y * signed_y

    def step(place, carry):
        freq_x = base_x + 2 * place
        signed_x = jnp.where(freq_x < 1024, freq_x, freq_x - 2048).astype(F32) * (1.0 / 2048)
        squared = signed_x * signed_x + square_y
        turns = travel * squared / (wave + jnp.sqrt(wave * wave - squared))
        c, w = cos_sin_quarters(4.0 * turns)
        cos_ref[o, place] = c
        sin_ref[o, place] = w
        return carry

    lax.fori_loop(0, 64, step, 0, unroll=4)


def put_split(place, re, im, hi_ref, lo_ref):
    for part, value in enumerate((re, im)):
        hi, lo = split(value)
        lanes = pl.ds(part * 128, 128)
        hi_ref[place, :, lanes] = hi
        lo_ref[place, :, lanes] = lo


def columns(o, in_ref, matrix_ref, back_ref, twist_ref, cos_ref, sin_ref, out_ref, re_ref, im_ref, hi_ref, lo_ref):
    row = lax.broadcasted_iota(jnp.int32, (8, 128), 0)
    top = row < 4
    for n2 in range(8):
        column = []
        for n1 in range(8):
            s = 8 * n1 + n2
            a, b = decode(in_ref[s, o]), decode(in_ref[s + 64, o])
            total, delta = a + b, a - b
            re = jnp.where(top, total, pltpu.roll(delta, 4, 0))
            im = jnp.where(top, pltpu.roll(total, 4, 0), delta)
            if s > 0:
                angle = 2.0 * math.pi * s / 128
                c = jnp.where(top, 1.0, math.cos(angle))
                w = jnp.where(top, 0.0, math.sin(angle))
                re, im = re * c + im * w, im * c - re * w
            column.append((re, im))
        for m1, v in enumerate(fft8(column, -1.0)):
            re, im = scaled(v, -2.0 * math.pi * n2 * m1 / 64)
            re_ref[m1 * 8 + n2] = re
            im_ref[m1 * 8 + n2] = im
    for m1 in range(8):
        column = [(re_ref[m1 * 8 + n2], im_ref[m1 * 8 + n2]) for n2 in range(8)]
        for m2, (re, im) in enumerate(fft8(column, -1.0)):
            place = m1 + 8 * m2
            c, w = twist_ref[0, place], twist_ref[1, place]
            put_split(place, re * c - im * w, re * w + im * c, hi_ref, lo_ref)
    data = (hi_ref[...].reshape(512, 256), lo_ref[...].reshape(512, 256))
    spectrum = dot3(data, (matrix_ref[0], matrix_ref[1]), NN).reshape(64, 8, 256)
    for place in range(64):
        c, w = cos_ref[o, place], sin_ref[o, place]
        re, im = spectrum[place, :, :128], spectrum[place, :, 128:]
        put_split(place, re * c + im * w, im * c - re * w, hi_ref, lo_ref)
    data = (hi_ref[...].reshape(512, 256), lo_ref[...].reshape(512, 256))
    spectrum = dot3(data, (back_ref[0], back_ref[1]), NN).reshape(64, 8, 256)
    for m1 in range(8):
        column = []
        for m2 in range(8):
            place = m1 + 8 * m2
            re, im = spectrum[place, :, :128], spectrum[place, :, 128:]
            c, w = twist_ref[0, place], twist_ref[1, place]
            column.append((re * c + im * w, im * c - re * w))
        for n2, v in enumerate(fft8(column, 1.0)):
            re, im = scaled(v, 2.0 * math.pi * n2 * m1 / 64)
            re_ref[m1 * 8 + n2] = re
            im_ref[m1 * 8 + n2] = im
    for n2 in range(8):
        column = [(re_ref[m1 * 8 + n2], im_ref[m1 * 8 + n2]) for m1 in range(8)]
        for n1, (re, im) in enumerate(fft8(column, 1.0)):
            s = 8 * n1 + n2
            if s > 0:
                angle = 2.0 * math.pi * s / 128
                c = jnp.where(top, 1.0, math.cos(angle))
                w = jnp.where(top, 0.0, math.sin(angle))
                re, im = re * c - im * w, im * c + re * w
            total = jnp.where(top, re, pltpu.roll(im, 4, 0))
            delta = jnp.where(top, pltpu.roll(re, 4, 0), im)
            out_ref[s, o] = encode(total + delta)
            out_ref[s + 64, o] = encode(total - delta)


def rows_inverse(o, in_ref, matrix_ref, twist_ref, value_ref, out_ref):
    for h in range(2):
        hi, lo = split(decode(in_ref[:, h, o]).reshape(512, 128))
        rows = pl.ds(h * 128, 128)
        value_ref[rows, :] = dot3((hi, lo), (matrix_ref[0], matrix_ref[1]), TN)
    for half in range(2):
        cols = pl.ds(half * 128, 128)
        spectrum = []
        for k1 in range(16):
            rows = pl.ds(k1 * 16, 16)
            re = value_ref[rows, cols] * 2.0**-13
            im = value_ref[rows, pl.ds(256 + half * 128, 128)] * 2.0**-13
            if k1 > 0:
                c = twist_ref[0, pl.ds(k1, 1), cols]
                s = twist_ref[1, pl.ds(k1, 1), cols]
                re, im = re * c + im * s, im * c - re * s
            spectrum.append((re, im))
        for j, field in enumerate(fft16(spectrum, 1.0)):
            for part in range(2):
                out_ref[o, part, :, pl.ds(j * 256 + half * 128, 128)] = field[part].astype(BF16)


def band(weight_ref, band_ref):
    x = lax.broadcasted_iota(jnp.int32, (32, 128), 0)
    lane = lax.broadcasted_iota(jnp.int32, (32, 128), 1)
    shift = lane % 64 - x - 15
    upper = lane < 64
    row = lax.broadcasted_iota(jnp.int32, (16, 128), 0)
    beyond = [(lane[:16] % 64 == source, u) for source, u in ((16, 2), (47, 0))]
    for pair in range(8):
        columns_of = pl.ds(pair * 128, 128)
        edges = [jnp.zeros((16, 128), F32), jnp.zeros((16, 128), F32)]
        for o in range(3):
            low = weight_ref[o, 2 * pair].astype(F32)
            high = weight_ref[o, 2 * pair + 1].astype(F32)
            for v in range(3):
                value = jnp.zeros((32, 128), F32)
                for u in range(3):
                    a = jnp.broadcast_to(low[u : u + 1, v : v + 1], (32, 128))
                    b = jnp.broadcast_to(high[u : u + 1, v : v + 1], (32, 128))
                    both = jnp.where(upper, a, b)
                    value = jnp.where(shift == u, both, value)
                    for n, (here, edge_u) in enumerate(beyond):
                        if u == edge_u:
                            edges[n] = jnp.where(here & (row == v * 3 + o), both[:16], edges[n])
                band_ref[(v * 3 + o) * 32 : (v * 3 + o) * 32 + 32, columns_of] = value.astype(BF16)
        for n in range(2):
            band_ref[288 + 16 * n : 304 + 16 * n, columns_of] = edges[n].astype(BF16)


def head(i, j, weight_ref, bias_ref, band_ref, tile_ref, sums_ref, sides_ref, edges_ref, got_sides_ref, got_edges_ref, phase_ref, down, border_sems, send_phase, meanwhile):
    band(weight_ref, band_ref)
    lane = lax.broadcasted_iota(jnp.int32, (32, 128), 1)
    to_right = jnp.zeros((32, 128), F32)
    to_left = jnp.zeros((32, 128), F32)
    for k in range(8):
        window = tile_ref[:, k * 32 : k * 32 + 64, :].reshape(1024, 256)
        count = 320 if k in (0, 7) else 288
        value = jnp.dot(band_ref[:count], window, preferred_element_type=F32)
        sums_ref[k] = value[:288].reshape(9, 32, 256)
        if k == 0:
            edges_ref[0] = value[288:304]
        if k == 7:
            edges_ref[1] = value[304:320]
        for o in range(3):
            to_right = jnp.where(lane == 3 * k + o, value[o * 32 : o * 32 + 32, 255:256], to_right)
            to_left = jnp.where(lane == 3 * k + o, value[192 + o * 32 : 224 + o * 32, 0:1], to_left)
    sides_ref[0] = to_right
    sides_ref[1] = to_left
    down()
    send_sems, recv_sems = border_sems
    copies = []
    for slot, step in enumerate((1, -1)):
        copies.append((sides_ref.at[slot], got_sides_ref.at[slot], i, (j + step + 16) % 16))
    for edge, down_step in enumerate((-1, 1)):
        for side, step in enumerate((-1, 0, 1)):
            copies.append((edges_ref.at[edge], got_edges_ref.at[edge * 3 + 2 - side], (i + down_step + 8) % 8, (j + step + 16) % 16))
    copies = [
        pltpu.make_async_remote_copy(
            src_ref=source, dst_ref=target, send_sem=send_sems.at[n], recv_sem=recv_sems.at[n],
            device_id=row * 16 + col, device_id_type=LOGICAL,
        )
        for n, (source, target, row, col) in enumerate(copies)
    ]
    for copy in copies:
        copy.start()
    meanwhile()
    for copy in copies:
        copy.wait()
    below, above = i < 7, i > 0
    left, right = j > 0, j < 15
    wide = lax.broadcasted_iota(jnp.int32, (32, 256), 1)
    tall = lax.broadcasted_iota(jnp.int32, (32, 1), 0)

    def rows_beyond(k, vo):
        first = (tall == 0) & (k == 0) & above
        last = (tall == 31) & (k == 7) & below
        top = got_edges_ref[4, vo : vo + 1, :]
        bottom = got_edges_ref[1, vo : vo + 1, :]
        return jnp.where(first, top, jnp.where(last, bottom, 0.0))

    def column_beyond(k, o, side):
        sides = got_sides_ref[side]
        value = jnp.sum(jnp.where(lane == 3 * k + o, sides, 0.0), axis=1, keepdims=True)
        first = (tall == 0) & (k == 0) & above
        last = (tall == 31) & (k == 7) & below
        vo, y = (o, 255) if side == 0 else (6 + o, 0)
        top = got_edges_ref[3 + 2 * side, vo : vo + 1, y : y + 1]
        bottom = got_edges_ref[2 * side, vo : vo + 1, y : y + 1]
        value = value + jnp.where(first, top, jnp.where(last, bottom, 0.0))
        return jnp.where(left if side == 0 else right, value, 0.0)

    def block(step, carry):
        k = (j // 2 + step) % 8
        for o in range(3):
            first = sums_ref[k, o] + rows_beyond(k, o)
            middle = sums_ref[k, 3 + o] + rows_beyond(k, 3 + o)
            last = sums_ref[k, 6 + o] + rows_beyond(k, 6 + o)
            first = jnp.where(wide == 0, column_beyond(k, o, 0), pltpu.roll(first, 1, 1))
            last = jnp.where(wide == 255, column_beyond(k, o, 1), pltpu.roll(last, 255, 1))
            value = encode(jnp.tanh(first + middle + last + bias_ref[o]))
            phase_ref[2 * k, o] = value[:16]
            phase_ref[2 * k + 1, o] = value[16:]
        send_phase(2 * k)
        send_phase(2 * k + 1)
        return carry

    lax.fori_loop(0, 8, block, 0)


def spectral_kernel(
    weight_ref, bias_ref, wave_ref, travel_ref, features_ref,
    forward_ref, lanes_ref, back_ref, twist_y_ref, twist_x_ref,
    out_ref,
    tile_ref, band_ref, sums_ref, sides_ref, edges_ref, got_sides_ref, got_edges_ref, phase_ref, got_phase_ref,
    packets_ref, spread_in_ref, filtered_ref, returned_ref, cos_ref, sin_ref, re_ref, im_ref, hi_ref, lo_ref, field_hi_ref, field_lo_ref, value_ref,
    tile_sem, border_send, border_recv, send_sems, recv_sems, local_sems,
):
    colors = 3
    i, j = lax.axis_index("row"), lax.axis_index("col")
    me = i * 16 + j
    down = enter(i, j)
    load = pltpu.make_async_copy(features_ref, tile_ref.at[:, pl.ds(16, 256), :], tile_sem)
    load.start()
    tile_ref[:, 0:16, :] = jnp.zeros((16, 16, 256), BF16)
    tile_ref[:, 272:288, :] = jnp.zeros((16, 16, 256), BF16)
    load.wait()

    def each(body):
        def step(o, carry):
            body(o)
            return carry

        lax.fori_loop(0, colors, step, 0)

    def send_phase(peer):
        @pl.when(peer == j)
        def _():
            pltpu.make_async_copy(phase_ref.at[peer], got_phase_ref.at[j], local_sems.at[2]).start()

        @pl.when(peer != j)
        def _():
            pltpu.make_async_remote_copy(
                src_ref=phase_ref.at[peer], dst_ref=got_phase_ref.at[j], send_sem=send_sems.at[2], recv_sem=recv_sems.at[2],
                device_id=i * 16 + peer, device_id_type=LOGICAL,
            ).start()

    head(
        i, j, weight_ref, bias_ref, band_ref, tile_ref, sums_ref, sides_ref, edges_ref, got_sides_ref, got_edges_ref, phase_ref,
        down, (border_send, border_recv), send_phase,
        lambda: each(lambda o: transfer(o, me, wave_ref[o], travel_ref[0], cos_ref, sin_ref)),
    )

    first = (send_sems.at[0], recv_sems.at[0], local_sems.at[0])
    second = (send_sems.at[1], recv_sems.at[1], local_sems.at[1])
    wait_all(got_phase_ref, send_sems.at[2], recv_sems.at[2], local_sems.at[2])
    by_pair = packets_ref.reshape(64, 2, colors, 8, 128)
    each(lambda o: rows_forward(o, got_phase_ref, forward_ref, twist_y_ref, by_pair, field_hi_ref, field_lo_ref))
    send_all(me, lambda d: packets_ref.at[d], spread_in_ref, *first)
    wait_all(spread_in_ref, *first)
    each(lambda o: columns(o, spread_in_ref, lanes_ref, back_ref, twist_x_ref, cos_ref, sin_ref, filtered_ref, re_ref, im_ref, hi_ref, lo_ref))
    send_all(me, lambda d: filtered_ref.at[d], returned_ref, *second)
    wait_all(returned_ref, *second)
    by_pair_back = returned_ref.reshape(64, 2, colors, 8, 128)
    each(lambda o: rows_inverse(o, by_pair_back, forward_ref, twist_y_ref, value_ref, out_ref))


def per_device(features, conv_weight, bias, wave, travel):
    table = tables()
    colors = 3
    names = ("forward_y", "lanes", "lanes_back", "twist_y", "twist_x")
    args = [jnp.asarray(table[k]) for k in names]
    smem = pl.BlockSpec(memory_space=pltpu.SMEM)
    vmem = pl.BlockSpec(memory_space=pltpu.VMEM)
    exchange = pltpu.VMEM((128, colors, 8, 128), BF16)
    return pl.pallas_call(
        spectral_kernel,
        in_specs=[vmem] + [smem] * 3 + [pl.BlockSpec(memory_space=pl.ANY)] + [vmem] * len(args),
        out_specs=vmem,
        out_shape=jax.ShapeDtypeStruct((colors, 2, 16, 4096), BF16),
        scratch_shapes=[
            pltpu.VMEM((16, 288, 256), BF16),
            pltpu.VMEM((320, 1024), BF16),
            pltpu.VMEM((8, 9, 32, 256), F32),
            pltpu.VMEM((2, 32, 128), F32),
            pltpu.VMEM((2, 16, 256), F32),
            pltpu.VMEM((2, 32, 128), F32),
            pltpu.VMEM((6, 16, 256), F32),
            pltpu.VMEM((16, colors, 16, 256), BF16),
            pltpu.VMEM((16, colors, 16, 256), BF16),
            exchange, exchange, exchange, exchange,
            pltpu.VMEM((colors, 64, 8, 128), F32),
            pltpu.VMEM((colors, 64, 8, 128), F32),
            pltpu.VMEM((64, 8, 128), F32),
            pltpu.VMEM((64, 8, 128), F32),
            pltpu.VMEM((64, 8, 256), BF16),
            pltpu.VMEM((64, 8, 256), BF16),
            pltpu.VMEM((256, 512), BF16),
            pltpu.VMEM((256, 512), BF16),
            pltpu.VMEM((256, 512), F32),
            pltpu.SemaphoreType.DMA,
            pltpu.SemaphoreType.DMA((8,)),
            pltpu.SemaphoreType.DMA((8,)),
            pltpu.SemaphoreType.DMA((3,)),
            pltpu.SemaphoreType.DMA((3,)),
            pltpu.SemaphoreType.DMA((3,)),
        ],
        compiler_params=pltpu.CompilerParams(collective_id=0, has_side_effects=True, vmem_limit_bytes=VMEM_LIMIT),
        name="spectral",
    )(conv_weight, bias, wave, travel, features, *args)


def solution(mesh):
    in_specs = (P(None, "row", "col"), P(), P(), P(), P())
    out_specs = P(None, None, ("row", "col"), None)
    return jax.shard_map(
        per_device, mesh=mesh, in_specs=in_specs, out_specs=out_specs, check_vma=False
    )
```

```python
import functools
import math

import jax
import jax.numpy as jnp
import numpy as np
from jax import lax
from jax.experimental import pallas as pl
from jax.experimental.pallas import tpu as pltpu
from jax.sharding import PartitionSpec as P

F32 = jnp.float32
BF16 = jnp.bfloat16
VMEM_LIMIT = 56 * 1024 * 1024


def split_np(table):
    hi = table.astype(np.float32).astype(jnp.bfloat16)
    lo = (table - hi.astype(np.float64)).astype(np.float32).astype(jnp.bfloat16)
    return np.stack([np.asarray(hi), np.asarray(lo)])


def rotation_np(theta):
    return np.array([[np.cos(theta), np.sin(theta)], [-np.sin(theta), np.cos(theta)]])


def tables():
    k2 = np.arange(256)
    b = np.arange(256)
    rot = rotation_np(2.0 * np.pi * ((k2[:, None] * b[None, :]) % 256) / 256.0)
    forward_y = rot.reshape(2, 2, 64, 4, 256).transpose(2, 0, 3, 1, 4).reshape(512, 512)
    j = np.arange(16)
    rot16 = rotation_np(2.0 * np.pi * ((j[:, None] * j[None, :]) % 16) / 16.0)
    back16 = np.stack([np.stack([rot16[0, 0], -rot16[0, 1]]), np.stack([-rot16[1, 0], rot16[1, 1]])])
    lanes = np.einsum("pqab,cd->qcbpda", rot16, np.eye(8)).reshape(256, 256)
    lanes_back = np.einsum("pqab,cd->qcbpda", back16, np.eye(8)).reshape(256, 256)
    k1 = np.arange(16)
    angle = 2.0 * np.pi * ((k1[:, None] * b[None, :]) % 4096) / 4096.0
    twist_y = np.stack([np.cos(angle), -np.sin(angle)]).astype(np.float32)
    p = np.arange(128).reshape(64, 2)
    r = np.arange(16)
    angle = 2.0 * np.pi * ((p[:, :, None] * r) % 2048) / 2048.0
    twist_x = np.stack([np.cos(angle), -np.sin(angle)])
    twist_x = np.broadcast_to(twist_x[:, :, :, None, None, :], (2, 64, 2, 4, 8, 16))
    twist_x = twist_x.reshape(2, 64, 8, 128).astype(np.float32)
    return {
        "forward_y": split_np(forward_y * 8.0),
        "lanes": split_np(lanes),
        "lanes_back": split_np(lanes_back * 2.0**-16),
        "twist_y": twist_y,
        "twist_x": twist_x,
    }


def encode(x):
    x = x * jnp.abs(x)
    x = x * jnp.abs(x)
    x = x * jnp.abs(x)
    return x.astype(BF16)


def decode(y):
    y = y.astype(F32)
    root = jnp.exp2(jnp.log2(jnp.abs(y)) * 0.125)
    return jnp.where(y < 0.0, -root, root)


def split(x):
    hi = x.astype(BF16)
    return hi, (x - hi.astype(F32)).astype(BF16)


def cos_sin_quarters(u):
    n = jnp.round(u)
    f = u - n
    n = n.astype(jnp.int32)
    z = f * f
    s = f * (1.5707963267948966 + z * (-0.6459640975062462 + z * (0.07969262624616703 + z * (-0.004681754135318688 + z * 0.00016044118478735982))))
    c = 1.0 + z * (-1.2337005501361697 + z * (0.253669507901048 + z * (-0.020863480763352960 + z * (0.0009192602748394265 - z * 2.5202042373060605e-05))))
    swap = (n & 1) == 1
    cos = jnp.where(swap, s, c)
    sin = jnp.where(swap, c, s)
    cos = jnp.where(((n + 1) & 2) == 2, -cos, cos)
    sin = jnp.where((n & 2) == 2, -sin, sin)
    return cos, sin


def fft4(x, sign):
    (ar, ai), (br, bi), (cr, ci), (dr, di) = x
    sr, si, tr, ti = ar + cr, ai + ci, ar - cr, ai - ci
    ur, ui, vr, vi = br + dr, bi + di, br - dr, bi - di
    if sign < 0:
        vr, vi = vi, -vr
    else:
        vr, vi = -vi, vr
    return [(sr + ur, si + ui), (tr + vr, ti + vi), (sr - ur, si - ui), (tr - vr, ti - vi)]


def scaled(x, angle):
    turn = angle / (0.5 * math.pi)
    xr, xi = x
    if abs(turn - round(turn)) < 1e-9:
        case = int(round(turn)) % 4
        return [(xr, xi), (-xi, xr), (-xr, -xi), (xi, -xr)][case]
    c, s = math.cos(angle), math.sin(angle)
    eighth = turn * 2
    if abs(eighth - round(eighth)) < 1e-9:
        case = int(round(eighth)) % 8
        h = math.sqrt(0.5)
        if case == 1:
            return ((xr - xi) * h, (xr + xi) * h)
        if case == 3:
            return ((xr + xi) * -h, (xr - xi) * h)
        if case == 5:
            return ((xi - xr) * h, (xr + xi) * -h)
        return ((xr + xi) * h, (xi - xr) * h)
    return (xr * c - xi * s, xr * s + xi * c)


def fft8(x, sign):
    even = fft4(x[0::2], sign)
    odd = fft4(x[1::2], sign)
    odd = [scaled(v, sign * 2.0 * math.pi * k / 8) for k, v in enumerate(odd)]
    first = [(a[0] + b[0], a[1] + b[1]) for a, b in zip(even, odd)]
    return first + [(a[0] - b[0], a[1] - b[1]) for a, b in zip(even, odd)]


def fft16(x, sign):
    inner = [fft4([x[4 * n1 + n2] for n1 in range(4)], sign) for n2 in range(4)]
    out = [None] * 16
    for k1 in range(4):
        column = [scaled(inner[n2][k1], sign * 2.0 * math.pi * n2 * k1 / 16) for n2 in range(4)]
        for k2, v in enumerate(fft4(column, sign)):
            out[k1 + 4 * k2] = v
    return out


def dot3(lhs, rhs, dims):
    one = functools.partial(lax.dot_general, dimension_numbers=(dims, ((), ())), preferred_element_type=F32)
    return one(lhs[0], rhs[0]) + (one(lhs[0], rhs[1]) + one(lhs[1], rhs[0]))


NN = ((1,), (0,))
NT = ((1,), (1,))
TN = ((0,), (0,))


LOGICAL = pl.DeviceIdType.LOGICAL


def enter(i, j):
    barrier = pltpu.get_barrier_semaphore()

    def signal(row, col):
        pl.semaphore_signal(barrier, inc=1, device_id=row * 16 + col, device_id_type=LOGICAL)

    for step in range(1, 16):
        signal(i, (j + step) % 16)
    for step in range(1, 8):
        signal((i + step) % 8, j)
    for row in (7, 1):
        for col in (15, 1):
            signal((i + row) % 8, (j + col) % 16)

    def down():
        pl.semaphore_wait(barrier, 26)

    return down


def send_all(me, block_of, landing, send_sem, recv_sem, local_sem):
    pltpu.make_async_copy(block_of(me), landing.at[me], local_sem).start()

    def one(k):
        peer = (me + k) % 128
        pltpu.make_async_remote_copy(
            src_ref=block_of(peer),
            dst_ref=landing.at[me],
            send_sem=send_sem,
            recv_sem=recv_sem,
            device_id=peer,
            device_id_type=LOGICAL,
        ).start()

    def group(g, carry):
        for k in range(8):
            one(8 * g + k)
        return carry

    for k in range(1, 8):
        one(k)
    lax.fori_loop(1, 16, group, 0)


def wait_all(landing, send_sem, recv_sem, local_sem):
    pltpu.make_async_copy(landing.at[0], landing.at[0], local_sem).wait()
    others = landing.at[pl.ds(0, landing.shape[0] - 1)]
    pltpu.make_async_copy(others, others, send_sem).wait()
    pltpu.make_async_copy(others, others, recv_sem).wait()


def rows_forward(o, phase_ref, matrix_ref, twist_ref, out_ref, hi_ref, lo_ref):
    for half in range(2):
        cols = pl.ds(half * 128, 128)
        field = []
        for j in range(16):
            field.append(cos_sin_quarters(2.0 * decode(phase_ref[o, j, :, cols])))
        spectrum = fft16(field, -1.0)
        for k1 in range(16):
            re, im = spectrum[k1]
            if k1 > 0:
                c = twist_ref[0, pl.ds(k1, 1), cols]
                s = twist_ref[1, pl.ds(k1, 1), cols]
                re, im = re * c - im * s, re * s + im * c
            rows = pl.ds(k1 * 16, 16)
            for part, value in enumerate((re, im)):
                hi, lo = split(value)
                place = pl.ds(part * 256 + half * 128, 128)
                hi_ref[rows, place] = hi
                lo_ref[rows, place] = lo
    result = dot3((matrix_ref[0], matrix_ref[1]), (hi_ref[...], lo_ref[...]), NT)
    for h in range(2):
        out_ref[:, h, o] = encode(result[:, h * 128 : (h + 1) * 128]).reshape(64, 8, 128)


def transfer(o, me, wave, travel, cos_ref, sin_ref):
    row = lax.broadcasted_iota(jnp.int32, (8, 128), 0)
    lane = lax.broadcasted_iota(jnp.int32, (8, 128), 1)
    base_x = (row // 4) + 128 * (lane % 16)
    freq_y = 8 * (me % 2) + lane // 16 + 16 * (4 * (me // 2) + row % 4)
    signed_y = jnp.where(freq_y < 2048, freq_y, freq_y - 4096).astype(F32) * (1.0 / 4096)
    square_y = signed_y * signed_y

    def step(place, carry):
        freq_x = base_x + 2 * place
        signed_x = jnp.where(freq_x < 1024, freq_x, freq_x - 2048).astype(F32) * (1.0 / 2048)
        squared = signed_x * signed_x + square_y
        turns = travel * squared / (wave + jnp.sqrt(wave * wave - squared))
        c, w = cos_sin_quarters(4.0 * turns)
        cos_ref[o, place] = c
        sin_ref[o, place] = w
        return carry

    lax.fori_loop(0, 64, step, 0, unroll=4)


def put_split(place, re, im, hi_ref, lo_ref):
    for part, value in enumerate((re, im)):
        hi, lo = split(value)
        lanes = pl.ds(part * 128, 128)
        hi_ref[place, :, lanes] = hi
        lo_ref[place, :, lanes] = lo


def columns(o, in_ref, matrix_ref, back_ref, twist_ref, cos_ref, sin_ref, out_ref, re_ref, im_ref, hi_ref, lo_ref):
    row = lax.broadcasted_iota(jnp.int32, (8, 128), 0)
    top = row < 4
    for n2 in range(8):
        column = []
        for n1 in range(8):
            s = 8 * n1 + n2
            a, b = decode(in_ref[s, o]), decode(in_ref[s + 64, o])
            total, delta = a + b, a - b
            re = jnp.where(top, total, pltpu.roll(delta, 4, 0))
            im = jnp.where(top, pltpu.roll(total, 4, 0), delta)
            if s > 0:
                angle = 2.0 * math.pi * s / 128
                c = jnp.where(top, 1.0, math.cos(angle))
                w = jnp.where(top, 0.0, math.sin(angle))
                re, im = re * c + im * w, im * c - re * w
            column.append((re, im))
        for m1, v in enumerate(fft8(column, -1.0)):
            re, im = scaled(v, -2.0 * math.pi * n2 * m1 / 64)
            re_ref[m1 * 8 + n2] = re
            im_ref[m1 * 8 + n2] = im
    for m1 in range(8):
        column = [(re_ref[m1 * 8 + n2], im_ref[m1 * 8 + n2]) for n2 in range(8)]
        for m2, (re, im) in enumerate(fft8(column, -1.0)):
            place = m1 + 8 * m2
            c, w = twist_ref[0, place], twist_ref[1, place]
            put_split(place, re * c - im * w, re * w + im * c, hi_ref, lo_ref)
    data = (hi_ref[...].reshape(512, 256), lo_ref[...].reshape(512, 256))
    spectrum = dot3(data, (matrix_ref[0], matrix_ref[1]), NN).reshape(64, 8, 256)
    for place in range(64):
        c, w = cos_ref[o, place], sin_ref[o, place]
        re, im = spectrum[place, :, :128], spectrum[place, :, 128:]
        put_split(place, re * c + im * w, im * c - re * w, hi_ref, lo_ref)
    data = (hi_ref[...].reshape(512, 256), lo_ref[...].reshape(512, 256))
    spectrum = dot3(data, (back_ref[0], back_ref[1]), NN).reshape(64, 8, 256)
    for m1 in range(8):
        column = []
        for m2 in range(8):
            place = m1 + 8 * m2
            re, im = spectrum[place, :, :128], spectrum[place, :, 128:]
            c, w = twist_ref[0, place], twist_ref[1, place]
            column.append((re * c + im * w, im * c - re * w))
        for n2, v in enumerate(fft8(column, 1.0)):
            re, im = scaled(v, 2.0 * math.pi * n2 * m1 / 64)
            re_ref[m1 * 8 + n2] = re
            im_ref[m1 * 8 + n2] = im
    for n2 in range(8):
        column = [(re_ref[m1 * 8 + n2], im_ref[m1 * 8 + n2]) for m1 in range(8)]
        for n1, (re, im) in enumerate(fft8(column, 1.0)):
            s = 8 * n1 + n2
            if s > 0:
                angle = 2.0 * math.pi * s / 128
                c = jnp.where(top, 1.0, math.cos(angle))
                w = jnp.where(top, 0.0, math.sin(angle))
                re, im = re * c - im * w, im * c + re * w
            total = jnp.where(top, re, pltpu.roll(im, 4, 0))
            delta = jnp.where(top, pltpu.roll(re, 4, 0), im)
            out_ref[s, o] = encode(total + delta)
            out_ref[s + 64, o] = encode(total - delta)


def rows_inverse(o, in_ref, matrix_ref, twist_ref, out_ref, value_ref):
    for h in range(2):
        hi, lo = split(decode(in_ref[:, h, o]).reshape(512, 128))
        rows = pl.ds(h * 128, 128)
        value_ref[rows, :] = dot3((hi, lo), (matrix_ref[0], matrix_ref[1]), TN)
    for half in range(2):
        cols = pl.ds(half * 128, 128)
        spectrum = []
        for k1 in range(16):
            rows = pl.ds(k1 * 16, 16)
            re = value_ref[rows, cols] * 2.0**-13
            im = value_ref[rows, pl.ds(256 + half * 128, 128)] * 2.0**-13
            if k1 > 0:
                c = twist_ref[0, pl.ds(k1, 1), cols]
                s = twist_ref[1, pl.ds(k1, 1), cols]
                re, im = re * c + im * s, im * c - re * s
            spectrum.append((re, im))
        for j, field in enumerate(fft16(spectrum, 1.0)):
            for part in range(2):
                out_ref[o, part, :, pl.ds(j * 256 + half * 128, 128)] = field[part].astype(BF16)


EDGE_ROW = (0, 6, 3)


def band(weight_ref, band_ref):
    x = lax.broadcasted_iota(jnp.int32, (32, 128), 0)
    lane = lax.broadcasted_iota(jnp.int32, (32, 128), 1)
    shift = lane % 64 - x - 15
    upper = lane < 64
    row = lax.broadcasted_iota(jnp.int32, (16, 128), 0)
    beyond = [(lane[:16] % 64 == source, u) for source, u in ((16, 2), (47, 0))]
    for pair in range(8):
        columns_of = pl.ds(pair * 128, 128)
        edges = [jnp.zeros((16, 128), F32), jnp.zeros((16, 128), F32)]
        for o in range(3):
            weights = [weight_ref[o, u].astype(F32) for u in range(3)]
            for v in range(3):
                value = jnp.zeros((32, 128), F32)
                for u in range(3):
                    c = 2 * pair
                    a = jnp.broadcast_to(weights[u][v : v + 1, c : c + 1], (32, 128))
                    b = jnp.broadcast_to(weights[u][v : v + 1, c + 1 : c + 2], (32, 128))
                    both = jnp.where(upper, a, b)
                    value = jnp.where(shift == u, both, value)
                    for n, (here, edge_u) in enumerate(beyond):
                        if u == edge_u:
                            edges[n] = jnp.where(here & (row == EDGE_ROW[v] + o), both[:16], edges[n])
                band_ref[(v * 3 + o) * 32 : (v * 3 + o) * 32 + 32, columns_of] = value.astype(BF16)
        for n in range(2):
            band_ref[288 + 16 * n : 304 + 16 * n, columns_of] = edges[n].astype(BF16)


def head(i, j, weight_ref, bias_ref, band_ref, tile_ref, sums_ref, sides_ref, edges_ref, got_sides_ref, got_edges_ref, got_corners_ref, phase_ref, down, border_sems, send_phase, meanwhile):
    band(weight_ref, band_ref)
    lane = lax.broadcasted_iota(jnp.int32, (32, 128), 1)
    to_right = jnp.zeros((32, 128), F32)
    to_left = jnp.zeros((32, 128), F32)
    for k in range(8):
        window = tile_ref[:, k * 32 : k * 32 + 64, :].reshape(1024, 256)
        count = 320 if k in (0, 7) else 288
        value = jnp.dot(band_ref[:count], window, preferred_element_type=F32)
        sums_ref[k] = value[:288].reshape(9, 32, 256)
        if k == 0:
            edges_ref[0] = value[288:304]
        if k == 7:
            edges_ref[1] = value[304:320]
        for o in range(3):
            to_right = jnp.where(lane == 3 * k + o, value[o * 32 : o * 32 + 32, 255:256], to_right)
            to_left = jnp.where(lane == 3 * k + o, value[192 + o * 32 : 224 + o * 32, 0:1], to_left)
    sides_ref[0] = to_right
    sides_ref[1] = to_left
    down()
    send_sems, recv_sems = border_sems
    copies = []
    for slot, step in enumerate((1, -1)):
        copies.append((sides_ref.at[slot], got_sides_ref.at[slot], i, (j + step + 16) % 16))
    for edge, down_step in enumerate((-1, 1)):
        row = (i + down_step + 8) % 8
        copies.append((edges_ref.at[edge], got_edges_ref.at[edge], row, j))
        for side, step in enumerate((1, -1)):
            corner = edges_ref.at[edge, pl.ds(0, 8), pl.ds(128 * (1 - side), 128)]
            copies.append((corner, got_corners_ref.at[edge * 2 + side], row, (j + step + 16) % 16))
    copies = [
        pltpu.make_async_remote_copy(
            src_ref=source, dst_ref=target, send_sem=send_sems.at[n], recv_sem=recv_sems.at[n],
            device_id=row * 16 + col, device_id_type=LOGICAL,
        )
        for n, (source, target, row, col) in enumerate(copies)
    ]
    for copy in copies:
        copy.start()
    meanwhile()
    for copy in copies:
        copy.wait()
    below, above = i < 7, i > 0
    left, right = j > 0, j < 15
    wide = lax.broadcasted_iota(jnp.int32, (32, 256), 1)
    tall = lax.broadcasted_iota(jnp.int32, (32, 1), 0)

    def rows_beyond(k, v, o):
        first = (tall == 0) & (k == 0) & above
        last = (tall == 31) & (k == 7) & below
        place = pl.ds(EDGE_ROW[v] + o, 1)
        top = got_edges_ref[1, place, :]
        bottom = got_edges_ref[0, place, :]
        return jnp.where(first, top, jnp.where(last, bottom, 0.0))

    def column_beyond(k, o, side):
        sides = got_sides_ref[side]
        value = jnp.sum(jnp.where(lane == 3 * k + o, sides, 0.0), axis=1, keepdims=True)
        first = (tall == 0) & (k == 0) & above
        last = (tall == 31) & (k == 7) & below
        place, y = pl.ds(EDGE_ROW[2 * side] + o, 1), 127 * (1 - side)
        top = got_corners_ref[2 + side, place, :][:, y : y + 1]
        bottom = got_corners_ref[side, place, :][:, y : y + 1]
        value = value + jnp.where(first, top, jnp.where(last, bottom, 0.0))
        return jnp.where(left if side == 0 else right, value, 0.0)

    for o in range(3):

        def block(step, carry):
            k = (j // 2 + step) % 8
            first = sums_ref[k, o] + rows_beyond(k, 0, o)
            middle = sums_ref[k, 3 + o] + rows_beyond(k, 1, o)
            last = sums_ref[k, 6 + o] + rows_beyond(k, 2, o)
            first = jnp.where(wide == 0, column_beyond(k, o, 0), pltpu.roll(first, 1, 1))
            last = jnp.where(wide == 255, column_beyond(k, o, 1), pltpu.roll(last, 255, 1))
            value = encode(jnp.tanh(first + middle + last + bias_ref[o]))
            phase_ref[o, 2 * k] = value[:16]
            phase_ref[o, 2 * k + 1] = value[16:]
            send_phase(o, 2 * k)
            send_phase(o, 2 * k + 1)
            return carry

        lax.fori_loop(0, 8, block, 0)


def spectral_kernel(
    weight_ref, bias_ref, wave_ref, travel_ref, features_ref,
    forward_hbm, lanes_hbm, back_hbm, twist_x_hbm, twist_y_ref,
    returned_ref,
    forward_ref, lanes_ref, back_ref, twist_x_ref,
    tile_ref, band_ref, sums_ref, sides_ref, edges_ref, got_sides_ref, got_edges_ref, got_corners_ref, phase_ref, got_phase_ref,
    packets_ref, spread_in_ref, filtered_ref, cos_ref, sin_ref, re_ref, im_ref, hi_ref, lo_ref, field_hi_ref, field_lo_ref,
    tile_sem, table_sems, border_send, border_recv, send_sems, recv_sems, local_sems,
):
    colors = 3
    i, j = lax.axis_index("row"), lax.axis_index("col")
    me = i * 16 + j
    down = enter(i, j)
    load = pltpu.make_async_copy(features_ref, tile_ref.at[:, pl.ds(16, 256), :], tile_sem)
    load.start()
    tables_in = []
    for n, (source, target) in enumerate(((forward_hbm, forward_ref), (lanes_hbm, lanes_ref), (back_hbm, back_ref), (twist_x_hbm, twist_x_ref))):
        tables_in.append(pltpu.make_async_copy(source, target, table_sems.at[n]))
        tables_in[n].start()
    tile_ref[:, 0:16, :] = jnp.zeros((16, 16, 256), BF16)
    tile_ref[:, 272:288, :] = jnp.zeros((16, 16, 256), BF16)
    load.wait()

    def each(body):
        def step(o, carry):
            body(o)
            return carry

        lax.fori_loop(0, colors, step, 0)

    def send_phase(o, peer):
        n = 2 + o

        @pl.when(peer == j)
        def _():
            pltpu.make_async_copy(phase_ref.at[o, peer], got_phase_ref.at[o, j], local_sems.at[n]).start()

        @pl.when(peer != j)
        def _():
            pltpu.make_async_remote_copy(
                src_ref=phase_ref.at[o, peer], dst_ref=got_phase_ref.at[o, j], send_sem=send_sems.at[n], recv_sem=recv_sems.at[n],
                device_id=i * 16 + peer, device_id_type=LOGICAL,
            ).start()

    head(
        i, j, weight_ref, bias_ref, band_ref, tile_ref, sums_ref, sides_ref, edges_ref, got_sides_ref, got_edges_ref, got_corners_ref, phase_ref,
        down, (border_send, border_recv), send_phase,
        lambda: each(lambda o: transfer(o, me, wave_ref[o], travel_ref[0], cos_ref, sin_ref)),
    )

    first = (send_sems.at[0], recv_sems.at[0], local_sems.at[0])
    second = (send_sems.at[1], recv_sems.at[1], local_sems.at[1])
    by_pair = packets_ref.reshape(64, 2, colors, 8, 128)

    def forward(o):
        wait_all(got_phase_ref.at[o], send_sems.at[2 + o], recv_sems.at[2 + o], local_sems.at[2 + o])
        rows_forward(o, got_phase_ref, forward_ref, twist_y_ref, by_pair, field_hi_ref, field_lo_ref)

    tables_in[0].wait()
    each(forward)
    send_all(me, lambda d: packets_ref.at[d], spread_in_ref, *first)
    for table in tables_in[1:]:
        table.wait()
    wait_all(spread_in_ref, *first)
    each(lambda o: columns(o, spread_in_ref, lanes_ref, back_ref, twist_x_ref, cos_ref, sin_ref, filtered_ref, re_ref, im_ref, hi_ref, lo_ref))
    send_all(me, lambda d: filtered_ref.at[d], returned_ref, *second)
    wait_all(returned_ref, *second)


def rows_inverse_kernel(returned_ref, matrix_ref, twist_ref, out_ref, value_ref, result_ref, sems):
    colors = result_ref.shape[0]
    by_pair = returned_ref.reshape(64, 2, colors, 8, 128)

    def step(o, carry):
        rows_inverse(o, by_pair, matrix_ref, twist_ref, result_ref, value_ref)
        pltpu.make_async_copy(result_ref.at[o], out_ref.at[o], sems.at[o]).start()
        return carry

    lax.fori_loop(0, colors, step, 0)
    for o in range(colors):
        pltpu.make_async_copy(result_ref.at[o], out_ref.at[o], sems.at[o]).wait()


def per_device(features, conv_weight, bias, wave, travel):
    table = tables()
    colors = 3
    names = ("forward_y", "lanes", "lanes_back", "twist_x", "twist_y")
    args = [jnp.asarray(table[k]) for k in names]
    smem = pl.BlockSpec(memory_space=pltpu.SMEM)
    vmem = pl.BlockSpec(memory_space=pltpu.VMEM)
    exchange = pltpu.VMEM((128, colors, 8, 128), BF16)
    returned = pl.pallas_call(
        spectral_kernel,
        in_specs=[vmem] + [smem] * 3 + [pl.BlockSpec(memory_space=pl.ANY)] * 5 + [vmem],
        out_specs=vmem,
        out_shape=pltpu.VMEM((128, colors, 8, 128), BF16),
        scratch_shapes=[
            *(pltpu.VMEM(a.shape, a.dtype) for a in args[:4]),
            pltpu.VMEM((16, 288, 256), BF16),
            pltpu.VMEM((320, 1024), BF16),
            pltpu.VMEM((8, 9, 32, 256), F32),
            pltpu.VMEM((2, 32, 128), F32),
            pltpu.VMEM((2, 16, 256), F32),
            pltpu.VMEM((2, 32, 128), F32),
            pltpu.VMEM((2, 16, 256), F32),
            pltpu.VMEM((4, 8, 128), F32),
            pltpu.VMEM((colors, 16, 16, 256), BF16),
            pltpu.VMEM((colors, 16, 16, 256), BF16),
            exchange, exchange, exchange,
            pltpu.VMEM((colors, 64, 8, 128), F32),
            pltpu.VMEM((colors, 64, 8, 128), F32),
            pltpu.VMEM((64, 8, 128), F32),
            pltpu.VMEM((64, 8, 128), F32),
            pltpu.VMEM((64, 8, 256), BF16),
            pltpu.VMEM((64, 8, 256), BF16),
            pltpu.VMEM((256, 512), BF16),
            pltpu.VMEM((256, 512), BF16),
            pltpu.SemaphoreType.DMA,
            pltpu.SemaphoreType.DMA((4,)),
            pltpu.SemaphoreType.DMA((8,)),
            pltpu.SemaphoreType.DMA((8,)),
            pltpu.SemaphoreType.DMA((5,)),
            pltpu.SemaphoreType.DMA((5,)),
            pltpu.SemaphoreType.DMA((5,)),
        ],
        compiler_params=pltpu.CompilerParams(collective_id=0, has_side_effects=True, vmem_limit_bytes=VMEM_LIMIT),
        name="spectral",
    )(conv_weight.transpose(0, 2, 3, 1), bias, wave, travel, features, *args)
    return pl.pallas_call(
        rows_inverse_kernel,
        in_specs=[vmem] * 3,
        out_specs=pl.BlockSpec(memory_space=pl.ANY),
        out_shape=jax.ShapeDtypeStruct((colors, 2, 16, 4096), BF16),
        scratch_shapes=[
            pltpu.VMEM((256, 512), F32),
            pltpu.VMEM((colors, 2, 16, 4096), BF16),
            pltpu.SemaphoreType.DMA((colors,)),
        ],
        compiler_params=pltpu.CompilerParams(vmem_limit_bytes=16 * 1024 * 1024),
        name="rows_inverse",
    )(returned, args[0], args[4])


def solution(mesh):
    in_specs = (P(None, "row", "col"), P(), P(), P(), P())
    out_specs = P(None, None, ("row", "col"), None)
    return jax.shard_map(
        per_device, mesh=mesh, in_specs=in_specs, out_specs=out_specs, check_vma=False
    )
```

```python
import functools
import math

import jax
import jax.numpy as jnp
import numpy as np
from jax import lax
from jax.experimental import pallas as pl
from jax.experimental.pallas import tpu as pltpu
from jax.sharding import PartitionSpec as P

F32 = jnp.float32
BF16 = jnp.bfloat16
VMEM_LIMIT = 56 * 1024 * 1024


def split_np(table):
    hi = table.astype(np.float32).astype(jnp.bfloat16)
    lo = (table - hi.astype(np.float64)).astype(np.float32).astype(jnp.bfloat16)
    return np.stack([np.asarray(hi), np.asarray(lo)])


def rotation_np(theta):
    return np.array([[np.cos(theta), np.sin(theta)], [-np.sin(theta), np.cos(theta)]])


def tables():
    k2 = np.arange(256)
    b = np.arange(256)
    rot = rotation_np(2.0 * np.pi * ((k2[:, None] * b[None, :]) % 256) / 256.0)
    forward_y = rot.reshape(2, 2, 64, 4, 256).transpose(2, 0, 3, 1, 4).reshape(512, 512)
    j = np.arange(16)
    rot16 = rotation_np(2.0 * np.pi * ((j[:, None] * j[None, :]) % 16) / 16.0)
    back16 = np.stack([np.stack([rot16[0, 0], -rot16[0, 1]]), np.stack([-rot16[1, 0], rot16[1, 1]])])
    lanes = np.einsum("pqab,cd->qcbpda", rot16, np.eye(8)).reshape(256, 256)
    lanes_back = np.einsum("pqab,cd->qcbpda", back16, np.eye(8)).reshape(256, 256)
    k1 = np.arange(16)
    angle = 2.0 * np.pi * ((k1[:, None] * b[None, :]) % 4096) / 4096.0
    twist_y = np.stack([np.cos(angle), -np.sin(angle)]).astype(np.float32)
    p = np.arange(128).reshape(64, 2)
    r = np.arange(16)
    angle = 2.0 * np.pi * ((p[:, :, None] * r) % 2048) / 2048.0
    twist_x = np.stack([np.cos(angle), -np.sin(angle)])
    twist_x = np.broadcast_to(twist_x[:, :, :, None, None, :], (2, 64, 2, 4, 8, 16))
    twist_x = twist_x.reshape(2, 64, 8, 128).astype(np.float32)
    return {
        "forward_y": split_np(forward_y * 8.0),
        "lanes": split_np(lanes),
        "lanes_back": split_np(lanes_back * 2.0**-16),
        "twist_y": twist_y,
        "twist_x": twist_x,
    }


def encode(x):
    x = x * jnp.abs(x)
    x = x * jnp.abs(x)
    x = x * jnp.abs(x)
    return x.astype(BF16)


def decode(y):
    y = y.astype(F32)
    root = jnp.exp2(jnp.log2(jnp.abs(y)) * 0.125)
    return jnp.where(y < 0.0, -root, root)


def split(x):
    hi = x.astype(BF16)
    return hi, (x - hi.astype(F32)).astype(BF16)


def cos_sin_quarters(u):
    n = jnp.round(u)
    f = u - n
    n = n.astype(jnp.int32)
    z = f * f
    s = f * (1.5707963267948966 + z * (-0.6459640975062462 + z * (0.07969262624616703 + z * (-0.004681754135318688 + z * 0.00016044118478735982))))
    c = 1.0 + z * (-1.2337005501361697 + z * (0.253669507901048 + z * (-0.020863480763352960 + z * (0.0009192602748394265 - z * 2.5202042373060605e-05))))
    swap = (n & 1) == 1
    cos = jnp.where(swap, s, c)
    sin = jnp.where(swap, c, s)
    cos = jnp.where(((n + 1) & 2) == 2, -cos, cos)
    sin = jnp.where((n & 2) == 2, -sin, sin)
    return cos, sin


def fft4(x, sign):
    (ar, ai), (br, bi), (cr, ci), (dr, di) = x
    sr, si, tr, ti = ar + cr, ai + ci, ar - cr, ai - ci
    ur, ui, vr, vi = br + dr, bi + di, br - dr, bi - di
    if sign < 0:
        vr, vi = vi, -vr
    else:
        vr, vi = -vi, vr
    return [(sr + ur, si + ui), (tr + vr, ti + vi), (sr - ur, si - ui), (tr - vr, ti - vi)]


def scaled(x, angle):
    turn = angle / (0.5 * math.pi)
    xr, xi = x
    if abs(turn - round(turn)) < 1e-9:
        case = int(round(turn)) % 4
        return [(xr, xi), (-xi, xr), (-xr, -xi), (xi, -xr)][case]
    c, s = math.cos(angle), math.sin(angle)
    eighth = turn * 2
    if abs(eighth - round(eighth)) < 1e-9:
        case = int(round(eighth)) % 8
        h = math.sqrt(0.5)
        if case == 1:
            return ((xr - xi) * h, (xr + xi) * h)
        if case == 3:
            return ((xr + xi) * -h, (xr - xi) * h)
        if case == 5:
            return ((xi - xr) * h, (xr + xi) * -h)
        return ((xr + xi) * h, (xi - xr) * h)
    return (xr * c - xi * s, xr * s + xi * c)


def fft8(x, sign):
    even = fft4(x[0::2], sign)
    odd = fft4(x[1::2], sign)
    odd = [scaled(v, sign * 2.0 * math.pi * k / 8) for k, v in enumerate(odd)]
    first = [(a[0] + b[0], a[1] + b[1]) for a, b in zip(even, odd)]
    return first + [(a[0] - b[0], a[1] - b[1]) for a, b in zip(even, odd)]


def fft16(x, sign):
    inner = [fft4([x[4 * n1 + n2] for n1 in range(4)], sign) for n2 in range(4)]
    out = [None] * 16
    for k1 in range(4):
        column = [scaled(inner[n2][k1], sign * 2.0 * math.pi * n2 * k1 / 16) for n2 in range(4)]
        for k2, v in enumerate(fft4(column, sign)):
            out[k1 + 4 * k2] = v
    return out


def dot3(lhs, rhs, dims):
    left = jnp.concatenate([lhs[0], lhs[1], lhs[0]], axis=dims[0][0])
    right = jnp.concatenate([rhs[0], rhs[0], rhs[1]], axis=dims[1][0])
    return lax.dot_general(left, right, (dims, ((), ())), preferred_element_type=F32)


NN = ((1,), (0,))
NT = ((1,), (1,))
TN = ((0,), (0,))


LOGICAL = pl.DeviceIdType.LOGICAL


def enter(i, j):
    barrier = pltpu.get_barrier_semaphore()

    def signal(row, col):
        pl.semaphore_signal(barrier, inc=1, device_id=row * 16 + col, device_id_type=LOGICAL)

    for step in range(1, 16):
        signal(i, (j + step) % 16)
    for step in range(1, 8):
        signal((i + step) % 8, j)
    for row in (7, 1):
        for col in (15, 1):
            signal((i + row) % 8, (j + col) % 16)

    def down():
        pl.semaphore_wait(barrier, 26)

    return down


def send_all(me, block_of, landing, send_sem, recv_sem, local_sem):
    pltpu.make_async_copy(block_of(me), landing.at[me], local_sem).start()

    turn = 1 - 2 * (me % 2)

    def one(k):
        peer = (me + turn * (k * 85)) % 128
        pltpu.make_async_remote_copy(
            src_ref=block_of(peer),
            dst_ref=landing.at[me],
            send_sem=send_sem,
            recv_sem=recv_sem,
            device_id=peer,
            device_id_type=LOGICAL,
        ).start()

    def group(g, carry):
        for k in range(8):
            one(8 * g + k)
        return carry

    for k in range(1, 8):
        one(k)
    lax.fori_loop(1, 16, group, 0)


def wait_all(landing, send_sem, recv_sem, local_sem):
    pltpu.make_async_copy(landing.at[0], landing.at[0], local_sem).wait()
    others = landing.at[pl.ds(0, landing.shape[0] - 1)]
    pltpu.make_async_copy(others, others, send_sem).wait()
    pltpu.make_async_copy(others, others, recv_sem).wait()


def rows_forward(o, phase_ref, matrix_ref, twist_ref, out_ref, hi_ref, lo_ref):
    for half in range(2):
        cols = pl.ds(half * 128, 128)
        field = []
        for j in range(16):
            field.append(cos_sin_quarters(2.0 * decode(phase_ref[o, j, :, cols])))
        spectrum = fft16(field, -1.0)
        for k1 in range(16):
            re, im = spectrum[k1]
            if k1 > 0:
                c = twist_ref[0, pl.ds(k1, 1), cols]
                s = twist_ref[1, pl.ds(k1, 1), cols]
                re, im = re * c - im * s, re * s + im * c
            rows = pl.ds(k1 * 16, 16)
            for part, value in enumerate((re, im)):
                hi, lo = split(value)
                place = pl.ds(part * 256 + half * 128, 128)
                hi_ref[rows, place] = hi
                lo_ref[rows, place] = lo
    result = dot3((matrix_ref[0], matrix_ref[1]), (hi_ref[...], lo_ref[...]), NT)
    for h in range(2):
        out_ref[:, h, o] = encode(result[:, h * 128 : (h + 1) * 128]).reshape(64, 8, 128)


def transfer(o, me, wave, travel, cos_ref, sin_ref):
    row = lax.broadcasted_iota(jnp.int32, (8, 128), 0)
    lane = lax.broadcasted_iota(jnp.int32, (8, 128), 1)
    base_x = (row // 4) + 128 * (lane % 16)
    freq_y = 8 * (me % 2) + lane // 16 + 16 * (4 * (me // 2) + row % 4)
    signed_y = jnp.where(freq_y < 2048, freq_y, freq_y - 4096).astype(F32) * (1.0 / 4096)
    square_y = signed_y * signed_y

    def step(place, carry):
        freq_x = base_x + 2 * place
        signed_x = jnp.where(freq_x < 1024, freq_x, freq_x - 2048).astype(F32) * (1.0 / 2048)
        squared = signed_x * signed_x + square_y
        turns = travel * squared / (wave + jnp.sqrt(wave * wave - squared))
        c, w = cos_sin_quarters(4.0 * turns)
        cos_ref[o, place] = c
        sin_ref[o, place] = w
        return carry

    lax.fori_loop(0, 64, step, 0, unroll=4)


def put_split(place, re, im, hi_ref, lo_ref):
    for part, value in enumerate((re, im)):
        hi, lo = split(value)
        lanes = pl.ds(part * 128, 128)
        hi_ref[place, :, lanes] = hi
        lo_ref[place, :, lanes] = lo


def columns(o, in_ref, matrix_ref, back_ref, twist_ref, cos_ref, sin_ref, out_ref, re_ref, im_ref, hi_ref, lo_ref):
    row = lax.broadcasted_iota(jnp.int32, (8, 128), 0)
    top = row < 4
    for n2 in range(8):
        column = []
        for n1 in range(8):
            s = 8 * n1 + n2
            a, b = decode(in_ref[s, o]), decode(in_ref[s + 64, o])
            total, delta = a + b, a - b
            re = jnp.where(top, total, pltpu.roll(delta, 4, 0))
            im = jnp.where(top, pltpu.roll(total, 4, 0), delta)
            if s > 0:
                angle = 2.0 * math.pi * s / 128
                c = jnp.where(top, 1.0, math.cos(angle))
                w = jnp.where(top, 0.0, math.sin(angle))
                re, im = re * c + im * w, im * c - re * w
            column.append((re, im))
        for m1, v in enumerate(fft8(column, -1.0)):
            re, im = scaled(v, -2.0 * math.pi * n2 * m1 / 64)
            re_ref[m1 * 8 + n2] = re
            im_ref[m1 * 8 + n2] = im
    for m1 in range(8):
        column = [(re_ref[m1 * 8 + n2], im_ref[m1 * 8 + n2]) for n2 in range(8)]
        for m2, (re, im) in enumerate(fft8(column, -1.0)):
            place = m1 + 8 * m2
            c, w = twist_ref[0, place], twist_ref[1, place]
            put_split(place, re * c - im * w, re * w + im * c, hi_ref, lo_ref)
    data = (hi_ref[...].reshape(512, 256), lo_ref[...].reshape(512, 256))
    spectrum = dot3(data, (matrix_ref[0], matrix_ref[1]), NN).reshape(64, 8, 256)
    for place in range(64):
        c, w = cos_ref[o, place], sin_ref[o, place]
        re, im = spectrum[place, :, :128], spectrum[place, :, 128:]
        put_split(place, re * c + im * w, im * c - re * w, hi_ref, lo_ref)
    data = (hi_ref[...].reshape(512, 256), lo_ref[...].reshape(512, 256))
    spectrum = dot3(data, (back_ref[0], back_ref[1]), NN).reshape(64, 8, 256)
    for m1 in range(8):
        column = []
        for m2 in range(8):
            place = m1 + 8 * m2
            re, im = spectrum[place, :, :128], spectrum[place, :, 128:]
            c, w = twist_ref[0, place], twist_ref[1, place]
            column.append((re * c + im * w, im * c - re * w))
        for n2, v in enumerate(fft8(column, 1.0)):
            re, im = scaled(v, 2.0 * math.pi * n2 * m1 / 64)
            re_ref[m1 * 8 + n2] = re
            im_ref[m1 * 8 + n2] = im
    for n2 in range(8):
        column = [(re_ref[m1 * 8 + n2], im_ref[m1 * 8 + n2]) for m1 in range(8)]
        for n1, (re, im) in enumerate(fft8(column, 1.0)):
            s = 8 * n1 + n2
            if s > 0:
                angle = 2.0 * math.pi * s / 128
                c = jnp.where(top, 1.0, math.cos(angle))
                w = jnp.where(top, 0.0, math.sin(angle))
                re, im = re * c - im * w, im * c + re * w
            total = jnp.where(top, re, pltpu.roll(im, 4, 0))
            delta = jnp.where(top, pltpu.roll(re, 4, 0), im)
            out_ref[s, o] = encode(total + delta)
            out_ref[s + 64, o] = encode(total - delta)


def rows_inverse(o, in_ref, matrix_ref, twist_ref, out_ref, value_ref):
    for h in range(2):
        hi, lo = split(decode(in_ref[:, h, o]).reshape(512, 128))
        rows = pl.ds(h * 128, 128)
        value_ref[rows, :] = dot3((hi, lo), (matrix_ref[0], matrix_ref[1]), TN)
    for half in range(2):
        cols = pl.ds(half * 128, 128)
        spectrum = []
        for k1 in range(16):
            rows = pl.ds(k1 * 16, 16)
            re = value_ref[rows, cols] * 2.0**-13
            im = value_ref[rows, pl.ds(256 + half * 128, 128)] * 2.0**-13
            if k1 > 0:
                c = twist_ref[0, pl.ds(k1, 1), cols]
                s = twist_ref[1, pl.ds(k1, 1), cols]
                re, im = re * c + im * s, im * c - re * s
            spectrum.append((re, im))
        for j, field in enumerate(fft16(spectrum, 1.0)):
            for part in range(2):
                out_ref[o, part, :, pl.ds(j * 256 + half * 128, 128)] = field[part].astype(BF16)


EDGE_ROW = (0, 6, 3)


def band(weight_ref, band_ref):
    x = lax.broadcasted_iota(jnp.int32, (32, 128), 0)
    lane = lax.broadcasted_iota(jnp.int32, (32, 128), 1)
    shift = lane % 64 - x - 15
    upper = lane < 64
    row = lax.broadcasted_iota(jnp.int32, (16, 128), 0)
    beyond = [(lane[:16] % 64 == source, u) for source, u in ((16, 2), (47, 0))]
    for pair in range(8):
        columns_of = pl.ds(pair * 128, 128)
        edges = [jnp.zeros((16, 128), F32), jnp.zeros((16, 128), F32)]
        for o in range(3):
            weights = [weight_ref[o, u].astype(F32) for u in range(3)]
            for v in range(3):
                value = jnp.zeros((32, 128), F32)
                for u in range(3):
                    c = 2 * pair
                    a = jnp.broadcast_to(weights[u][v : v + 1, c : c + 1], (32, 128))
                    b = jnp.broadcast_to(weights[u][v : v + 1, c + 1 : c + 2], (32, 128))
                    both = jnp.where(upper, a, b)
                    value = jnp.where(shift == u, both, value)
                    for n, (here, edge_u) in enumerate(beyond):
                        if u == edge_u:
                            edges[n] = jnp.where(here & (row == EDGE_ROW[v] + o), both[:16], edges[n])
                band_ref[(v * 3 + o) * 32 : (v * 3 + o) * 32 + 32, columns_of] = value.astype(BF16)
        for n in range(2):
            band_ref[288 + 16 * n : 304 + 16 * n, columns_of] = edges[n].astype(BF16)


PHASE_ORDER = ((1, 0), (0, 1), (3, 0), (1, 1), (2, 0), (3, 1), (2, 1), (0, 0))


def head(i, j, weight_ref, bias_ref, band_ref, tile_ref, sums_ref, sides_ref, edges_ref, got_sides_ref, got_edges_ref, got_corners_ref, phase_ref, down, border_sems, send_phase, meanwhile):
    band(weight_ref, band_ref)
    lane = lax.broadcasted_iota(jnp.int32, (32, 128), 1)
    tall = lax.broadcasted_iota(jnp.int32, (32, 128), 0)
    to_right = jnp.zeros((32, 128), F32)
    to_left = jnp.zeros((32, 128), F32)
    for k in range(8):
        window = tile_ref[:, k * 32 : k * 32 + 64, :].reshape(1024, 256)
        count = 320 if k in (0, 7) else 288
        value = jnp.dot(band_ref[:count], window, preferred_element_type=F32)
        sums_ref[k] = value[:288].reshape(9, 32, 256)
        if k == 0:
            edges_ref[0] = value[288:304]
        if k == 7:
            edges_ref[1] = value[304:320]
        for o in range(3):
            to_right = jnp.where(lane == 3 * k + o, value[o * 32 : o * 32 + 32, 255:256], to_right)
            to_left = jnp.where(lane == 3 * k + o, value[192 + o * 32 : 224 + o * 32, 0:1], to_left)
    sides_ref[0] = to_right
    sides_ref[1] = to_left
    down()
    send_sems, recv_sems = border_sems
    copies = []
    for slot, step in enumerate((1, -1)):
        copies.append((sides_ref.at[slot], got_sides_ref.at[slot], i, (j + step + 16) % 16))
    for edge, down_step in enumerate((-1, 1)):
        row = (i + down_step + 8) % 8
        copies.append((edges_ref.at[edge], got_edges_ref.at[edge], row, j))
        for side, step in enumerate((1, -1)):
            corner = edges_ref.at[edge, pl.ds(0, 8), pl.ds(128 * (1 - side), 128)]
            copies.append((corner, got_corners_ref.at[edge * 2 + side], row, (j + step + 16) % 16))
    copies = [
        pltpu.make_async_remote_copy(
            src_ref=source, dst_ref=target, send_sem=send_sems.at[n], recv_sem=recv_sems.at[n],
            device_id=row * 16 + col, device_id_type=LOGICAL,
        )
        for n, (source, target, row, col) in enumerate(copies)
    ]
    for copy in copies:
        copy.start()
    meanwhile()
    for copy in copies:
        copy.wait()
    below, above = i < 7, i > 0
    left, right = j > 0, j < 15
    wide = lax.broadcasted_iota(jnp.int32, (32, 256), 1)
    row = lax.broadcasted_iota(jnp.int32, (8, 256), 0)
    for edge, (k, rows, here) in enumerate(((7, pl.ds(24, 8), (row == 7) & below), (0, pl.ds(0, 8), (row == 0) & above))):
        for v in range(3):
            for o in range(3):
                beyond = got_edges_ref[edge, pl.ds(EDGE_ROW[v] + o, 1), :]
                sums_ref[k, v * 3 + o, rows, :] += jnp.where(here, beyond, 0.0)
    for side, there in enumerate((left, right)):
        column = got_sides_ref[side]
        for edge, (k, x, inside) in enumerate(((7, 31, below), (0, 0, above))):
            corners = got_corners_ref[edge * 2 + side]
            for o in range(3):
                y = 127 * (1 - side)
                corner = corners[EDGE_ROW[2 * side] + o : EDGE_ROW[2 * side] + o + 1, y : y + 1]
                here = (lane == 3 * k + o) & (tall == x) & inside
                column = column + jnp.where(here, corner, 0.0)
        got_sides_ref[side] = jnp.where(there, column, 0.0)

    turn = 1 - 2 * (j % 2)
    for o in range(3):

        def block(k):
            index = 3 * k + o
            before = pltpu.roll(got_sides_ref[0], 128 - index, 1)
            after = pltpu.roll(got_sides_ref[1], 127 - index, 1)
            first = pltpu.roll(sums_ref[k, o], 1, 1)
            last = pltpu.roll(sums_ref[k, 6 + o], 255, 1)
            first = jnp.where(wide == 0, jnp.concatenate([before, before], 1), first)
            last = jnp.where(wide == 255, jnp.concatenate([after, after], 1), last)
            value = encode(jnp.tanh(first + last + (sums_ref[k, 3 + o] + bias_ref[o])))
            phase_ref[o, 2 * k] = value[:16]
            phase_ref[o, 2 * k + 1] = value[16:]
            send_phase(o, 2 * k)
            send_phase(o, 2 * k + 1)

        for x_step, z_step in PHASE_ORDER:
            block(((j // 8 + z_step) % 2) * 4 + (j // 2 + turn * x_step) % 4)


def spectral_kernel(
    weight_ref, bias_ref, wave_ref, travel_ref, features_ref,
    forward_hbm, lanes_hbm, back_hbm, twist_x_hbm, twist_y_ref,
    returned_ref,
    forward_ref, lanes_ref, back_ref, twist_x_ref,
    tile_ref, band_ref, sums_ref, sides_ref, edges_ref, got_sides_ref, got_edges_ref, got_corners_ref, phase_ref, got_phase_ref,
    packets_ref, spread_in_ref, filtered_ref, cos_ref, sin_ref, re_ref, im_ref, hi_ref, lo_ref, field_hi_ref, field_lo_ref,
    tile_sem, table_sems, border_send, border_recv, send_sems, recv_sems, local_sems,
):
    colors = 3
    i, j = lax.axis_index("row"), lax.axis_index("col")
    me = i * 16 + j
    down = enter(i, j)
    load = pltpu.make_async_copy(features_ref, tile_ref.at[:, pl.ds(16, 256), :], tile_sem)
    load.start()
    tables_in = []
    for n, (source, target) in enumerate(((forward_hbm, forward_ref), (lanes_hbm, lanes_ref), (back_hbm, back_ref), (twist_x_hbm, twist_x_ref))):
        tables_in.append(pltpu.make_async_copy(source, target, table_sems.at[n]))
        tables_in[n].start()
    tile_ref[:, 0:16, :] = jnp.zeros((16, 16, 256), BF16)
    tile_ref[:, 272:288, :] = jnp.zeros((16, 16, 256), BF16)
    load.wait()

    def each(body):
        def step(o, carry):
            body(o)
            return carry

        lax.fori_loop(0, colors, step, 0)

    def send_phase(o, peer):
        n = 2 + o

        @pl.when(peer == j)
        def _():
            pltpu.make_async_copy(phase_ref.at[o, peer], got_phase_ref.at[o, j], local_sems.at[n]).start()

        @pl.when(peer != j)
        def _():
            pltpu.make_async_remote_copy(
                src_ref=phase_ref.at[o, peer], dst_ref=got_phase_ref.at[o, j], send_sem=send_sems.at[n], recv_sem=recv_sems.at[n],
                device_id=i * 16 + peer, device_id_type=LOGICAL,
            ).start()

    head(
        i, j, weight_ref, bias_ref, band_ref, tile_ref, sums_ref, sides_ref, edges_ref, got_sides_ref, got_edges_ref, got_corners_ref, phase_ref,
        down, (border_send, border_recv), send_phase,
        lambda: each(lambda o: transfer(o, me, wave_ref[o], travel_ref[0], cos_ref, sin_ref)),
    )

    first = (send_sems.at[0], recv_sems.at[0], local_sems.at[0])
    second = (send_sems.at[1], recv_sems.at[1], local_sems.at[1])
    by_pair = packets_ref.reshape(64, 2, colors, 8, 128)

    def forward(o):
        wait_all(got_phase_ref.at[o], send_sems.at[2 + o], recv_sems.at[2 + o], local_sems.at[2 + o])
        rows_forward(o, got_phase_ref, forward_ref, twist_y_ref, by_pair, field_hi_ref, field_lo_ref)

    tables_in[0].wait()
    each(forward)
    send_all(me, lambda d: packets_ref.at[d], spread_in_ref, *first)
    for table in tables_in[1:]:
        table.wait()
    wait_all(spread_in_ref, *first)
    each(lambda o: columns(o, spread_in_ref, lanes_ref, back_ref, twist_x_ref, cos_ref, sin_ref, filtered_ref, re_ref, im_ref, hi_ref, lo_ref))
    send_all(me, lambda d: filtered_ref.at[d], returned_ref, *second)
    wait_all(returned_ref, *second)


def rows_inverse_kernel(returned_ref, matrix_ref, twist_ref, out_ref, value_ref, result_ref, sems):
    colors = result_ref.shape[0]
    by_pair = returned_ref.reshape(64, 2, colors, 8, 128)

    def step(o, carry):
        rows_inverse(o, by_pair, matrix_ref, twist_ref, result_ref, value_ref)
        pltpu.make_async_copy(result_ref.at[o], out_ref.at[o], sems.at[o]).start()
        return carry

    lax.fori_loop(0, colors, step, 0)
    for o in range(colors):
        pltpu.make_async_copy(result_ref.at[o], out_ref.at[o], sems.at[o]).wait()


def per_device(features, conv_weight, bias, wave, travel):
    table = tables()
    colors = 3
    names = ("forward_y", "lanes", "lanes_back", "twist_x", "twist_y")
    args = [jnp.asarray(table[k]) for k in names]
    smem = pl.BlockSpec(memory_space=pltpu.SMEM)
    vmem = pl.BlockSpec(memory_space=pltpu.VMEM)
    exchange = pltpu.VMEM((128, colors, 8, 128), BF16)
    returned = pl.pallas_call(
        spectral_kernel,
        in_specs=[vmem] + [smem] * 3 + [pl.BlockSpec(memory_space=pl.ANY)] * 5 + [vmem],
        out_specs=vmem,
        out_shape=pltpu.VMEM((128, colors, 8, 128), BF16),
        scratch_shapes=[
            *(pltpu.VMEM(a.shape, a.dtype) for a in args[:4]),
            pltpu.VMEM((16, 288, 256), BF16),
            pltpu.VMEM((320, 1024), BF16),
            pltpu.VMEM((8, 9, 32, 256), F32),
            pltpu.VMEM((2, 32, 128), F32),
            pltpu.VMEM((2, 16, 256), F32),
            pltpu.VMEM((2, 32, 128), F32),
            pltpu.VMEM((2, 16, 256), F32),
            pltpu.VMEM((4, 8, 128), F32),
            pltpu.VMEM((colors, 16, 16, 256), BF16),
            pltpu.VMEM((colors, 16, 16, 256), BF16),
            exchange, exchange, exchange,
            pltpu.VMEM((colors, 64, 8, 128), F32),
            pltpu.VMEM((colors, 64, 8, 128), F32),
            pltpu.VMEM((64, 8, 128), F32),
            pltpu.VMEM((64, 8, 128), F32),
            pltpu.VMEM((64, 8, 256), BF16),
            pltpu.VMEM((64, 8, 256), BF16),
            pltpu.VMEM((256, 512), BF16),
            pltpu.VMEM((256, 512), BF16),
            pltpu.SemaphoreType.DMA,
            pltpu.SemaphoreType.DMA((4,)),
            pltpu.SemaphoreType.DMA((8,)),
            pltpu.SemaphoreType.DMA((8,)),
            pltpu.SemaphoreType.DMA((5,)),
            pltpu.SemaphoreType.DMA((5,)),
            pltpu.SemaphoreType.DMA((5,)),
        ],
        compiler_params=pltpu.CompilerParams(collective_id=0, has_side_effects=True, vmem_limit_bytes=VMEM_LIMIT),
        name="spectral",
    )(conv_weight.transpose(0, 2, 3, 1), bias, wave, travel, features, *args)
    return pl.pallas_call(
        rows_inverse_kernel,
        in_specs=[vmem] * 3,
        out_specs=pl.BlockSpec(memory_space=pl.ANY),
        out_shape=jax.ShapeDtypeStruct((colors, 2, 16, 4096), BF16),
        scratch_shapes=[
            pltpu.VMEM((256, 512), F32),
            pltpu.VMEM((colors, 2, 16, 4096), BF16),
            pltpu.SemaphoreType.DMA((colors,)),
        ],
        compiler_params=pltpu.CompilerParams(vmem_limit_bytes=16 * 1024 * 1024),
        name="rows_inverse",
    )(returned, args[0], args[4])


def solution(mesh):
    in_specs = (P(None, "row", "col"), P(), P(), P(), P())
    out_specs = P(None, None, ("row", "col"), None)
    return jax.shard_map(
        per_device, mesh=mesh, in_specs=in_specs, out_specs=out_specs, check_vma=False
    )
```

```python
import functools
import math

import jax
import jax.numpy as jnp
import numpy as np
from jax import lax
from jax.experimental import pallas as pl
from jax.experimental.pallas import tpu as pltpu
from jax.sharding import PartitionSpec as P

F32 = jnp.float32
BF16 = jnp.bfloat16
VMEM_LIMIT = 56 * 1024 * 1024


def split_np(table):
    hi = table.astype(np.float32).astype(jnp.bfloat16)
    lo = (table - hi.astype(np.float64)).astype(np.float32).astype(jnp.bfloat16)
    return np.stack([np.asarray(hi), np.asarray(lo)])


def rotation_np(theta):
    return np.array([[np.cos(theta), np.sin(theta)], [-np.sin(theta), np.cos(theta)]])


def tables():
    k2 = np.arange(256)
    b = np.arange(256)
    rot = rotation_np(2.0 * np.pi * ((k2[:, None] * b[None, :]) % 256) / 256.0)
    forward_y = rot.reshape(2, 2, 64, 4, 256).transpose(2, 0, 3, 1, 4).reshape(512, 512)
    j = np.arange(16)
    rot16 = rotation_np(2.0 * np.pi * ((j[:, None] * j[None, :]) % 16) / 16.0)
    back16 = np.stack([np.stack([rot16[0, 0], -rot16[0, 1]]), np.stack([-rot16[1, 0], rot16[1, 1]])])
    lanes = np.einsum("pqab,cd->qcbpda", rot16, np.eye(8)).reshape(256, 256)
    lanes_back = np.einsum("pqab,cd->qcbpda", back16, np.eye(8)).reshape(256, 256)
    k1 = np.arange(16)
    angle = 2.0 * np.pi * ((k1[:, None] * b[None, :]) % 4096) / 4096.0
    twist_y = np.stack([np.cos(angle), -np.sin(angle)]).astype(np.float32)
    p = np.arange(128).reshape(64, 2)
    r = np.arange(16)
    angle = 2.0 * np.pi * ((p[:, :, None] * r) % 2048) / 2048.0
    twist_x = np.stack([np.cos(angle), -np.sin(angle)])
    twist_x = np.broadcast_to(twist_x[:, :, :, None, None, :], (2, 64, 2, 4, 8, 16))
    twist_x = twist_x.reshape(2, 64, 8, 128).astype(np.float32)
    s = np.arange(64)
    pairs = np.stack([np.cos(2.0 * np.pi * s / 128), np.sin(2.0 * np.pi * s / 128)]).astype(np.float32)
    turn = 2.0 * np.pi * ((s // 8) * (s % 8)) / 64.0
    turns = np.stack([np.cos(turn), np.sin(turn)]).astype(np.float32)
    return {
        "pairs": pairs,
        "turns": turns,
        "forward_y": split_np(forward_y * 8.0),
        "lanes": split_np(lanes),
        "lanes_back": split_np(lanes_back * 2.0**-16),
        "twist_y": twist_y,
        "twist_x": twist_x,
    }


def encode(x):
    x = x * jnp.abs(x)
    x = x * jnp.abs(x)
    x = x * jnp.abs(x)
    return x.astype(BF16)


def decode(y):
    y = y.astype(F32)
    root = jnp.exp2(jnp.log2(jnp.abs(y)) * 0.125)
    return jnp.where(y < 0.0, -root, root)


def split(x):
    hi = x.astype(BF16)
    return hi, (x - hi.astype(F32)).astype(BF16)


def cos_sin_quarters(u):
    n = jnp.round(u)
    f = u - n
    n = n.astype(jnp.int32)
    z = f * f
    s = f * (1.5707963267948966 + z * (-0.6459640975062462 + z * (0.07969262624616703 + z * (-0.004681754135318688 + z * 0.00016044118478735982))))
    c = 1.0 + z * (-1.2337005501361697 + z * (0.253669507901048 + z * (-0.020863480763352960 + z * (0.0009192602748394265 - z * 2.5202042373060605e-05))))
    swap = (n & 1) == 1
    cos = jnp.where(swap, s, c)
    sin = jnp.where(swap, c, s)
    cos = jnp.where(((n + 1) & 2) == 2, -cos, cos)
    sin = jnp.where((n & 2) == 2, -sin, sin)
    return cos, sin


def fft4(x, sign):
    (ar, ai), (br, bi), (cr, ci), (dr, di) = x
    sr, si, tr, ti = ar + cr, ai + ci, ar - cr, ai - ci
    ur, ui, vr, vi = br + dr, bi + di, br - dr, bi - di
    if sign < 0:
        vr, vi = vi, -vr
    else:
        vr, vi = -vi, vr
    return [(sr + ur, si + ui), (tr + vr, ti + vi), (sr - ur, si - ui), (tr - vr, ti - vi)]


def scaled(x, angle):
    turn = angle / (0.5 * math.pi)
    xr, xi = x
    if abs(turn - round(turn)) < 1e-9:
        case = int(round(turn)) % 4
        return [(xr, xi), (-xi, xr), (-xr, -xi), (xi, -xr)][case]
    c, s = math.cos(angle), math.sin(angle)
    eighth = turn * 2
    if abs(eighth - round(eighth)) < 1e-9:
        case = int(round(eighth)) % 8
        h = math.sqrt(0.5)
        if case == 1:
            return ((xr - xi) * h, (xr + xi) * h)
        if case == 3:
            return ((xr + xi) * -h, (xr - xi) * h)
        if case == 5:
            return ((xi - xr) * h, (xr + xi) * -h)
        return ((xr + xi) * h, (xi - xr) * h)
    return (xr * c - xi * s, xr * s + xi * c)


def fft8(x, sign):
    even = fft4(x[0::2], sign)
    odd = fft4(x[1::2], sign)
    odd = [scaled(v, sign * 2.0 * math.pi * k / 8) for k, v in enumerate(odd)]
    first = [(a[0] + b[0], a[1] + b[1]) for a, b in zip(even, odd)]
    return first + [(a[0] - b[0], a[1] - b[1]) for a, b in zip(even, odd)]


def fft16(x, sign):
    inner = [fft4([x[4 * n1 + n2] for n1 in range(4)], sign) for n2 in range(4)]
    out = [None] * 16
    for k1 in range(4):
        column = [scaled(inner[n2][k1], sign * 2.0 * math.pi * n2 * k1 / 16) for n2 in range(4)]
        for k2, v in enumerate(fft4(column, sign)):
            out[k1 + 4 * k2] = v
    return out


def dot3(lhs, rhs, dims):
    left = jnp.concatenate([lhs[0], lhs[1], lhs[0]], axis=dims[0][0])
    right = jnp.concatenate([rhs[0], rhs[0], rhs[1]], axis=dims[1][0])
    return lax.dot_general(left, right, (dims, ((), ())), preferred_element_type=F32)


NN = ((1,), (0,))
NT = ((1,), (1,))
TN = ((0,), (0,))


LOGICAL = pl.DeviceIdType.LOGICAL


def enter(i, j):
    barrier = pltpu.get_barrier_semaphore()

    def signal(row, col):
        pl.semaphore_signal(barrier, inc=1, device_id=row * 16 + col, device_id_type=LOGICAL)

    for step in range(1, 16):
        signal(i, (j + step) % 16)
    for step in range(1, 8):
        signal((i + step) % 8, j)
    for row in (7, 1):
        for col in (15, 1):
            signal((i + row) % 8, (j + col) % 16)

    def down():
        pl.semaphore_wait(barrier, 26)

    return down


def send_group(c, me, source, landing, send_sem, recv_sem, local_sem):
    def remote(m):
        peer = (me + c + 8 * m) % 128
        pltpu.make_async_remote_copy(
            src_ref=source.at[peer],
            dst_ref=landing.at[me],
            send_sem=send_sem,
            recv_sem=recv_sem,
            device_id=peer,
            device_id_type=LOGICAL,
        ).start()

    @pl.when(c == 0)
    def _():
        pltpu.make_async_copy(source.at[me], landing.at[me], local_sem).start()

    @pl.when(c != 0)
    def _():
        remote(0)

    for m in range(1, 16):
        remote(m)


def wait_for(refs, sem):
    pltpu.make_async_copy(refs, refs, sem).wait()


def wait_all(landing, send_sem, recv_sem, local_sem):
    others = landing.at[pl.ds(0, landing.shape[0] - 1)]
    wait_for(landing.at[0], local_sem)
    wait_for(others, send_sem)
    wait_for(others, recv_sem)


def rows_forward(o, phase_ref, matrix_ref, twist_ref, out_ref, hi_ref, lo_ref):
    for half in range(2):
        cols = pl.ds(half * 128, 128)
        field = []
        for j in range(16):
            field.append(cos_sin_quarters(2.0 * decode(phase_ref[o, j, :, cols])))
        spectrum = fft16(field, -1.0)
        for k1 in range(16):
            re, im = spectrum[k1]
            if k1 > 0:
                c = twist_ref[0, pl.ds(k1, 1), cols]
                s = twist_ref[1, pl.ds(k1, 1), cols]
                re, im = re * c - im * s, re * s + im * c
            rows = pl.ds(k1 * 16, 16)
            for part, value in enumerate((re, im)):
                hi, lo = split(value)
                place = pl.ds(part * 256 + half * 128, 128)
                hi_ref[rows, place] = hi
                lo_ref[rows, place] = lo
    result = dot3((matrix_ref[0], matrix_ref[1]), (hi_ref[...], lo_ref[...]), NT)
    for h in range(2):
        out_ref[:, h, o] = encode(result[:, h * 128 : (h + 1) * 128]).reshape(64, 8, 128)


def transfer(o, me, wave, travel, cos_ref, sin_ref):
    row = lax.broadcasted_iota(jnp.int32, (8, 128), 0)
    lane = lax.broadcasted_iota(jnp.int32, (8, 128), 1)
    base_x = (row // 4) + 128 * (lane % 16)
    freq_y = 8 * (me % 2) + lane // 16 + 16 * (4 * (me // 2) + row % 4)
    signed_y = jnp.where(freq_y < 2048, freq_y, freq_y - 4096).astype(F32) * (1.0 / 4096)
    square_y = signed_y * signed_y

    def step(place, carry):
        freq_x = base_x + 2 * place
        signed_x = jnp.where(freq_x < 1024, freq_x, freq_x - 2048).astype(F32) * (1.0 / 2048)
        squared = signed_x * signed_x + square_y
        turns = travel * squared / (wave + jnp.sqrt(wave * wave - squared))
        c, w = cos_sin_quarters(4.0 * turns)
        cos_ref[o, place] = c
        sin_ref[o, place] = w
        return carry

    lax.fori_loop(0, 64, step, 0, unroll=4)


def put_split(place, re, im, hi_ref, lo_ref):
    for part, value in enumerate((re, im)):
        hi, lo = split(value)
        lanes = pl.ds(part * 128, 128)
        hi_ref[place, :, lanes] = hi
        lo_ref[place, :, lanes] = lo


def columns_in(n2, o, in_ref, pairs_ref, turns_ref, re_ref, im_ref):
    top = lax.broadcasted_iota(jnp.int32, (8, 128), 0) < 4
    column = []
    for n1 in range(8):
        s = 8 * n1 + n2
        a, b = decode(in_ref[s, o]), decode(in_ref[s + 64, o])
        total, delta = a + b, a - b
        re = jnp.where(top, total, pltpu.roll(delta, 4, 0))
        im = jnp.where(top, pltpu.roll(total, 4, 0), delta)
        c = jnp.where(top, 1.0, pairs_ref[0, s])
        w = jnp.where(top, 0.0, pairs_ref[1, s])
        column.append((re * c + im * w, im * c - re * w))
    for m1, (re, im) in enumerate(fft8(column, -1.0)):
        if m1 > 0:
            c, w = turns_ref[0, n2 * 8 + m1], turns_ref[1, n2 * 8 + m1]
            re, im = re * c + im * w, im * c - re * w
        re_ref[o, m1 * 8 + n2] = re
        im_ref[o, m1 * 8 + n2] = im


def columns(o, matrix_ref, back_ref, twist_ref, cos_ref, sin_ref, re_ref, im_ref, hi_ref, lo_ref):
    for m1 in range(8):
        column = [(re_ref[o, m1 * 8 + n2], im_ref[o, m1 * 8 + n2]) for n2 in range(8)]
        for m2, (re, im) in enumerate(fft8(column, -1.0)):
            place = m1 + 8 * m2
            c, w = twist_ref[0, place], twist_ref[1, place]
            put_split(place, re * c - im * w, re * w + im * c, hi_ref, lo_ref)
    data = (hi_ref[...].reshape(512, 256), lo_ref[...].reshape(512, 256))
    spectrum = dot3(data, (matrix_ref[0], matrix_ref[1]), NN).reshape(64, 8, 256)
    for place in range(64):
        c, w = cos_ref[o, place], sin_ref[o, place]
        re, im = spectrum[place, :, :128], spectrum[place, :, 128:]
        put_split(place, re * c + im * w, im * c - re * w, hi_ref, lo_ref)
    data = (hi_ref[...].reshape(512, 256), lo_ref[...].reshape(512, 256))
    spectrum = dot3(data, (back_ref[0], back_ref[1]), NN).reshape(64, 8, 256)
    for m1 in range(8):
        column = []
        for m2 in range(8):
            place = m1 + 8 * m2
            re, im = spectrum[place, :, :128], spectrum[place, :, 128:]
            c, w = twist_ref[0, place], twist_ref[1, place]
            column.append((re * c + im * w, im * c - re * w))
        for n2, v in enumerate(fft8(column, 1.0)):
            re, im = scaled(v, 2.0 * math.pi * n2 * m1 / 64)
            re_ref[o, m1 * 8 + n2] = re
            im_ref[o, m1 * 8 + n2] = im


def columns_out(n2, o, pairs_ref, re_ref, im_ref, out_ref):
    top = lax.broadcasted_iota(jnp.int32, (8, 128), 0) < 4
    column = [(re_ref[o, m1 * 8 + n2], im_ref[o, m1 * 8 + n2]) for m1 in range(8)]
    for n1, (re, im) in enumerate(fft8(column, 1.0)):
        s = 8 * n1 + n2
        c = jnp.where(top, 1.0, pairs_ref[0, s])
        w = jnp.where(top, 0.0, pairs_ref[1, s])
        re, im = re * c - im * w, im * c + re * w
        total = jnp.where(top, re, pltpu.roll(im, 4, 0))
        delta = jnp.where(top, pltpu.roll(re, 4, 0), im)
        out_ref[s, o] = encode(total + delta)
        out_ref[s + 64, o] = encode(total - delta)


def rows_inverse(o, hi_ref, lo_ref, matrix_ref, twist_ref, out_ref, value_ref):
    for h in range(2):
        hi, lo = hi_ref[:, h, o].reshape(512, 128), lo_ref[:, h, o].reshape(512, 128)
        rows = pl.ds(h * 128, 128)
        value_ref[rows, :] = dot3((hi, lo), (matrix_ref[0], matrix_ref[1]), TN)
    for half in range(2):
        cols = pl.ds(half * 128, 128)
        spectrum = []
        for k1 in range(16):
            rows = pl.ds(k1 * 16, 16)
            re = value_ref[rows, cols] * 2.0**-13
            im = value_ref[rows, pl.ds(256 + half * 128, 128)] * 2.0**-13
            if k1 > 0:
                c = twist_ref[0, pl.ds(k1, 1), cols]
                s = twist_ref[1, pl.ds(k1, 1), cols]
                re, im = re * c + im * s, im * c - re * s
            spectrum.append((re, im))
        for j, field in enumerate(fft16(spectrum, 1.0)):
            for part in range(2):
                out_ref[o, part, :, pl.ds(j * 256 + half * 128, 128)] = field[part].astype(BF16)


EDGE_ROW = (0, 6, 3)


def band(weight_ref, band_ref):
    x = lax.broadcasted_iota(jnp.int32, (32, 128), 0)
    lane = lax.broadcasted_iota(jnp.int32, (32, 128), 1)
    shift = lane % 64 - x - 15
    upper = lane < 64
    row = lax.broadcasted_iota(jnp.int32, (16, 128), 0)
    beyond = [(lane[:16] % 64 == source, u) for source, u in ((16, 2), (47, 0))]
    for pair in range(8):
        columns_of = pl.ds(pair * 128, 128)
        edges = [jnp.zeros((16, 128), F32), jnp.zeros((16, 128), F32)]
        for o in range(3):
            weights = [weight_ref[o, u].astype(F32) for u in range(3)]
            for v in range(3):
                value = jnp.zeros((32, 128), F32)
                for u in range(3):
                    c = 2 * pair
                    a = jnp.broadcast_to(weights[u][v : v + 1, c : c + 1], (32, 128))
                    b = jnp.broadcast_to(weights[u][v : v + 1, c + 1 : c + 2], (32, 128))
                    both = jnp.where(upper, a, b)
                    value = jnp.where(shift == u, both, value)
                    for n, (here, edge_u) in enumerate(beyond):
                        if u == edge_u:
                            edges[n] = jnp.where(here & (row == EDGE_ROW[v] + o), both[:16], edges[n])
                band_ref[(v * 3 + o) * 32 : (v * 3 + o) * 32 + 32, columns_of] = value.astype(BF16)
        for n in range(2):
            band_ref[288 + 16 * n : 304 + 16 * n, columns_of] = edges[n].astype(BF16)


PHASE_ORDER = ((1, 0), (0, 1), (3, 0), (1, 1), (2, 0), (3, 1), (2, 1), (0, 0))


def head(i, j, weight_ref, bias_ref, band_ref, tile_ref, sums_ref, sides_ref, edges_ref, got_sides_ref, got_edges_ref, got_corners_ref, phase_ref, load, down, border_sems, send_phase, meanwhile):
    band(weight_ref, band_ref)
    load.wait()
    lane = lax.broadcasted_iota(jnp.int32, (32, 128), 1)
    tall = lax.broadcasted_iota(jnp.int32, (32, 128), 0)
    to_right = jnp.zeros((32, 128), F32)
    to_left = jnp.zeros((32, 128), F32)
    for k in range(8):
        window = tile_ref[:, k * 32 : k * 32 + 64, :].reshape(1024, 256)
        count = 320 if k in (0, 7) else 288
        value = jnp.dot(band_ref[:count], window, preferred_element_type=F32)
        sums_ref[k] = value[:288].reshape(9, 32, 256)
        if k == 0:
            edges_ref[0] = value[288:304]
        if k == 7:
            edges_ref[1] = value[304:320]
        for o in range(3):
            to_right = jnp.where(lane == 3 * k + o, value[o * 32 : o * 32 + 32, 255:256], to_right)
            to_left = jnp.where(lane == 3 * k + o, value[192 + o * 32 : 224 + o * 32, 0:1], to_left)
    sides_ref[0] = to_right
    sides_ref[1] = to_left
    down()
    send_sems, recv_sems = border_sems
    copies = []
    for slot, step in enumerate((1, -1)):
        copies.append((sides_ref.at[slot], got_sides_ref.at[slot], i, (j + step + 16) % 16))
    for edge, down_step in enumerate((-1, 1)):
        row = (i + down_step + 8) % 8
        copies.append((edges_ref.at[edge], got_edges_ref.at[edge], row, j))
        for side, step in enumerate((1, -1)):
            corner = edges_ref.at[edge, pl.ds(0, 8), pl.ds(128 * (1 - side), 128)]
            copies.append((corner, got_corners_ref.at[edge * 2 + side], row, (j + step + 16) % 16))
    copies = [
        pltpu.make_async_remote_copy(
            src_ref=source, dst_ref=target, send_sem=send_sems.at[n], recv_sem=recv_sems.at[n],
            device_id=row * 16 + col, device_id_type=LOGICAL,
        )
        for n, (source, target, row, col) in enumerate(copies)
    ]
    for copy in copies:
        copy.start()
    meanwhile()
    for copy in copies:
        copy.wait()
    below, above = i < 7, i > 0
    left, right = j > 0, j < 15
    wide = lax.broadcasted_iota(jnp.int32, (32, 256), 1)
    row = lax.broadcasted_iota(jnp.int32, (8, 256), 0)
    for edge, (k, rows, here) in enumerate(((7, pl.ds(24, 8), (row == 7) & below), (0, pl.ds(0, 8), (row == 0) & above))):
        for v in range(3):
            for o in range(3):
                beyond = got_edges_ref[edge, pl.ds(EDGE_ROW[v] + o, 1), :]
                sums_ref[k, v * 3 + o, rows, :] += jnp.where(here, beyond, 0.0)
    for side, there in enumerate((left, right)):
        column = got_sides_ref[side]
        for edge, (k, x, inside) in enumerate(((7, 31, below), (0, 0, above))):
            corners = got_corners_ref[edge * 2 + side]
            for o in range(3):
                y = 127 * (1 - side)
                corner = corners[EDGE_ROW[2 * side] + o : EDGE_ROW[2 * side] + o + 1, y : y + 1]
                here = (lane == 3 * k + o) & (tall == x) & inside
                column = column + jnp.where(here, corner, 0.0)
        got_sides_ref[side] = jnp.where(there, column, 0.0)

    turn = 1 - 2 * (j % 2)
    for o in range(3):

        def block(k):
            index = 3 * k + o
            before = pltpu.roll(got_sides_ref[0], 128 - index, 1)
            after = pltpu.roll(got_sides_ref[1], 127 - index, 1)
            first = pltpu.roll(sums_ref[k, o], 1, 1)
            last = pltpu.roll(sums_ref[k, 6 + o], 255, 1)
            first = jnp.where(wide == 0, jnp.concatenate([before, before], 1), first)
            last = jnp.where(wide == 255, jnp.concatenate([after, after], 1), last)
            value = encode(jnp.tanh(first + last + (sums_ref[k, 3 + o] + bias_ref[o])))
            phase_ref[o, 2 * k] = value[:16]
            phase_ref[o, 2 * k + 1] = value[16:]
            send_phase(o, 2 * k)
            send_phase(o, 2 * k + 1)

        for x_step, z_step in PHASE_ORDER:
            block(((j // 8 + z_step) % 2) * 4 + (j // 2 + turn * x_step) % 4)


def spectral_kernel(
    weight_ref, bias_ref, wave_ref, travel_ref, pairs_ref, turns_ref, features_ref,
    forward_hbm, lanes_hbm, back_hbm, twist_x_hbm, twist_y_ref,
    high_ref, low_ref,
    forward_ref, lanes_ref, back_ref, twist_x_ref,
    tile_ref, band_ref, sums_ref, sides_ref, edges_ref, got_sides_ref, got_edges_ref, got_corners_ref, phase_ref, got_phase_ref,
    packets_ref, spread_in_ref, filtered_ref, returned_ref, cos_ref, sin_ref, re_ref, im_ref, hi_ref, lo_ref, field_hi_ref, field_lo_ref,
    tile_sem, table_sems, border_send, border_recv, send_sems, recv_sems, local_sems, group_sems,
):
    colors = 3
    i, j = lax.axis_index("row"), lax.axis_index("col")
    me = i * 16 + j
    load = pltpu.make_async_copy(features_ref, tile_ref.at[:, pl.ds(16, 256), :], tile_sem)
    load.start()
    down = enter(i, j)
    tables_in = []
    for n, (source, target) in enumerate(((forward_hbm, forward_ref), (lanes_hbm, lanes_ref), (back_hbm, back_ref), (twist_x_hbm, twist_x_ref))):
        tables_in.append(pltpu.make_async_copy(source, target, table_sems.at[n]))
        tables_in[n].start()
    tile_ref[:, 0:16, :] = jnp.zeros((16, 16, 256), BF16)
    tile_ref[:, 272:288, :] = jnp.zeros((16, 16, 256), BF16)

    def each(body):
        def step(o, carry):
            body(o)
            return carry

        lax.fori_loop(0, colors, step, 0)

    def send_phase(o, peer):
        n = 2 + o

        @pl.when(peer == j)
        def _():
            pltpu.make_async_copy(phase_ref.at[o, peer], got_phase_ref.at[o, j], local_sems.at[n]).start()

        @pl.when(peer != j)
        def _():
            pltpu.make_async_remote_copy(
                src_ref=phase_ref.at[o, peer], dst_ref=got_phase_ref.at[o, j], send_sem=send_sems.at[n], recv_sem=recv_sems.at[n],
                device_id=i * 16 + peer, device_id_type=LOGICAL,
            ).start()

    head(
        i, j, weight_ref, bias_ref, band_ref, tile_ref, sums_ref, sides_ref, edges_ref, got_sides_ref, got_edges_ref, got_corners_ref, phase_ref,
        load, down, (border_send, border_recv), send_phase,
        lambda: each(lambda o: transfer(o, me, wave_ref[o], travel_ref[0], cos_ref, sin_ref)),
    )

    by_pair = packets_ref.reshape(64, 2, colors, 8, 128)

    def forward(o):
        wait_all(got_phase_ref.at[o], send_sems.at[2 + o], recv_sems.at[2 + o], local_sems.at[2 + o])
        rows_forward(o, got_phase_ref, forward_ref, twist_y_ref, by_pair, field_hi_ref, field_lo_ref)

    tables_in[0].wait()
    each(forward)

    def groups(body):
        def step(c, carry):
            body(c)
            return carry

        lax.fori_loop(0, 8, step, 0)

    groups(lambda c: send_group(c, me, packets_ref, spread_in_ref, send_sems.at[0], group_sems.at[c], local_sems.at[0]))

    def wait_group(c, landing, local_sem, sem):
        @pl.when(c == 0)
        def _():
            wait_for(landing.at[0], local_sem)
            wait_for(landing.at[pl.ds(0, 15)], sem)

        @pl.when(c != 0)
        def _():
            wait_for(landing.at[pl.ds(0, 16)], sem)

    def arrive(c):
        wait_group(c, spread_in_ref, local_sems.at[0], group_sems.at[c])
        for o in range(colors):
            columns_in((me - c + 8) % 8, o, spread_in_ref, pairs_ref, turns_ref, re_ref, im_ref)

    def leave(c):
        for o in range(colors):
            columns_out((me + c) % 8, o, pairs_ref, re_ref, im_ref, filtered_ref)
        send_group(c, me, filtered_ref, returned_ref, send_sems.at[1], group_sems.at[8 + c], local_sems.at[1])

    groups(arrive)
    for table in tables_in[1:]:
        table.wait()
    each(lambda o: columns(o, lanes_ref, back_ref, twist_x_ref, cos_ref, sin_ref, re_ref, im_ref, hi_ref, lo_ref))
    groups(leave)
    wait_for(packets_ref.at[pl.ds(0, 127)], send_sems.at[0])

    def finish(c):
        wait_group(c, returned_ref, local_sems.at[1], group_sems.at[8 + c])
        for m in range(16):
            d = (me - c + 8 * m + 8) % 128
            high_ref[d], low_ref[d] = split(decode(returned_ref[d]))

    groups(finish)
    wait_for(filtered_ref.at[pl.ds(0, 127)], send_sems.at[1])


def rows_inverse_kernel(hi_ref, lo_ref, matrix_ref, twist_ref, out_ref, value_ref, result_ref, sems):
    colors = result_ref.shape[0]
    by_pair = [ref.reshape(64, 2, colors, 8, 128) for ref in (hi_ref, lo_ref)]

    def step(o, carry):
        rows_inverse(o, *by_pair, matrix_ref, twist_ref, result_ref, value_ref)
        pltpu.make_async_copy(result_ref.at[o], out_ref.at[o], sems.at[o]).start()
        return carry

    lax.fori_loop(0, colors, step, 0)
    for o in range(colors):
        pltpu.make_async_copy(result_ref.at[o], out_ref.at[o], sems.at[o]).wait()


def per_device(features, conv_weight, bias, wave, travel):
    table = tables()
    colors = 3
    names = ("forward_y", "lanes", "lanes_back", "twist_x", "twist_y")
    args = [jnp.asarray(table[k]) for k in names]
    smem = pl.BlockSpec(memory_space=pltpu.SMEM)
    vmem = pl.BlockSpec(memory_space=pltpu.VMEM)
    exchange = pltpu.VMEM((128, colors, 8, 128), BF16)
    high, low = pl.pallas_call(
        spectral_kernel,
        in_specs=[vmem] + [smem] * 5 + [pl.BlockSpec(memory_space=pl.ANY)] * 5 + [vmem],
        out_specs=[vmem] * 2,
        out_shape=[pltpu.VMEM((128, colors, 8, 128), BF16)] * 2,
        scratch_shapes=[
            *(pltpu.VMEM(a.shape, a.dtype) for a in args[:4]),
            pltpu.VMEM((16, 288, 256), BF16),
            pltpu.VMEM((320, 1024), BF16),
            pltpu.VMEM((8, 9, 32, 256), F32),
            pltpu.VMEM((2, 32, 128), F32),
            pltpu.VMEM((2, 16, 256), F32),
            pltpu.VMEM((2, 32, 128), F32),
            pltpu.VMEM((2, 16, 256), F32),
            pltpu.VMEM((4, 8, 128), F32),
            pltpu.VMEM((colors, 16, 16, 256), BF16),
            pltpu.VMEM((colors, 16, 16, 256), BF16),
            exchange, exchange, exchange, exchange,
            pltpu.VMEM((colors, 64, 8, 128), F32),
            pltpu.VMEM((colors, 64, 8, 128), F32),
            pltpu.VMEM((colors, 64, 8, 128), F32),
            pltpu.VMEM((colors, 64, 8, 128), F32),
            pltpu.VMEM((64, 8, 256), BF16),
            pltpu.VMEM((64, 8, 256), BF16),
            pltpu.VMEM((256, 512), BF16),
            pltpu.VMEM((256, 512), BF16),
            pltpu.SemaphoreType.DMA,
            pltpu.SemaphoreType.DMA((4,)),
            pltpu.SemaphoreType.DMA((8,)),
            pltpu.SemaphoreType.DMA((8,)),
            pltpu.SemaphoreType.DMA((5,)),
            pltpu.SemaphoreType.DMA((5,)),
            pltpu.SemaphoreType.DMA((5,)),
            pltpu.SemaphoreType.DMA((16,)),
        ],
        compiler_params=pltpu.CompilerParams(collective_id=0, has_side_effects=True, vmem_limit_bytes=VMEM_LIMIT),
        name="spectral",
    )(conv_weight.transpose(0, 2, 3, 1), bias, wave, travel, jnp.asarray(table["pairs"]), jnp.asarray(table["turns"]), features, *args)
    return pl.pallas_call(
        rows_inverse_kernel,
        in_specs=[vmem] * 4,
        out_specs=pl.BlockSpec(memory_space=pl.ANY),
        out_shape=jax.ShapeDtypeStruct((colors, 2, 16, 4096), BF16),
        scratch_shapes=[
            pltpu.VMEM((256, 512), F32),
            pltpu.VMEM((colors, 2, 16, 4096), BF16),
            pltpu.SemaphoreType.DMA((colors,)),
        ],
        compiler_params=pltpu.CompilerParams(vmem_limit_bytes=16 * 1024 * 1024),
        name="rows_inverse",
    )(high, low, args[0], args[4])


def solution(mesh):
    in_specs = (P(None, "row", "col"), P(), P(), P(), P())
    out_specs = P(None, None, ("row", "col"), None)
    return jax.shard_map(
        per_device, mesh=mesh, in_specs=in_specs, out_specs=out_specs, check_vma=False
    )
```

```python
import functools
import math

import jax
import jax.numpy as jnp
import numpy as np
from jax import lax
from jax.experimental import pallas as pl
from jax.experimental.pallas import tpu as pltpu
from jax.sharding import PartitionSpec as P

F32 = jnp.float32
BF16 = jnp.bfloat16
VMEM_LIMIT = 56 * 1024 * 1024


def split_np(table):
    hi = table.astype(np.float32).astype(jnp.bfloat16)
    lo = (table - hi.astype(np.float64)).astype(np.float32).astype(jnp.bfloat16)
    return np.stack([np.asarray(hi), np.asarray(lo)])


def rotation_np(theta):
    return np.array([[np.cos(theta), np.sin(theta)], [-np.sin(theta), np.cos(theta)]])


def tables():
    b = np.arange(256)
    m = np.arange(128)
    rot = rotation_np(2.0 * np.pi * ((m[:, None] * m[None, :]) % 128) / 128.0)
    forward_y = rot.reshape(2, 2, 32, 4, 128).transpose(2, 0, 3, 1, 4).reshape(256, 256)
    j = np.arange(16)
    rot16 = rotation_np(2.0 * np.pi * ((j[:, None] * j[None, :]) % 16) / 16.0)
    back16 = np.stack([np.stack([rot16[0, 0], -rot16[0, 1]]), np.stack([-rot16[1, 0], rot16[1, 1]])])
    lanes = np.einsum("pqab,cd->qcbpda", rot16, np.eye(8)).reshape(256, 256)
    lanes_back = np.einsum("pqab,cd->qcbpda", back16, np.eye(8)).reshape(256, 256)
    k1 = np.minimum(np.arange(24), 16)
    angle = 2.0 * np.pi * ((k1[:, None] * b[None, :]) % 4096) / 4096.0
    twist_y = np.stack([np.cos(angle), -np.sin(angle)]).astype(np.float32)
    p = np.arange(128).reshape(64, 2)
    r = np.arange(16)
    angle = 2.0 * np.pi * ((p[:, :, None] * r) % 2048) / 2048.0
    twist_x = np.stack([np.cos(angle), -np.sin(angle)])
    twist_x = np.broadcast_to(twist_x[:, :, :, None, None, :], (2, 64, 2, 4, 8, 16))
    twist_x = twist_x.reshape(2, 64, 8, 128).astype(np.float32)
    s = np.arange(64)
    pairs = np.stack([np.cos(2.0 * np.pi * s / 128), np.sin(2.0 * np.pi * s / 128)]).astype(np.float32)
    turn = 2.0 * np.pi * ((s // 8) * (s % 8)) / 64.0
    turns = np.stack([np.cos(turn), np.sin(turn)]).astype(np.float32)
    return {
        "pairs": pairs,
        "turns": turns,
        "forward_y": split_np(forward_y * 8.0),
        "lanes": split_np(lanes),
        "lanes_back": split_np(lanes_back * 2.0**-16),
        "twist_y": twist_y,
        "twist_x": twist_x,
    }


def encode(x):
    x = x * jnp.abs(x)
    x = x * jnp.abs(x)
    x = x * jnp.abs(x)
    return x.astype(BF16)


def decode(y):
    y = y.astype(F32)
    root = jnp.exp2(jnp.log2(jnp.abs(y)) * 0.125)
    return jnp.where(y < 0.0, -root, root)


def split(x):
    hi = x.astype(BF16)
    return hi, (x - hi.astype(F32)).astype(BF16)


def cos_sin_quarters(u):
    n = jnp.round(u)
    f = u - n
    n = n.astype(jnp.int32)
    z = f * f
    s = f * (1.5707963267948966 + z * (-0.6459640975062462 + z * (0.07969262624616703 + z * (-0.004681754135318688 + z * 0.00016044118478735982))))
    c = 1.0 + z * (-1.2337005501361697 + z * (0.253669507901048 + z * (-0.020863480763352960 + z * (0.0009192602748394265 - z * 2.5202042373060605e-05))))
    swap = (n & 1) == 1
    cos = jnp.where(swap, s, c)
    sin = jnp.where(swap, c, s)
    cos = jnp.where(((n + 1) & 2) == 2, -cos, cos)
    sin = jnp.where((n & 2) == 2, -sin, sin)
    return cos, sin


def fft4(x, sign):
    (ar, ai), (br, bi), (cr, ci), (dr, di) = x
    sr, si, tr, ti = ar + cr, ai + ci, ar - cr, ai - ci
    ur, ui, vr, vi = br + dr, bi + di, br - dr, bi - di
    if sign < 0:
        vr, vi = vi, -vr
    else:
        vr, vi = -vi, vr
    return [(sr + ur, si + ui), (tr + vr, ti + vi), (sr - ur, si - ui), (tr - vr, ti - vi)]


def scaled(x, angle):
    turn = angle / (0.5 * math.pi)
    xr, xi = x
    if abs(turn - round(turn)) < 1e-9:
        case = int(round(turn)) % 4
        return [(xr, xi), (-xi, xr), (-xr, -xi), (xi, -xr)][case]
    c, s = math.cos(angle), math.sin(angle)
    eighth = turn * 2
    if abs(eighth - round(eighth)) < 1e-9:
        case = int(round(eighth)) % 8
        h = math.sqrt(0.5)
        if case == 1:
            return ((xr - xi) * h, (xr + xi) * h)
        if case == 3:
            return ((xr + xi) * -h, (xr - xi) * h)
        if case == 5:
            return ((xi - xr) * h, (xr + xi) * -h)
        return ((xr + xi) * h, (xi - xr) * h)
    return (xr * c - xi * s, xr * s + xi * c)


def fft8(x, sign):
    even = fft4(x[0::2], sign)
    odd = fft4(x[1::2], sign)
    odd = [scaled(v, sign * 2.0 * math.pi * k / 8) for k, v in enumerate(odd)]
    first = [(a[0] + b[0], a[1] + b[1]) for a, b in zip(even, odd)]
    return first + [(a[0] - b[0], a[1] - b[1]) for a, b in zip(even, odd)]


def fft16(x, sign):
    inner = [fft4([x[4 * n1 + n2] for n1 in range(4)], sign) for n2 in range(4)]
    out = [None] * 16
    for k1 in range(4):
        column = [scaled(inner[n2][k1], sign * 2.0 * math.pi * n2 * k1 / 16) for n2 in range(4)]
        for k2, v in enumerate(fft4(column, sign)):
            out[k1 + 4 * k2] = v
    return out


def dot3(lhs, rhs, dims):
    left = jnp.concatenate([lhs[0], lhs[1], lhs[0]], axis=dims[0][0])
    right = jnp.concatenate([rhs[0], rhs[0], rhs[1]], axis=dims[1][0])
    return lax.dot_general(left, right, (dims, ((), ())), preferred_element_type=F32)


NN = ((1,), (0,))
NT = ((1,), (1,))
TN = ((0,), (0,))


LOGICAL = pl.DeviceIdType.LOGICAL


def enter(i, j):
    barrier = pltpu.get_barrier_semaphore()

    def signal(row, col):
        pl.semaphore_signal(barrier, inc=1, device_id=row * 16 + col, device_id_type=LOGICAL)

    for step in range(1, 16):
        signal(i, (j + step) % 16)
    for step in range(1, 8):
        signal((i + step) % 8, j)
    for row in (7, 1):
        for col in (15, 1):
            signal((i + row) % 8, (j + col) % 16)

    def down():
        pl.semaphore_wait(barrier, 26)

    return down


def send_group(c, me, source, landing, send_sem, recv_sem, local_sem):
    def remote(m):
        peer = (me + c + 8 * m) % 128
        pltpu.make_async_remote_copy(
            src_ref=source.at[peer],
            dst_ref=landing.at[me],
            send_sem=send_sem,
            recv_sem=recv_sem,
            device_id=peer,
            device_id_type=LOGICAL,
        ).start()

    @pl.when(c == 0)
    def _():
        pltpu.make_async_copy(source.at[me], landing.at[me], local_sem).start()

    @pl.when(c != 0)
    def _():
        remote(0)

    for m in range(1, 16):
        remote(m)


def wait_for(refs, sem):
    pltpu.make_async_copy(refs, refs, sem).wait()


def wait_all(landing, send_sem, recv_sem, local_sem):
    others = landing.at[pl.ds(0, landing.shape[0] - 1)]
    wait_for(landing.at[0], local_sem)
    wait_for(others, send_sem)
    wait_for(others, recv_sem)


def rows_forward(o, phase_ref, matrix_ref, twist_ref, out_ref, half_ref, hi_ref, lo_ref):
    step_c, step_s = twist_ref[0, 16:17, :128], twist_ref[1, 16:17, :128]
    for half in range(2):
        cols = pl.ds(half * 128, 128)
        field = []
        for j in range(16):
            field.append(cos_sin_quarters(2.0 * decode(phase_ref[o, j, :, cols])))
        spectrum = fft16(field, -1.0)
        for k1 in range(16):
            re, im = spectrum[k1]
            if k1 > 0:
                c = twist_ref[0, pl.ds(k1, 1), cols]
                s = twist_ref[1, pl.ds(k1, 1), cols]
                re, im = re * c - im * s, re * s + im * c
            rows = pl.ds(k1 * 16, 16)
            if half == 0:
                half_ref[0, rows, :] = re
                half_ref[1, rows, :] = im
                continue
            low_re, low_im = half_ref[0, rows, :], half_ref[1, rows, :]
            dre, dim = low_re - re, low_im - im
            even = (low_re + re, low_im + im)
            odd = (dre * step_c - dim * step_s, dre * step_s + dim * step_c)
            for parity, values in enumerate((even, odd)):
                rows = pl.ds(parity * 256 + k1 * 16, 16)
                for part, value in enumerate(values):
                    hi, lo = split(value)
                    place = pl.ds(part * 128, 128)
                    hi_ref[rows, place] = hi
                    lo_ref[rows, place] = lo
    for parity in range(2):
        rows = pl.ds(parity * 256, 256)
        result = dot3((matrix_ref[0], matrix_ref[1]), (hi_ref[rows, :], lo_ref[rows, :]), NT)
        for h in range(2):
            out_ref[pl.ds(parity * 32, 32), h, o] = encode(result[:, h * 128 : (h + 1) * 128]).reshape(32, 8, 128)


def transfer(o, me, wave, travel, cos_ref, sin_ref):
    row = lax.broadcasted_iota(jnp.int32, (8, 128), 0)
    lane = lax.broadcasted_iota(jnp.int32, (8, 128), 1)
    base_x = (row // 4) + 128 * (lane % 16)
    group = me // 2
    freq_y = 8 * (me % 2) + lane // 16 + 16 * (2 * (4 * (group % 32) + row % 4) + group // 32)
    signed_y = jnp.where(freq_y < 2048, freq_y, freq_y - 4096).astype(F32) * (1.0 / 4096)
    square_y = signed_y * signed_y

    def step(place, carry):
        freq_x = base_x + 2 * place
        signed_x = jnp.where(freq_x < 1024, freq_x, freq_x - 2048).astype(F32) * (1.0 / 2048)
        squared = signed_x * signed_x + square_y
        turns = travel * squared / (wave + jnp.sqrt(wave * wave - squared))
        c, w = cos_sin_quarters(4.0 * turns)
        cos_ref[o, place] = c
        sin_ref[o, place] = w
        return carry

    lax.fori_loop(0, 64, step, 0, unroll=4)


def put_split(place, re, im, hi_ref, lo_ref):
    for part, value in enumerate((re, im)):
        hi, lo = split(value)
        lanes = pl.ds(part * 128, 128)
        hi_ref[place, :, lanes] = hi
        lo_ref[place, :, lanes] = lo


def columns_in(n2, o, in_ref, pairs_ref, turns_ref, re_ref, im_ref):
    top = lax.broadcasted_iota(jnp.int32, (8, 128), 0) < 4
    column = []
    for n1 in range(8):
        s = 8 * n1 + n2
        a, b = decode(in_ref[s, o]), decode(in_ref[s + 64, o])
        total, delta = a + b, a - b
        re = jnp.where(top, total, pltpu.roll(delta, 4, 0))
        im = jnp.where(top, pltpu.roll(total, 4, 0), delta)
        c = jnp.where(top, 1.0, pairs_ref[0, s])
        w = jnp.where(top, 0.0, pairs_ref[1, s])
        column.append((re * c + im * w, im * c - re * w))
    for m1, (re, im) in enumerate(fft8(column, -1.0)):
        if m1 > 0:
            c, w = turns_ref[0, n2 * 8 + m1], turns_ref[1, n2 * 8 + m1]
            re, im = re * c + im * w, im * c - re * w
        re_ref[o, m1 * 8 + n2] = re
        im_ref[o, m1 * 8 + n2] = im


def columns(o, matrix_ref, back_ref, twist_ref, cos_ref, sin_ref, re_ref, im_ref, hi_ref, lo_ref):
    for m1 in range(8):
        column = [(re_ref[o, m1 * 8 + n2], im_ref[o, m1 * 8 + n2]) for n2 in range(8)]
        for m2, (re, im) in enumerate(fft8(column, -1.0)):
            place = m1 + 8 * m2
            c, w = twist_ref[0, place], twist_ref[1, place]
            put_split(place, re * c - im * w, re * w + im * c, hi_ref, lo_ref)
    data = (hi_ref[...].reshape(512, 256), lo_ref[...].reshape(512, 256))
    spectrum = dot3(data, (matrix_ref[0], matrix_ref[1]), NN).reshape(64, 8, 256)
    for place in range(64):
        c, w = cos_ref[o, place], sin_ref[o, place]
        re, im = spectrum[place, :, :128], spectrum[place, :, 128:]
        put_split(place, re * c + im * w, im * c - re * w, hi_ref, lo_ref)
    data = (hi_ref[...].reshape(512, 256), lo_ref[...].reshape(512, 256))
    spectrum = dot3(data, (back_ref[0], back_ref[1]), NN).reshape(64, 8, 256)
    for m1 in range(8):
        column = []
        for m2 in range(8):
            place = m1 + 8 * m2
            re, im = spectrum[place, :, :128], spectrum[place, :, 128:]
            c, w = twist_ref[0, place], twist_ref[1, place]
            column.append((re * c + im * w, im * c - re * w))
        for n2, v in enumerate(fft8(column, 1.0)):
            re, im = scaled(v, 2.0 * math.pi * n2 * m1 / 64)
            re_ref[o, m1 * 8 + n2] = re
            im_ref[o, m1 * 8 + n2] = im


def columns_out(n2, o, pairs_ref, re_ref, im_ref, out_ref):
    top = lax.broadcasted_iota(jnp.int32, (8, 128), 0) < 4
    column = [(re_ref[o, m1 * 8 + n2], im_ref[o, m1 * 8 + n2]) for m1 in range(8)]
    for n1, (re, im) in enumerate(fft8(column, 1.0)):
        s = 8 * n1 + n2
        c = jnp.where(top, 1.0, pairs_ref[0, s])
        w = jnp.where(top, 0.0, pairs_ref[1, s])
        re, im = re * c - im * w, im * c + re * w
        total = jnp.where(top, re, pltpu.roll(im, 4, 0))
        delta = jnp.where(top, pltpu.roll(re, 4, 0), im)
        out_ref[s, o] = encode(total + delta)
        out_ref[s + 64, o] = encode(total - delta)


def rows_inverse(o, hi_ref, lo_ref, matrix_ref, twist_ref, out_ref, value_ref):
    step_c, step_s = twist_ref[0, 16:17, :128], twist_ref[1, 16:17, :128]
    for h in range(2):
        hi, lo = hi_ref[:, h, o].reshape(512, 128), lo_ref[:, h, o].reshape(512, 128)
        rows = pl.ds(h * 128, 128)
        even = dot3((hi[:256], lo[:256]), (matrix_ref[0], matrix_ref[1]), TN)
        odd = dot3((hi[256:], lo[256:]), (matrix_ref[0], matrix_ref[1]), TN)
        re, im = odd[:, :128], odd[:, 128:]
        re, im = re * step_c + im * step_s, im * step_c - re * step_s
        value_ref[rows, 0:128] = even[:, :128] + re
        value_ref[rows, 128:256] = even[:, :128] - re
        value_ref[rows, 256:384] = even[:, 128:] + im
        value_ref[rows, 384:512] = even[:, 128:] - im
    for half in range(2):
        cols = pl.ds(half * 128, 128)
        spectrum = []
        for k1 in range(16):
            rows = pl.ds(k1 * 16, 16)
            re = value_ref[rows, cols] * 2.0**-13
            im = value_ref[rows, pl.ds(256 + half * 128, 128)] * 2.0**-13
            if k1 > 0:
                c = twist_ref[0, pl.ds(k1, 1), cols]
                s = twist_ref[1, pl.ds(k1, 1), cols]
                re, im = re * c + im * s, im * c - re * s
            spectrum.append((re, im))
        for j, field in enumerate(fft16(spectrum, 1.0)):
            for part in range(2):
                out_ref[o, part, :, pl.ds(j * 256 + half * 128, 128)] = field[part].astype(BF16)


EDGE_ROW = (0, 6, 3)


def band(weight_ref, band_ref):
    x = lax.broadcasted_iota(jnp.int32, (32, 128), 0)
    lane = lax.broadcasted_iota(jnp.int32, (32, 128), 1)
    shift = lane % 64 - x - 15
    upper = lane < 64
    row = lax.broadcasted_iota(jnp.int32, (16, 128), 0)
    beyond = [(lane[:16] % 64 == source, u) for source, u in ((16, 2), (47, 0))]
    for pair in range(8):
        columns_of = pl.ds(pair * 128, 128)
        edges = [jnp.zeros((16, 128), F32), jnp.zeros((16, 128), F32)]
        for o in range(3):
            weights = [weight_ref[o, u].astype(F32) for u in range(3)]
            for v in range(3):
                value = jnp.zeros((32, 128), F32)
                for u in range(3):
                    c = 2 * pair
                    a = jnp.broadcast_to(weights[u][v : v + 1, c : c + 1], (32, 128))
                    b = jnp.broadcast_to(weights[u][v : v + 1, c + 1 : c + 2], (32, 128))
                    both = jnp.where(upper, a, b)
                    value = jnp.where(shift == u, both, value)
                    for n, (here, edge_u) in enumerate(beyond):
                        if u == edge_u:
                            edges[n] = jnp.where(here & (row == EDGE_ROW[v] + o), both[:16], edges[n])
                band_ref[(v * 3 + o) * 32 : (v * 3 + o) * 32 + 32, columns_of] = value.astype(BF16)
        for n in range(2):
            band_ref[288 + 16 * n : 304 + 16 * n, columns_of] = edges[n].astype(BF16)


PHASE_ORDER = ((1, 0), (0, 1), (3, 0), (1, 1), (2, 0), (3, 1), (2, 1), (0, 0))


def head(i, j, weight_ref, bias_ref, band_ref, tile_ref, sums_ref, sides_ref, edges_ref, got_sides_ref, got_edges_ref, got_corners_ref, phase_ref, load, down, border_sems, send_phase, meanwhile):
    band(weight_ref, band_ref)
    load.wait()
    lane = lax.broadcasted_iota(jnp.int32, (32, 128), 1)
    tall = lax.broadcasted_iota(jnp.int32, (32, 128), 0)
    to_right = jnp.zeros((32, 128), F32)
    to_left = jnp.zeros((32, 128), F32)
    for k in range(8):
        window = tile_ref[:, k * 32 : k * 32 + 64, :].reshape(1024, 256)
        count = 320 if k in (0, 7) else 288
        value = jnp.dot(band_ref[:count], window, preferred_element_type=F32)
        sums_ref[k] = value[:288].reshape(9, 32, 256)
        if k == 0:
            edges_ref[0] = value[288:304]
        if k == 7:
            edges_ref[1] = value[304:320]
        for o in range(3):
            to_right = jnp.where(lane == 3 * k + o, value[o * 32 : o * 32 + 32, 255:256], to_right)
            to_left = jnp.where(lane == 3 * k + o, value[192 + o * 32 : 224 + o * 32, 0:1], to_left)
    sides_ref[0] = to_right
    sides_ref[1] = to_left
    down()
    send_sems, recv_sems = border_sems
    copies = []
    for slot, step in enumerate((1, -1)):
        copies.append((sides_ref.at[slot], got_sides_ref.at[slot], i, (j + step + 16) % 16))
    for edge, down_step in enumerate((-1, 1)):
        row = (i + down_step + 8) % 8
        copies.append((edges_ref.at[edge], got_edges_ref.at[edge], row, j))
        for side, step in enumerate((1, -1)):
            corner = edges_ref.at[edge, pl.ds(0, 8), pl.ds(128 * (1 - side), 128)]
            copies.append((corner, got_corners_ref.at[edge * 2 + side], row, (j + step + 16) % 16))
    copies = [
        pltpu.make_async_remote_copy(
            src_ref=source, dst_ref=target, send_sem=send_sems.at[n], recv_sem=recv_sems.at[n],
            device_id=row * 16 + col, device_id_type=LOGICAL,
        )
        for n, (source, target, row, col) in enumerate(copies)
    ]
    for copy in copies:
        copy.start()
    meanwhile()
    for copy in copies:
        copy.wait()
    below, above = i < 7, i > 0
    left, right = j > 0, j < 15
    wide = lax.broadcasted_iota(jnp.int32, (32, 256), 1)
    row = lax.broadcasted_iota(jnp.int32, (8, 256), 0)
    for edge, (k, rows, here) in enumerate(((7, pl.ds(24, 8), (row == 7) & below), (0, pl.ds(0, 8), (row == 0) & above))):
        for v in range(3):
            for o in range(3):
                beyond = got_edges_ref[edge, pl.ds(EDGE_ROW[v] + o, 1), :]
                sums_ref[k, v * 3 + o, rows, :] += jnp.where(here, beyond, 0.0)
    for side, there in enumerate((left, right)):
        column = got_sides_ref[side]
        for edge, (k, x, inside) in enumerate(((7, 31, below), (0, 0, above))):
            corners = got_corners_ref[edge * 2 + side]
            for o in range(3):
                y = 127 * (1 - side)
                corner = corners[EDGE_ROW[2 * side] + o : EDGE_ROW[2 * side] + o + 1, y : y + 1]
                here = (lane == 3 * k + o) & (tall == x) & inside
                column = column + jnp.where(here, corner, 0.0)
        got_sides_ref[side] = jnp.where(there, column, 0.0)

    turn = 1 - 2 * (j % 2)
    for o in range(3):

        def block(k):
            index = 3 * k + o
            before = pltpu.roll(got_sides_ref[0], 128 - index, 1)
            after = pltpu.roll(got_sides_ref[1], 127 - index, 1)
            first = pltpu.roll(sums_ref[k, o], 1, 1)
            last = pltpu.roll(sums_ref[k, 6 + o], 255, 1)
            first = jnp.where(wide == 0, jnp.concatenate([before, before], 1), first)
            last = jnp.where(wide == 255, jnp.concatenate([after, after], 1), last)
            value = encode(jnp.tanh(first + last + (sums_ref[k, 3 + o] + bias_ref[o])))
            phase_ref[o, 2 * k] = value[:16]
            phase_ref[o, 2 * k + 1] = value[16:]
            send_phase(o, 2 * k)
            send_phase(o, 2 * k + 1)

        for x_step, z_step in PHASE_ORDER:
            block(((j // 8 + z_step) % 2) * 4 + (j // 2 + turn * x_step) % 4)


def spectral_kernel(
    weight_ref, bias_ref, wave_ref, travel_ref, pairs_ref, turns_ref, features_ref,
    forward_hbm, lanes_hbm, back_hbm, twist_x_hbm, twist_y_ref,
    high_ref, low_ref,
    forward_ref, lanes_ref, back_ref, twist_x_ref,
    tile_ref, band_ref, sums_ref, sides_ref, edges_ref, got_sides_ref, got_edges_ref, got_corners_ref, phase_ref, got_phase_ref,
    packets_ref, spread_in_ref, filtered_ref, returned_ref, cos_ref, sin_ref, re_ref, im_ref, hi_ref, lo_ref, half_ref, field_hi_ref, field_lo_ref,
    tile_sem, table_sems, border_send, border_recv, send_sems, recv_sems, local_sems, group_sems,
):
    colors = 3
    i, j = lax.axis_index("row"), lax.axis_index("col")
    me = i * 16 + j
    load = pltpu.make_async_copy(features_ref, tile_ref.at[:, pl.ds(16, 256), :], tile_sem)
    load.start()
    down = enter(i, j)
    tables_in = []
    for n, (source, target) in enumerate(((forward_hbm, forward_ref), (lanes_hbm, lanes_ref), (back_hbm, back_ref), (twist_x_hbm, twist_x_ref))):
        tables_in.append(pltpu.make_async_copy(source, target, table_sems.at[n]))
        tables_in[n].start()
    tile_ref[:, 0:16, :] = jnp.zeros((16, 16, 256), BF16)
    tile_ref[:, 272:288, :] = jnp.zeros((16, 16, 256), BF16)

    def each(body):
        def step(o, carry):
            body(o)
            return carry

        lax.fori_loop(0, colors, step, 0)

    def send_phase(o, peer):
        n = 2 + o

        @pl.when(peer == j)
        def _():
            pltpu.make_async_copy(phase_ref.at[o, peer], got_phase_ref.at[o, j], local_sems.at[n]).start()

        @pl.when(peer != j)
        def _():
            pltpu.make_async_remote_copy(
                src_ref=phase_ref.at[o, peer], dst_ref=got_phase_ref.at[o, j], send_sem=send_sems.at[n], recv_sem=recv_sems.at[n],
                device_id=i * 16 + peer, device_id_type=LOGICAL,
            ).start()

    head(
        i, j, weight_ref, bias_ref, band_ref, tile_ref, sums_ref, sides_ref, edges_ref, got_sides_ref, got_edges_ref, got_corners_ref, phase_ref,
        load, down, (border_send, border_recv), send_phase,
        lambda: each(lambda o: transfer(o, me, wave_ref[o], travel_ref[0], cos_ref, sin_ref)),
    )

    by_pair = packets_ref.reshape(64, 2, colors, 8, 128)

    def forward(o):
        wait_all(got_phase_ref.at[o], send_sems.at[2 + o], recv_sems.at[2 + o], local_sems.at[2 + o])
        rows_forward(o, got_phase_ref, forward_ref, twist_y_ref, by_pair, half_ref, field_hi_ref, field_lo_ref)

    tables_in[0].wait()
    each(forward)

    def groups(body):
        def step(c, carry):
            body(c)
            return carry

        lax.fori_loop(0, 8, step, 0)

    groups(lambda c: send_group(c, me, packets_ref, spread_in_ref, send_sems.at[0], group_sems.at[c], local_sems.at[0]))

    def wait_group(c, landing, local_sem, sem):
        @pl.when(c == 0)
        def _():
            wait_for(landing.at[0], local_sem)
            wait_for(landing.at[pl.ds(0, 15)], sem)

        @pl.when(c != 0)
        def _():
            wait_for(landing.at[pl.ds(0, 16)], sem)

    def arrive(c):
        wait_group(c, spread_in_ref, local_sems.at[0], group_sems.at[c])
        for o in range(colors):
            columns_in((me - c + 8) % 8, o, spread_in_ref, pairs_ref, turns_ref, re_ref, im_ref)

    def leave(c):
        for o in range(colors):
            columns_out((me + c) % 8, o, pairs_ref, re_ref, im_ref, filtered_ref)
        send_group(c, me, filtered_ref, returned_ref, send_sems.at[1], group_sems.at[8 + c], local_sems.at[1])

    groups(arrive)
    for table in tables_in[1:]:
        table.wait()
    each(lambda o: columns(o, lanes_ref, back_ref, twist_x_ref, cos_ref, sin_ref, re_ref, im_ref, hi_ref, lo_ref))
    groups(leave)
    wait_for(packets_ref.at[pl.ds(0, 127)], send_sems.at[0])

    def finish(c):
        wait_group(c, returned_ref, local_sems.at[1], group_sems.at[8 + c])
        for m in range(16):
            d = (me - c + 8 * m + 8) % 128
            high_ref[d], low_ref[d] = split(decode(returned_ref[d]))

    groups(finish)
    wait_for(filtered_ref.at[pl.ds(0, 127)], send_sems.at[1])


def rows_inverse_kernel(hi_ref, lo_ref, matrix_ref, twist_ref, out_ref, value_ref, result_ref, sems):
    colors = result_ref.shape[0]
    by_pair = [ref.reshape(64, 2, colors, 8, 128) for ref in (hi_ref, lo_ref)]

    def step(o, carry):
        rows_inverse(o, *by_pair, matrix_ref, twist_ref, result_ref, value_ref)
        pltpu.make_async_copy(result_ref.at[o], out_ref.at[o], sems.at[o]).start()
        return carry

    lax.fori_loop(0, colors, step, 0)
    for o in range(colors):
        pltpu.make_async_copy(result_ref.at[o], out_ref.at[o], sems.at[o]).wait()


def per_device(features, conv_weight, bias, wave, travel):
    table = tables()
    colors = 3
    names = ("forward_y", "lanes", "lanes_back", "twist_x", "twist_y")
    args = [jnp.asarray(table[k]) for k in names]
    smem = pl.BlockSpec(memory_space=pltpu.SMEM)
    vmem = pl.BlockSpec(memory_space=pltpu.VMEM)
    exchange = pltpu.VMEM((128, colors, 8, 128), BF16)
    high, low = pl.pallas_call(
        spectral_kernel,
        in_specs=[vmem] + [smem] * 5 + [pl.BlockSpec(memory_space=pl.ANY)] * 5 + [vmem],
        out_specs=[vmem] * 2,
        out_shape=[pltpu.VMEM((128, colors, 8, 128), BF16)] * 2,
        scratch_shapes=[
            *(pltpu.VMEM(a.shape, a.dtype) for a in args[:4]),
            pltpu.VMEM((16, 288, 256), BF16),
            pltpu.VMEM((320, 1024), BF16),
            pltpu.VMEM((8, 9, 32, 256), F32),
            pltpu.VMEM((2, 32, 128), F32),
            pltpu.VMEM((2, 16, 256), F32),
            pltpu.VMEM((2, 32, 128), F32),
            pltpu.VMEM((2, 16, 256), F32),
            pltpu.VMEM((4, 8, 128), F32),
            pltpu.VMEM((colors, 16, 16, 256), BF16),
            pltpu.VMEM((colors, 16, 16, 256), BF16),
            exchange, exchange, exchange, exchange,
            pltpu.VMEM((colors, 64, 8, 128), F32),
            pltpu.VMEM((colors, 64, 8, 128), F32),
            pltpu.VMEM((colors, 64, 8, 128), F32),
            pltpu.VMEM((colors, 64, 8, 128), F32),
            pltpu.VMEM((64, 8, 256), BF16),
            pltpu.VMEM((64, 8, 256), BF16),
            pltpu.VMEM((2, 256, 128), F32),
            pltpu.VMEM((512, 256), BF16),
            pltpu.VMEM((512, 256), BF16),
            pltpu.SemaphoreType.DMA,
            pltpu.SemaphoreType.DMA((4,)),
            pltpu.SemaphoreType.DMA((8,)),
            pltpu.SemaphoreType.DMA((8,)),
            pltpu.SemaphoreType.DMA((5,)),
            pltpu.SemaphoreType.DMA((5,)),
            pltpu.SemaphoreType.DMA((5,)),
            pltpu.SemaphoreType.DMA((16,)),
        ],
        compiler_params=pltpu.CompilerParams(collective_id=0, has_side_effects=True, vmem_limit_bytes=VMEM_LIMIT),
        name="spectral",
    )(conv_weight.transpose(0, 2, 3, 1), bias, wave, travel, jnp.asarray(table["pairs"]), jnp.asarray(table["turns"]), features, *args)
    return pl.pallas_call(
        rows_inverse_kernel,
        in_specs=[vmem] * 4,
        out_specs=pl.BlockSpec(memory_space=pl.ANY),
        out_shape=jax.ShapeDtypeStruct((colors, 2, 16, 4096), BF16),
        scratch_shapes=[
            pltpu.VMEM((256, 512), F32),
            pltpu.VMEM((colors, 2, 16, 4096), BF16),
            pltpu.SemaphoreType.DMA((colors,)),
        ],
        compiler_params=pltpu.CompilerParams(vmem_limit_bytes=16 * 1024 * 1024),
        name="rows_inverse",
    )(high, low, args[0], args[4])


def solution(mesh):
    in_specs = (P(None, "row", "col"), P(), P(), P(), P())
    out_specs = P(None, None, ("row", "col"), None)
    return jax.shard_map(
        per_device, mesh=mesh, in_specs=in_specs, out_specs=out_specs, check_vma=False
    )
```

```python
import functools
import math

import jax
import jax.numpy as jnp
import numpy as np
from jax import lax
from jax.experimental import pallas as pl
from jax.experimental.pallas import tpu as pltpu
from jax.sharding import PartitionSpec as P

F32 = jnp.float32
BF16 = jnp.bfloat16
VMEM_LIMIT = 56 * 1024 * 1024


def split_np(table):
    hi = table.astype(np.float32).astype(jnp.bfloat16)
    lo = (table - hi.astype(np.float64)).astype(np.float32).astype(jnp.bfloat16)
    return np.stack([np.asarray(hi), np.asarray(lo)])


def rotation_np(theta):
    return np.array([[np.cos(theta), np.sin(theta)], [-np.sin(theta), np.cos(theta)]])


def tables():
    b = np.arange(256)
    m = np.arange(128)
    rot = rotation_np(2.0 * np.pi * ((m[:, None] * m[None, :]) % 128) / 128.0)
    forward_y = rot.reshape(2, 2, 32, 4, 128).transpose(2, 0, 3, 1, 4).reshape(256, 256)
    j = np.arange(16)
    rot16 = rotation_np(2.0 * np.pi * ((j[:, None] * j[None, :]) % 16) / 16.0)
    back16 = np.stack([np.stack([rot16[0, 0], -rot16[0, 1]]), np.stack([-rot16[1, 0], rot16[1, 1]])])
    lanes = np.einsum("pqab,cd->qcbpda", rot16, np.eye(8)).reshape(256, 256)
    lanes_back = np.einsum("pqab,cd->qcbpda", back16, np.eye(8)).reshape(256, 256)
    k1 = np.minimum(np.arange(24), 16)
    angle = 2.0 * np.pi * ((k1[:, None] * b[None, :]) % 4096) / 4096.0
    twist_y = np.stack([np.cos(angle), -np.sin(angle)]).astype(np.float32)
    p = np.arange(128).reshape(64, 2)
    r = np.arange(16)
    angle = 2.0 * np.pi * ((p[:, :, None] * r) % 2048) / 2048.0
    twist_x = np.stack([np.cos(angle), -np.sin(angle)])
    twist_x = np.broadcast_to(twist_x[:, :, :, None, None, :], (2, 64, 2, 4, 8, 16))
    twist_x = twist_x.reshape(2, 64, 8, 128).astype(np.float32)
    s = np.arange(64)
    pairs = np.stack([np.cos(2.0 * np.pi * s / 128), np.sin(2.0 * np.pi * s / 128)]).astype(np.float32)
    turn = 2.0 * np.pi * ((s // 8) * (s % 8)) / 64.0
    turns = np.stack([np.cos(turn), np.sin(turn)]).astype(np.float32)
    return {
        "pairs": pairs,
        "turns": turns,
        "forward_y": split_np(forward_y * 8.0),
        "lanes": split_np(lanes),
        "lanes_back": split_np(lanes_back * 2.0**-16),
        "twist_y": twist_y,
        "twist_x": twist_x,
    }


def encode(x):
    x = x * jnp.abs(x)
    x = x * jnp.abs(x)
    x = x * jnp.abs(x)
    return x.astype(BF16)


def decode(y):
    y = y.astype(F32)
    root = jnp.exp2(jnp.log2(jnp.abs(y)) * 0.125)
    return jnp.where(y < 0.0, -root, root)


def split(x):
    hi = x.astype(BF16)
    return hi, (x - hi.astype(F32)).astype(BF16)


def cos_sin_quarters(u):
    n = jnp.round(u)
    f = u - n
    n = n.astype(jnp.int32)
    z = f * f
    s = f * (1.5707963267948966 + z * (-0.6459640975062462 + z * (0.07969262624616703 + z * (-0.004681754135318688 + z * 0.00016044118478735982))))
    c = 1.0 + z * (-1.2337005501361697 + z * (0.253669507901048 + z * (-0.020863480763352960 + z * (0.0009192602748394265 - z * 2.5202042373060605e-05))))
    swap = (n & 1) == 1
    cos = jnp.where(swap, s, c)
    sin = jnp.where(swap, c, s)
    cos = jnp.where(((n + 1) & 2) == 2, -cos, cos)
    sin = jnp.where((n & 2) == 2, -sin, sin)
    return cos, sin


def fft4(x, sign):
    (ar, ai), (br, bi), (cr, ci), (dr, di) = x
    sr, si, tr, ti = ar + cr, ai + ci, ar - cr, ai - ci
    ur, ui, vr, vi = br + dr, bi + di, br - dr, bi - di
    if sign < 0:
        vr, vi = vi, -vr
    else:
        vr, vi = -vi, vr
    return [(sr + ur, si + ui), (tr + vr, ti + vi), (sr - ur, si - ui), (tr - vr, ti - vi)]


def scaled(x, angle):
    turn = angle / (0.5 * math.pi)
    xr, xi = x
    if abs(turn - round(turn)) < 1e-9:
        case = int(round(turn)) % 4
        return [(xr, xi), (-xi, xr), (-xr, -xi), (xi, -xr)][case]
    c, s = math.cos(angle), math.sin(angle)
    eighth = turn * 2
    if abs(eighth - round(eighth)) < 1e-9:
        case = int(round(eighth)) % 8
        h = math.sqrt(0.5)
        if case == 1:
            return ((xr - xi) * h, (xr + xi) * h)
        if case == 3:
            return ((xr + xi) * -h, (xr - xi) * h)
        if case == 5:
            return ((xi - xr) * h, (xr + xi) * -h)
        return ((xr + xi) * h, (xi - xr) * h)
    return (xr * c - xi * s, xr * s + xi * c)


def fft8(x, sign):
    even = fft4(x[0::2], sign)
    odd = fft4(x[1::2], sign)
    odd = [scaled(v, sign * 2.0 * math.pi * k / 8) for k, v in enumerate(odd)]
    first = [(a[0] + b[0], a[1] + b[1]) for a, b in zip(even, odd)]
    return first + [(a[0] - b[0], a[1] - b[1]) for a, b in zip(even, odd)]


def fft16(x, sign):
    inner = [fft4([x[4 * n1 + n2] for n1 in range(4)], sign) for n2 in range(4)]
    out = [None] * 16
    for k1 in range(4):
        column = [scaled(inner[n2][k1], sign * 2.0 * math.pi * n2 * k1 / 16) for n2 in range(4)]
        for k2, v in enumerate(fft4(column, sign)):
            out[k1 + 4 * k2] = v
    return out


def dot3(lhs, rhs, dims):
    left = jnp.concatenate([lhs[0], lhs[1], lhs[0]], axis=dims[0][0])
    right = jnp.concatenate([rhs[0], rhs[0], rhs[1]], axis=dims[1][0])
    return lax.dot_general(left, right, (dims, ((), ())), preferred_element_type=F32)


NN = ((1,), (0,))
NT = ((1,), (1,))
TN = ((0,), (0,))


LOGICAL = pl.DeviceIdType.LOGICAL


def enter(i, j):
    barrier = pltpu.get_barrier_semaphore()

    def signal(row, col):
        pl.semaphore_signal(barrier, inc=1, device_id=row * 16 + col, device_id_type=LOGICAL)

    for step in range(1, 16):
        signal(i, (j + step) % 16)
    for step in range(1, 8):
        signal((i + step) % 8, j)
    for row in (7, 1):
        for col in (15, 1):
            signal((i + row) % 8, (j + col) % 16)

    def down():
        pl.semaphore_wait(barrier, 26)

    return down


def send_group(c, me, source, landing, send_sem, recv_sem, local_sem):
    def remote(m):
        peer = (me + c + 8 * m) % 128
        pltpu.make_async_remote_copy(
            src_ref=source.at[peer],
            dst_ref=landing.at[me],
            send_sem=send_sem,
            recv_sem=recv_sem,
            device_id=peer,
            device_id_type=LOGICAL,
        ).start()

    @pl.when(c == 0)
    def _():
        pltpu.make_async_copy(source.at[me], landing.at[me], local_sem).start()

    @pl.when(c != 0)
    def _():
        remote(0)

    for m in range(1, 16):
        remote(m)


def wait_for(refs, sem):
    pltpu.make_async_copy(refs, refs, sem).wait()


def wait_all(landing, send_sem, recv_sem, local_sem):
    others = landing.at[pl.ds(0, landing.shape[0] - 1)]
    wait_for(landing.at[0], local_sem)
    wait_for(others, send_sem)
    wait_for(others, recv_sem)


def rows_forward(o, phase_ref, matrix_ref, twist_ref, out_ref, half_ref, hi_ref, lo_ref):
    step_c, step_s = twist_ref[0, 16:17, :128], twist_ref[1, 16:17, :128]
    for half in range(2):
        cols = pl.ds(half * 128, 128)
        field = []
        for j in range(16):
            field.append(cos_sin_quarters(2.0 * decode(phase_ref[o, j, :, cols])))
        spectrum = fft16(field, -1.0)
        for k1 in range(16):
            re, im = spectrum[k1]
            if k1 > 0:
                c = twist_ref[0, pl.ds(k1, 1), cols]
                s = twist_ref[1, pl.ds(k1, 1), cols]
                re, im = re * c - im * s, re * s + im * c
            rows = pl.ds(k1 * 16, 16)
            if half == 0:
                half_ref[0, rows, :] = re
                half_ref[1, rows, :] = im
                continue
            low_re, low_im = half_ref[0, rows, :], half_ref[1, rows, :]
            dre, dim = low_re - re, low_im - im
            even = (low_re + re, low_im + im)
            odd = (dre * step_c - dim * step_s, dre * step_s + dim * step_c)
            for parity, values in enumerate((even, odd)):
                rows = pl.ds(parity * 256 + k1 * 16, 16)
                for part, value in enumerate(values):
                    hi, lo = split(value)
                    place = pl.ds(part * 128, 128)
                    hi_ref[rows, place] = hi
                    lo_ref[rows, place] = lo
    for parity in range(2):
        rows = pl.ds(parity * 256, 256)
        result = dot3((matrix_ref[0], matrix_ref[1]), (hi_ref[rows, :], lo_ref[rows, :]), NT)
        for h in range(2):
            out_ref[pl.ds(parity * 32, 32), h, o] = encode(result[:, h * 128 : (h + 1) * 128]).reshape(32, 8, 128)


def transfer(o, me, wave, travel, cos_ref, sin_ref):
    row = lax.broadcasted_iota(jnp.int32, (8, 128), 0)
    lane = lax.broadcasted_iota(jnp.int32, (8, 128), 1)
    base_x = (row // 4) + 128 * (lane % 16)
    group = me // 2
    freq_y = 8 * (me % 2) + lane // 16 + 16 * (2 * (4 * (group % 32) + row % 4) + group // 32)
    signed_y = jnp.where(freq_y < 2048, freq_y, freq_y - 4096).astype(F32) * (1.0 / 4096)
    square_y = signed_y * signed_y

    def step(place, carry):
        freq_x = base_x + 2 * place
        signed_x = jnp.where(freq_x < 1024, freq_x, freq_x - 2048).astype(F32) * (1.0 / 2048)
        squared = signed_x * signed_x + square_y
        turns = travel * squared / (wave + jnp.sqrt(wave * wave - squared))
        c, w = cos_sin_quarters(4.0 * turns)
        cos_ref[o, place] = c
        sin_ref[o, place] = w
        return carry

    lax.fori_loop(0, 64, step, 0, unroll=4)


def put_split(place, re, im, hi_ref, lo_ref):
    for part, value in enumerate((re, im)):
        hi, lo = split(value)
        lanes = pl.ds(part * 128, 128)
        hi_ref[place, :, lanes] = hi
        lo_ref[place, :, lanes] = lo


def columns_in(n2, o, in_ref, pairs_ref, turns_ref, re_ref, im_ref):
    top = lax.broadcasted_iota(jnp.int32, (8, 128), 0) < 4
    column = []
    for n1 in range(8):
        s = 8 * n1 + n2
        a, b = decode(in_ref[s, o]), decode(in_ref[s + 64, o])
        total, delta = a + b, a - b
        re = jnp.where(top, total, pltpu.roll(delta, 4, 0))
        im = jnp.where(top, pltpu.roll(total, 4, 0), delta)
        c = jnp.where(top, 1.0, pairs_ref[0, s])
        w = jnp.where(top, 0.0, pairs_ref[1, s])
        column.append((re * c + im * w, im * c - re * w))
    for m1, (re, im) in enumerate(fft8(column, -1.0)):
        if m1 > 0:
            c, w = turns_ref[0, n2 * 8 + m1], turns_ref[1, n2 * 8 + m1]
            re, im = re * c + im * w, im * c - re * w
        re_ref[o, m1 * 8 + n2] = re
        im_ref[o, m1 * 8 + n2] = im


def columns(o, matrix_ref, back_ref, twist_ref, cos_ref, sin_ref, re_ref, im_ref, hi_ref, lo_ref):
    for m1 in range(8):
        column = [(re_ref[o, m1 * 8 + n2], im_ref[o, m1 * 8 + n2]) for n2 in range(8)]
        for m2, (re, im) in enumerate(fft8(column, -1.0)):
            place = m1 + 8 * m2
            c, w = twist_ref[0, place], twist_ref[1, place]
            put_split(place, re * c - im * w, re * w + im * c, hi_ref, lo_ref)
    data = (hi_ref[...].reshape(512, 256), lo_ref[...].reshape(512, 256))
    spectrum = dot3(data, (matrix_ref[0], matrix_ref[1]), NN).reshape(64, 8, 256)
    for place in range(64):
        c, w = cos_ref[o, place], sin_ref[o, place]
        re, im = spectrum[place, :, :128], spectrum[place, :, 128:]
        put_split(place, re * c + im * w, im * c - re * w, hi_ref, lo_ref)
    data = (hi_ref[...].reshape(512, 256), lo_ref[...].reshape(512, 256))
    spectrum = dot3(data, (back_ref[0], back_ref[1]), NN).reshape(64, 8, 256)
    for m1 in range(8):
        column = []
        for m2 in range(8):
            place = m1 + 8 * m2
            re, im = spectrum[place, :, :128], spectrum[place, :, 128:]
            c, w = twist_ref[0, place], twist_ref[1, place]
            column.append((re * c + im * w, im * c - re * w))
        for n2, v in enumerate(fft8(column, 1.0)):
            re, im = scaled(v, 2.0 * math.pi * n2 * m1 / 64)
            re_ref[o, m1 * 8 + n2] = re
            im_ref[o, m1 * 8 + n2] = im


def columns_out(n2, o, pairs_ref, re_ref, im_ref, out_ref):
    top = lax.broadcasted_iota(jnp.int32, (8, 128), 0) < 4
    column = [(re_ref[o, m1 * 8 + n2], im_ref[o, m1 * 8 + n2]) for m1 in range(8)]
    for n1, (re, im) in enumerate(fft8(column, 1.0)):
        s = 8 * n1 + n2
        c = jnp.where(top, 1.0, pairs_ref[0, s])
        w = jnp.where(top, 0.0, pairs_ref[1, s])
        re, im = re * c - im * w, im * c + re * w
        total = jnp.where(top, re, pltpu.roll(im, 4, 0))
        delta = jnp.where(top, pltpu.roll(re, 4, 0), im)
        out_ref[s, o] = encode(total + delta)
        out_ref[s + 64, o] = encode(total - delta)


def rows_inverse(o, hi_ref, lo_ref, matrix_ref, twist_ref, out_ref, value_ref):
    step_c, step_s = twist_ref[0, 16:17, :128], twist_ref[1, 16:17, :128]
    for h in range(2):
        hi, lo = hi_ref[:, h, o].reshape(512, 128), lo_ref[:, h, o].reshape(512, 128)
        rows = pl.ds(h * 128, 128)
        even = dot3((hi[:256], lo[:256]), (matrix_ref[0], matrix_ref[1]), TN)
        odd = dot3((hi[256:], lo[256:]), (matrix_ref[0], matrix_ref[1]), TN)
        re, im = odd[:, :128], odd[:, 128:]
        re, im = re * step_c + im * step_s, im * step_c - re * step_s
        value_ref[rows, 0:128] = even[:, :128] + re
        value_ref[rows, 128:256] = even[:, :128] - re
        value_ref[rows, 256:384] = even[:, 128:] + im
        value_ref[rows, 384:512] = even[:, 128:] - im
    for half in range(2):
        cols = pl.ds(half * 128, 128)
        spectrum = []
        for k1 in range(16):
            rows = pl.ds(k1 * 16, 16)
            re = value_ref[rows, cols] * 2.0**-13
            im = value_ref[rows, pl.ds(256 + half * 128, 128)] * 2.0**-13
            if k1 > 0:
                c = twist_ref[0, pl.ds(k1, 1), cols]
                s = twist_ref[1, pl.ds(k1, 1), cols]
                re, im = re * c + im * s, im * c - re * s
            spectrum.append((re, im))
        for j, field in enumerate(fft16(spectrum, 1.0)):
            for part in range(2):
                out_ref[o, part, :, pl.ds(j * 256 + half * 128, 128)] = field[part].astype(BF16)


EDGE_ROW = (0, 6, 3)


def band(weight_ref, band_ref):
    x = lax.broadcasted_iota(jnp.int32, (32, 128), 0)
    lane = lax.broadcasted_iota(jnp.int32, (32, 128), 1)
    shift = lane % 64 - x - 15
    upper = lane < 64
    row = lax.broadcasted_iota(jnp.int32, (16, 128), 0)
    beyond = [(lane[:16] % 64 == source, u) for source, u in ((16, 2), (47, 0))]
    for pair in range(8):
        columns_of = pl.ds(pair * 128, 128)
        edges = [jnp.zeros((16, 128), F32), jnp.zeros((16, 128), F32)]
        for o in range(3):
            weights = [weight_ref[o, u].astype(F32) for u in range(3)]
            for v in range(3):
                value = jnp.zeros((32, 128), F32)
                for u in range(3):
                    c = 2 * pair
                    a = jnp.broadcast_to(weights[u][v : v + 1, c : c + 1], (32, 128))
                    b = jnp.broadcast_to(weights[u][v : v + 1, c + 1 : c + 2], (32, 128))
                    both = jnp.where(upper, a, b)
                    value = jnp.where(shift == u, both, value)
                    for n, (here, edge_u) in enumerate(beyond):
                        if u == edge_u:
                            edges[n] = jnp.where(here & (row == EDGE_ROW[v] + o), both[:16], edges[n])
                band_ref[(v * 3 + o) * 32 : (v * 3 + o) * 32 + 32, columns_of] = value.astype(BF16)
        for n in range(2):
            band_ref[288 + 16 * n : 304 + 16 * n, columns_of] = edges[n].astype(BF16)


PHASE_ORDER = ((1, 0), (0, 1), (3, 0), (1, 1), (2, 0), (3, 1), (2, 1), (0, 0))


def head(i, j, weight_ref, bias_ref, band_ref, tile_ref, sums_ref, sides_ref, edges_ref, got_sides_ref, got_edges_ref, got_corners_ref, phase_ref, load, down, border_sems, send_phase, meanwhile):
    band(weight_ref, band_ref)
    load[0].wait()
    lane = lax.broadcasted_iota(jnp.int32, (32, 128), 1)
    tall = lax.broadcasted_iota(jnp.int32, (32, 128), 0)
    to_right = jnp.zeros((32, 128), F32)
    to_left = jnp.zeros((32, 128), F32)
    for k in range(8):
        if k == 3:
            load[1].wait()
        window = tile_ref[:, k * 32 : k * 32 + 64, :].reshape(1024, 256)
        count = 320 if k in (0, 7) else 288
        value = jnp.dot(band_ref[:count], window, preferred_element_type=F32)
        sums_ref[k] = value[:288].reshape(9, 32, 256)
        if k == 0:
            edges_ref[0] = value[288:304]
        if k == 7:
            edges_ref[1] = value[304:320]
        for o in range(3):
            to_right = jnp.where(lane == 3 * k + o, value[o * 32 : o * 32 + 32, 255:256], to_right)
            to_left = jnp.where(lane == 3 * k + o, value[192 + o * 32 : 224 + o * 32, 0:1], to_left)
    sides_ref[0] = to_right
    sides_ref[1] = to_left
    down()
    send_sems, recv_sems = border_sems
    copies = []
    for slot, step in enumerate((1, -1)):
        copies.append((sides_ref.at[slot], got_sides_ref.at[slot], i, (j + step + 16) % 16))
    for edge, down_step in enumerate((-1, 1)):
        row = (i + down_step + 8) % 8
        copies.append((edges_ref.at[edge], got_edges_ref.at[edge], row, j))
        for side, step in enumerate((1, -1)):
            corner = edges_ref.at[edge, pl.ds(0, 8), pl.ds(128 * (1 - side), 128)]
            copies.append((corner, got_corners_ref.at[edge * 2 + side], row, (j + step + 16) % 16))
    copies = [
        pltpu.make_async_remote_copy(
            src_ref=source, dst_ref=target, send_sem=send_sems.at[n], recv_sem=recv_sems.at[n],
            device_id=row * 16 + col, device_id_type=LOGICAL,
        )
        for n, (source, target, row, col) in enumerate(copies)
    ]
    for copy in copies:
        copy.start()
    meanwhile()
    for copy in copies:
        copy.wait()
    below, above = i < 7, i > 0
    left, right = j > 0, j < 15
    wide = lax.broadcasted_iota(jnp.int32, (32, 256), 1)
    row = lax.broadcasted_iota(jnp.int32, (8, 256), 0)
    for edge, (k, rows, here) in enumerate(((7, pl.ds(24, 8), (row == 7) & below), (0, pl.ds(0, 8), (row == 0) & above))):
        for v in range(3):
            for o in range(3):
                beyond = got_edges_ref[edge, pl.ds(EDGE_ROW[v] + o, 1), :]
                sums_ref[k, v * 3 + o, rows, :] += jnp.where(here, beyond, 0.0)
    for side, there in enumerate((left, right)):
        column = got_sides_ref[side]
        for edge, (k, x, inside) in enumerate(((7, 31, below), (0, 0, above))):
            corners = got_corners_ref[edge * 2 + side]
            for o in range(3):
                y = 127 * (1 - side)
                corner = corners[EDGE_ROW[2 * side] + o : EDGE_ROW[2 * side] + o + 1, y : y + 1]
                here = (lane == 3 * k + o) & (tall == x) & inside
                column = column + jnp.where(here, corner, 0.0)
        got_sides_ref[side] = jnp.where(there, column, 0.0)

    turn = 1 - 2 * (j % 2)
    for o in range(3):

        def block(k):
            index = 3 * k + o
            before = pltpu.roll(got_sides_ref[0], (128 - index) % 128, 1)
            after = pltpu.roll(got_sides_ref[1], 127 - index, 1)
            first = pltpu.roll(sums_ref[k, o], 1, 1)
            last = pltpu.roll(sums_ref[k, 6 + o], 255, 1)
            first = jnp.where(wide == 0, jnp.concatenate([before, before], 1), first)
            last = jnp.where(wide == 255, jnp.concatenate([after, after], 1), last)
            value = encode(jnp.tanh(first + last + (sums_ref[k, 3 + o] + bias_ref[o])))
            phase_ref[o, 2 * k] = value[:16]
            phase_ref[o, 2 * k + 1] = value[16:]
            send_phase(o, 2 * k)
            send_phase(o, 2 * k + 1)

        for x_step, z_step in PHASE_ORDER:
            block(((j // 8 + z_step) % 2) * 4 + (j // 2 + turn * x_step) % 4)


def spectral_kernel(
    weight_ref, bias_ref, wave_ref, travel_ref, pairs_ref, turns_ref, features_ref,
    forward_hbm, lanes_hbm, back_hbm, twist_x_hbm, twist_y_ref,
    high_ref, low_ref,
    forward_ref, lanes_ref, back_ref, twist_x_ref,
    tile_ref, band_ref, sums_ref, sides_ref, edges_ref, got_sides_ref, got_edges_ref, got_corners_ref, phase_ref, got_phase_ref,
    packets_ref, spread_in_ref, filtered_ref, returned_ref, cos_ref, sin_ref, re_ref, im_ref, hi_ref, lo_ref, half_ref, field_hi_ref, field_lo_ref,
    tile_sem, table_sems, border_send, border_recv, send_sems, recv_sems, local_sems, group_sems,
):
    colors = 3
    i, j = lax.axis_index("row"), lax.axis_index("col")
    me = i * 16 + j
    load = [
        pltpu.make_async_copy(features_ref.at[:, pl.ds(128 * n, 128), :], tile_ref.at[:, pl.ds(16 + 128 * n, 128), :], tile_sem.at[n])
        for n in range(2)
    ]
    for part in load:
        part.start()
    down = enter(i, j)
    tables_in = []
    for n, (source, target) in enumerate(((forward_hbm, forward_ref), (lanes_hbm, lanes_ref), (back_hbm, back_ref), (twist_x_hbm, twist_x_ref))):
        tables_in.append(pltpu.make_async_copy(source, target, table_sems.at[n]))
        tables_in[n].start()
    tile_ref[:, 0:16, :] = jnp.zeros((16, 16, 256), BF16)
    tile_ref[:, 272:288, :] = jnp.zeros((16, 16, 256), BF16)

    def each(body):
        def step(o, carry):
            body(o)
            return carry

        lax.fori_loop(0, colors, step, 0)

    def send_phase(o, peer):
        n = 2 + o

        @pl.when(peer == j)
        def _():
            pltpu.make_async_copy(phase_ref.at[o, peer], got_phase_ref.at[o, j], local_sems.at[n]).start()

        @pl.when(peer != j)
        def _():
            pltpu.make_async_remote_copy(
                src_ref=phase_ref.at[o, peer], dst_ref=got_phase_ref.at[o, j], send_sem=send_sems.at[n], recv_sem=recv_sems.at[n],
                device_id=i * 16 + peer, device_id_type=LOGICAL,
            ).start()

    head(
        i, j, weight_ref, bias_ref, band_ref, tile_ref, sums_ref, sides_ref, edges_ref, got_sides_ref, got_edges_ref, got_corners_ref, phase_ref,
        load, down, (border_send, border_recv), send_phase,
        lambda: each(lambda o: transfer(o, me, wave_ref[o], travel_ref[0], cos_ref, sin_ref)),
    )

    by_pair = packets_ref.reshape(64, 2, colors, 8, 128)

    def forward(o):
        wait_all(got_phase_ref.at[o], send_sems.at[2 + o], recv_sems.at[2 + o], local_sems.at[2 + o])
        rows_forward(o, got_phase_ref, forward_ref, twist_y_ref, by_pair, half_ref, field_hi_ref, field_lo_ref)

    tables_in[0].wait()
    each(forward)

    def groups(body):
        def step(c, carry):
            body(c)
            return carry

        lax.fori_loop(0, 8, step, 0)

    groups(lambda c: send_group(c, me, packets_ref, spread_in_ref, send_sems.at[0], group_sems.at[c], local_sems.at[0]))

    def wait_group(c, landing, local_sem, sem):
        @pl.when(c == 0)
        def _():
            wait_for(landing.at[0], local_sem)
            wait_for(landing.at[pl.ds(0, 15)], sem)

        @pl.when(c != 0)
        def _():
            wait_for(landing.at[pl.ds(0, 16)], sem)

    def arrive(c):
        wait_group(c, spread_in_ref, local_sems.at[0], group_sems.at[c])
        for o in range(colors):
            columns_in((me - c + 8) % 8, o, spread_in_ref, pairs_ref, turns_ref, re_ref, im_ref)

    def leave(c):
        for o in range(colors):
            columns_out((me + c) % 8, o, pairs_ref, re_ref, im_ref, filtered_ref)
        send_group(c, me, filtered_ref, returned_ref, send_sems.at[1], group_sems.at[8 + c], local_sems.at[1])

    groups(arrive)
    for table in tables_in[1:]:
        table.wait()
    each(lambda o: columns(o, lanes_ref, back_ref, twist_x_ref, cos_ref, sin_ref, re_ref, im_ref, hi_ref, lo_ref))
    groups(leave)
    wait_for(packets_ref.at[pl.ds(0, 127)], send_sems.at[0])

    def finish(c):
        wait_group(c, returned_ref, local_sems.at[1], group_sems.at[8 + c])
        for m in range(16):
            d = (me - c + 8 * m + 8) % 128
            high_ref[d], low_ref[d] = split(decode(returned_ref[d]))

    groups(finish)
    wait_for(filtered_ref.at[pl.ds(0, 127)], send_sems.at[1])


def rows_inverse_kernel(hi_ref, lo_ref, matrix_ref, twist_ref, out_ref, value_ref, result_ref, sems):
    colors = result_ref.shape[0]
    by_pair = [ref.reshape(64, 2, colors, 8, 128) for ref in (hi_ref, lo_ref)]

    def step(o, carry):
        rows_inverse(o, *by_pair, matrix_ref, twist_ref, result_ref, value_ref)
        pltpu.make_async_copy(result_ref.at[o], out_ref.at[o], sems.at[o]).start()
        return carry

    lax.fori_loop(0, colors, step, 0)
    for o in range(colors):
        pltpu.make_async_copy(result_ref.at[o], out_ref.at[o], sems.at[o]).wait()


def per_device(features, conv_weight, bias, wave, travel):
    table = tables()
    colors = 3
    names = ("forward_y", "lanes", "lanes_back", "twist_x", "twist_y")
    args = [jnp.asarray(table[k]) for k in names]
    smem = pl.BlockSpec(memory_space=pltpu.SMEM)
    vmem = pl.BlockSpec(memory_space=pltpu.VMEM)
    exchange = pltpu.VMEM((128, colors, 8, 128), BF16)
    high, low = pl.pallas_call(
        spectral_kernel,
        in_specs=[vmem] + [smem] * 5 + [pl.BlockSpec(memory_space=pl.ANY)] * 5 + [vmem],
        out_specs=[vmem] * 2,
        out_shape=[pltpu.VMEM((128, colors, 8, 128), BF16)] * 2,
        scratch_shapes=[
            *(pltpu.VMEM(a.shape, a.dtype) for a in args[:4]),
            pltpu.VMEM((16, 288, 256), BF16),
            pltpu.VMEM((320, 1024), BF16),
            pltpu.VMEM((8, 9, 32, 256), F32),
            pltpu.VMEM((2, 32, 128), F32),
            pltpu.VMEM((2, 16, 256), F32),
            pltpu.VMEM((2, 32, 128), F32),
            pltpu.VMEM((2, 16, 256), F32),
            pltpu.VMEM((4, 8, 128), F32),
            pltpu.VMEM((colors, 16, 16, 256), BF16),
            pltpu.VMEM((colors, 16, 16, 256), BF16),
            exchange, exchange, exchange, exchange,
            pltpu.VMEM((colors, 64, 8, 128), F32),
            pltpu.VMEM((colors, 64, 8, 128), F32),
            pltpu.VMEM((colors, 64, 8, 128), F32),
            pltpu.VMEM((colors, 64, 8, 128), F32),
            pltpu.VMEM((64, 8, 256), BF16),
            pltpu.VMEM((64, 8, 256), BF16),
            pltpu.VMEM((2, 256, 128), F32),
            pltpu.VMEM((512, 256), BF16),
            pltpu.VMEM((512, 256), BF16),
            pltpu.SemaphoreType.DMA((2,)),
            pltpu.SemaphoreType.DMA((4,)),
            pltpu.SemaphoreType.DMA((8,)),
            pltpu.SemaphoreType.DMA((8,)),
            pltpu.SemaphoreType.DMA((5,)),
            pltpu.SemaphoreType.DMA((5,)),
            pltpu.SemaphoreType.DMA((5,)),
            pltpu.SemaphoreType.DMA((16,)),
        ],
        compiler_params=pltpu.CompilerParams(collective_id=0, has_side_effects=True, vmem_limit_bytes=VMEM_LIMIT),
        name="spectral",
    )(conv_weight.transpose(0, 2, 3, 1), bias, wave, travel, jnp.asarray(table["pairs"]), jnp.asarray(table["turns"]), features, *args)
    return pl.pallas_call(
        rows_inverse_kernel,
        in_specs=[vmem] * 4,
        out_specs=pl.BlockSpec(memory_space=pl.ANY),
        out_shape=jax.ShapeDtypeStruct((colors, 2, 16, 4096), BF16),
        scratch_shapes=[
            pltpu.VMEM((256, 512), F32),
            pltpu.VMEM((colors, 2, 16, 4096), BF16),
            pltpu.SemaphoreType.DMA((colors,)),
        ],
        compiler_params=pltpu.CompilerParams(vmem_limit_bytes=16 * 1024 * 1024),
        name="rows_inverse",
    )(high, low, args[0], args[4])


def solution(mesh):
    in_specs = (P(None, "row", "col"), P(), P(), P(), P())
    out_specs = P(None, None, ("row", "col"), None)
    return jax.shard_map(
        per_device, mesh=mesh, in_specs=in_specs, out_specs=out_specs, check_vma=False
    )
```

```python
import functools
import math

import jax
import jax.numpy as jnp
import numpy as np
from jax import lax
from jax.experimental import pallas as pl
from jax.experimental.pallas import tpu as pltpu
from jax.sharding import PartitionSpec as P

F32 = jnp.float32
BF16 = jnp.bfloat16
VMEM_LIMIT = 56 * 1024 * 1024


def split_np(table):
    hi = table.astype(np.float32).astype(jnp.bfloat16)
    lo = (table - hi.astype(np.float64)).astype(np.float32).astype(jnp.bfloat16)
    return np.stack([np.asarray(hi), np.asarray(lo)])


def rotation_np(theta):
    return np.array([[np.cos(theta), np.sin(theta)], [-np.sin(theta), np.cos(theta)]])


def tables():
    b = np.arange(256)
    m = np.arange(128)
    rot = rotation_np(2.0 * np.pi * ((m[:, None] * m[None, :]) % 128) / 128.0)
    forward_y = rot.reshape(2, 2, 32, 4, 128).transpose(2, 0, 3, 1, 4).reshape(256, 256)
    j = np.arange(16)
    rot16 = rotation_np(2.0 * np.pi * ((j[:, None] * j[None, :]) % 16) / 16.0)
    back16 = np.stack([np.stack([rot16[0, 0], -rot16[0, 1]]), np.stack([-rot16[1, 0], rot16[1, 1]])])
    lanes = np.einsum("pqab,cd->qcbpda", rot16, np.eye(8)).reshape(256, 256)
    lanes_back = np.einsum("pqab,cd->qcbpda", back16, np.eye(8)).reshape(256, 256)
    k1 = np.minimum(np.arange(24), 16)
    angle = 2.0 * np.pi * ((k1[:, None] * b[None, :]) % 4096) / 4096.0
    twist_y = np.stack([np.cos(angle), -np.sin(angle)]).astype(np.float32)
    p = np.arange(128).reshape(64, 2)
    r = np.arange(16)
    angle = 2.0 * np.pi * ((p[:, :, None] * r) % 2048) / 2048.0
    twist_x = np.stack([np.cos(angle), -np.sin(angle)])
    twist_x = np.broadcast_to(twist_x[:, :, :, None, None, :], (2, 64, 2, 4, 8, 16))
    twist_x = twist_x.reshape(2, 64, 8, 128).astype(np.float32)
    s = np.arange(64)
    pairs = np.stack([np.cos(2.0 * np.pi * s / 128), np.sin(2.0 * np.pi * s / 128)]).astype(np.float32)
    turn = 2.0 * np.pi * ((s // 8) * (s % 8)) / 64.0
    turns = np.stack([np.cos(turn), np.sin(turn)]).astype(np.float32)
    return {
        "pairs": pairs,
        "turns": turns,
        "forward_y": split_np(forward_y * 8.0),
        "lanes": split_np(lanes),
        "lanes_back": split_np(lanes_back * 2.0**-16),
        "twist_y": twist_y,
        "twist_x": twist_x,
    }


def encode(x):
    x = x * jnp.abs(x)
    x = x * jnp.abs(x)
    x = x * jnp.abs(x)
    return x.astype(BF16)


def decode(y):
    y = y.astype(F32)
    root = jnp.exp2(jnp.log2(jnp.abs(y)) * 0.125)
    return jnp.where(y < 0.0, -root, root)


def split(x):
    hi = x.astype(BF16)
    return hi, (x - hi.astype(F32)).astype(BF16)


def cos_sin_quarters(u):
    n = jnp.round(u)
    f = u - n
    n = n.astype(jnp.int32)
    z = f * f
    s = f * (1.5707963267948966 + z * (-0.6459640975062462 + z * (0.07969262624616703 + z * (-0.004681754135318688 + z * 0.00016044118478735982))))
    c = 1.0 + z * (-1.2337005501361697 + z * (0.253669507901048 + z * (-0.020863480763352960 + z * (0.0009192602748394265 - z * 2.5202042373060605e-05))))
    swap = (n & 1) == 1
    cos = jnp.where(swap, s, c)
    sin = jnp.where(swap, c, s)
    cos = jnp.where(((n + 1) & 2) == 2, -cos, cos)
    sin = jnp.where((n & 2) == 2, -sin, sin)
    return cos, sin


def fft4(x, sign):
    (ar, ai), (br, bi), (cr, ci), (dr, di) = x
    sr, si, tr, ti = ar + cr, ai + ci, ar - cr, ai - ci
    ur, ui, vr, vi = br + dr, bi + di, br - dr, bi - di
    if sign < 0:
        vr, vi = vi, -vr
    else:
        vr, vi = -vi, vr
    return [(sr + ur, si + ui), (tr + vr, ti + vi), (sr - ur, si - ui), (tr - vr, ti - vi)]


def scaled(x, angle):
    turn = angle / (0.5 * math.pi)
    xr, xi = x
    if abs(turn - round(turn)) < 1e-9:
        case = int(round(turn)) % 4
        return [(xr, xi), (-xi, xr), (-xr, -xi), (xi, -xr)][case]
    c, s = math.cos(angle), math.sin(angle)
    eighth = turn * 2
    if abs(eighth - round(eighth)) < 1e-9:
        case = int(round(eighth)) % 8
        h = math.sqrt(0.5)
        if case == 1:
            return ((xr - xi) * h, (xr + xi) * h)
        if case == 3:
            return ((xr + xi) * -h, (xr - xi) * h)
        if case == 5:
            return ((xi - xr) * h, (xr + xi) * -h)
        return ((xr + xi) * h, (xi - xr) * h)
    return (xr * c - xi * s, xr * s + xi * c)


def fft8(x, sign):
    even = fft4(x[0::2], sign)
    odd = fft4(x[1::2], sign)
    odd = [scaled(v, sign * 2.0 * math.pi * k / 8) for k, v in enumerate(odd)]
    first = [(a[0] + b[0], a[1] + b[1]) for a, b in zip(even, odd)]
    return first + [(a[0] - b[0], a[1] - b[1]) for a, b in zip(even, odd)]


def fft16(x, sign):
    inner = [fft4([x[4 * n1 + n2] for n1 in range(4)], sign) for n2 in range(4)]
    out = [None] * 16
    for k1 in range(4):
        column = [scaled(inner[n2][k1], sign * 2.0 * math.pi * n2 * k1 / 16) for n2 in range(4)]
        for k2, v in enumerate(fft4(column, sign)):
            out[k1 + 4 * k2] = v
    return out


def dot3(lhs, rhs, dims):
    left = jnp.concatenate([lhs[0], lhs[1], lhs[0]], axis=dims[0][0])
    right = jnp.concatenate([rhs[0], rhs[0], rhs[1]], axis=dims[1][0])
    return lax.dot_general(left, right, (dims, ((), ())), preferred_element_type=F32)


NN = ((1,), (0,))
NT = ((1,), (1,))
TN = ((0,), (0,))


LOGICAL = pl.DeviceIdType.LOGICAL


def enter(i, j):
    barrier = pltpu.get_barrier_semaphore()

    def signal(row, col):
        pl.semaphore_signal(barrier, inc=1, device_id=row * 16 + col, device_id_type=LOGICAL)

    for step in range(1, 16):
        signal(i, (j + step) % 16)
    for step in range(1, 8):
        signal((i + step) % 8, j)
    for row in (7, 1):
        for col in (15, 1):
            signal((i + row) % 8, (j + col) % 16)

    def down():
        pl.semaphore_wait(barrier, 26)

    return down


def send_group(c, me, source, landing, send_sem, recv_sem, local_sem):
    def remote(m):
        peer = (me + c + 8 * m) % 128
        pltpu.make_async_remote_copy(
            src_ref=source.at[peer],
            dst_ref=landing.at[me],
            send_sem=send_sem,
            recv_sem=recv_sem,
            device_id=peer,
            device_id_type=LOGICAL,
        ).start()

    @pl.when(c == 0)
    def _():
        pltpu.make_async_copy(source.at[me], landing.at[me], local_sem).start()

    @pl.when(c != 0)
    def _():
        remote(0)

    for m in range(1, 16):
        remote(m)


def wait_for(refs, sem):
    pltpu.make_async_copy(refs, refs, sem).wait()


def wait_all(landing, send_sem, recv_sem, local_sem):
    others = landing.at[pl.ds(0, landing.shape[0] - 1)]
    wait_for(landing.at[0], local_sem)
    wait_for(others, send_sem)
    wait_for(others, recv_sem)


def rows_forward(o, phase_ref, matrix_ref, twist_ref, out_ref, half_ref, hi_ref, lo_ref):
    step_c, step_s = twist_ref[0, 16:17, :128], twist_ref[1, 16:17, :128]
    for half in range(2):
        cols = pl.ds(half * 128, 128)
        field = []
        for j in range(16):
            field.append(cos_sin_quarters(2.0 * decode(phase_ref[o, j, :, cols])))
        spectrum = fft16(field, -1.0)
        for k1 in range(16):
            re, im = spectrum[k1]
            if k1 > 0:
                c = twist_ref[0, pl.ds(k1, 1), cols]
                s = twist_ref[1, pl.ds(k1, 1), cols]
                re, im = re * c - im * s, re * s + im * c
            rows = pl.ds(k1 * 16, 16)
            if half == 0:
                half_ref[0, rows, :] = re
                half_ref[1, rows, :] = im
                continue
            low_re, low_im = half_ref[0, rows, :], half_ref[1, rows, :]
            dre, dim = low_re - re, low_im - im
            even = (low_re + re, low_im + im)
            odd = (dre * step_c - dim * step_s, dre * step_s + dim * step_c)
            for parity, values in enumerate((even, odd)):
                rows = pl.ds(parity * 256 + k1 * 16, 16)
                for part, value in enumerate(values):
                    hi, lo = split(value)
                    place = pl.ds(part * 128, 128)
                    hi_ref[rows, place] = hi
                    lo_ref[rows, place] = lo
    for parity in range(2):
        rows = pl.ds(parity * 256, 256)
        result = dot3((matrix_ref[0], matrix_ref[1]), (hi_ref[rows, :], lo_ref[rows, :]), NT)
        for h in range(2):
            out_ref[pl.ds(parity * 32, 32), h, o] = encode(result[:, h * 128 : (h + 1) * 128]).reshape(32, 8, 128)


def transfer(o, me, wave, travel, cos_ref, sin_ref):
    row = lax.broadcasted_iota(jnp.int32, (8, 128), 0)
    lane = lax.broadcasted_iota(jnp.int32, (8, 128), 1)
    base_x = (row // 4) + 128 * (lane % 16)
    group = me // 2
    freq_y = 8 * (me % 2) + lane // 16 + 16 * (2 * (4 * (group % 32) + row % 4) + group // 32)
    signed_y = jnp.where(freq_y < 2048, freq_y, freq_y - 4096).astype(F32) * (1.0 / 4096)
    square_y = signed_y * signed_y

    def step(place, carry):
        freq_x = base_x + 2 * place
        signed_x = jnp.where(freq_x < 1024, freq_x, freq_x - 2048).astype(F32) * (1.0 / 2048)
        squared = signed_x * signed_x + square_y
        turns = travel * squared / (wave + jnp.sqrt(wave * wave - squared))
        c, w = cos_sin_quarters(4.0 * turns)
        cos_ref[o, place] = c
        sin_ref[o, place] = w
        return carry

    lax.fori_loop(0, 64, step, 0, unroll=4)


def put_split(place, re, im, hi_ref, lo_ref):
    for part, value in enumerate((re, im)):
        hi, lo = split(value)
        lanes = pl.ds(part * 128, 128)
        hi_ref[place, :, lanes] = hi
        lo_ref[place, :, lanes] = lo


def columns_in(n2, o, in_ref, pairs_ref, turns_ref, re_ref, im_ref):
    top = lax.broadcasted_iota(jnp.int32, (8, 128), 0) < 4
    column = []
    for n1 in range(8):
        s = 8 * n1 + n2
        a, b = decode(in_ref[s, o]), decode(in_ref[s + 64, o])
        total, delta = a + b, a - b
        re = jnp.where(top, total, pltpu.roll(delta, 4, 0))
        im = jnp.where(top, pltpu.roll(total, 4, 0), delta)
        c = jnp.where(top, 1.0, pairs_ref[0, s])
        w = jnp.where(top, 0.0, pairs_ref[1, s])
        column.append((re * c + im * w, im * c - re * w))
    for m1, (re, im) in enumerate(fft8(column, -1.0)):
        if m1 > 0:
            c, w = turns_ref[0, n2 * 8 + m1], turns_ref[1, n2 * 8 + m1]
            re, im = re * c + im * w, im * c - re * w
        re_ref[o, m1 * 8 + n2] = re
        im_ref[o, m1 * 8 + n2] = im


def columns(o, matrix_ref, back_ref, twist_ref, cos_ref, sin_ref, re_ref, im_ref, hi_ref, lo_ref):
    for m1 in range(8):
        column = [(re_ref[o, m1 * 8 + n2], im_ref[o, m1 * 8 + n2]) for n2 in range(8)]
        for m2, (re, im) in enumerate(fft8(column, -1.0)):
            place = m1 + 8 * m2
            c, w = twist_ref[0, place], twist_ref[1, place]
            put_split(place, re * c - im * w, re * w + im * c, hi_ref, lo_ref)
    data = (hi_ref[...].reshape(512, 256), lo_ref[...].reshape(512, 256))
    spectrum = dot3(data, (matrix_ref[0], matrix_ref[1]), NN).reshape(64, 8, 256)
    for place in range(64):
        c, w = cos_ref[o, place], sin_ref[o, place]
        re, im = spectrum[place, :, :128], spectrum[place, :, 128:]
        put_split(place, re * c + im * w, im * c - re * w, hi_ref, lo_ref)
    data = (hi_ref[...].reshape(512, 256), lo_ref[...].reshape(512, 256))
    spectrum = dot3(data, (back_ref[0], back_ref[1]), NN).reshape(64, 8, 256)
    for m1 in range(8):
        column = []
        for m2 in range(8):
            place = m1 + 8 * m2
            re, im = spectrum[place, :, :128], spectrum[place, :, 128:]
            c, w = twist_ref[0, place], twist_ref[1, place]
            column.append((re * c + im * w, im * c - re * w))
        for n2, v in enumerate(fft8(column, 1.0)):
            re, im = scaled(v, 2.0 * math.pi * n2 * m1 / 64)
            re_ref[o, m1 * 8 + n2] = re
            im_ref[o, m1 * 8 + n2] = im


def columns_out(n2, o, pairs_ref, re_ref, im_ref, out_ref):
    top = lax.broadcasted_iota(jnp.int32, (8, 128), 0) < 4
    column = [(re_ref[o, m1 * 8 + n2], im_ref[o, m1 * 8 + n2]) for m1 in range(8)]
    for n1, (re, im) in enumerate(fft8(column, 1.0)):
        s = 8 * n1 + n2
        c = jnp.where(top, 1.0, pairs_ref[0, s])
        w = jnp.where(top, 0.0, pairs_ref[1, s])
        re, im = re * c - im * w, im * c + re * w
        total = jnp.where(top, re, pltpu.roll(im, 4, 0))
        delta = jnp.where(top, pltpu.roll(re, 4, 0), im)
        out_ref[s, o] = encode(total + delta)
        out_ref[s + 64, o] = encode(total - delta)


def rows_inverse(o, hi_ref, lo_ref, matrix_ref, twist_ref, out_ref, value_ref):
    step_c, step_s = twist_ref[0, 16:17, :128], twist_ref[1, 16:17, :128]
    for h in range(2):
        hi, lo = hi_ref[:, h, o].reshape(512, 128), lo_ref[:, h, o].reshape(512, 128)
        rows = pl.ds(h * 128, 128)
        even = dot3((hi[:256], lo[:256]), (matrix_ref[0], matrix_ref[1]), TN)
        odd = dot3((hi[256:], lo[256:]), (matrix_ref[0], matrix_ref[1]), TN)
        re, im = odd[:, :128], odd[:, 128:]
        re, im = re * step_c + im * step_s, im * step_c - re * step_s
        value_ref[rows, 0:128] = even[:, :128] + re
        value_ref[rows, 128:256] = even[:, :128] - re
        value_ref[rows, 256:384] = even[:, 128:] + im
        value_ref[rows, 384:512] = even[:, 128:] - im
    for half in range(2):
        cols = pl.ds(half * 128, 128)
        spectrum = []
        for k1 in range(16):
            rows = pl.ds(k1 * 16, 16)
            re = value_ref[rows, cols] * 2.0**-13
            im = value_ref[rows, pl.ds(256 + half * 128, 128)] * 2.0**-13
            if k1 > 0:
                c = twist_ref[0, pl.ds(k1, 1), cols]
                s = twist_ref[1, pl.ds(k1, 1), cols]
                re, im = re * c + im * s, im * c - re * s
            spectrum.append((re, im))
        for j, field in enumerate(fft16(spectrum, 1.0)):
            for part in range(2):
                out_ref[o, part, :, pl.ds(j * 256 + half * 128, 128)] = field[part].astype(BF16)


EDGE_ROW = (0, 6, 3)


def band(weight_ref, band_ref):
    x = lax.broadcasted_iota(jnp.int32, (32, 128), 0)
    lane = lax.broadcasted_iota(jnp.int32, (32, 128), 1)
    shift = lane % 64 - x - 15
    upper = lane < 64
    row = lax.broadcasted_iota(jnp.int32, (16, 128), 0)
    beyond = [(lane[:16] % 64 == source, u) for source, u in ((16, 2), (47, 0))]
    for pair in range(8):
        columns_of = pl.ds(pair * 128, 128)
        edges = [jnp.zeros((16, 128), F32), jnp.zeros((16, 128), F32)]
        for o in range(3):
            weights = [weight_ref[o, u].astype(F32) for u in range(3)]
            for v in range(3):
                value = jnp.zeros((32, 128), F32)
                for u in range(3):
                    c = 2 * pair
                    a = jnp.broadcast_to(weights[u][v : v + 1, c : c + 1], (32, 128))
                    b = jnp.broadcast_to(weights[u][v : v + 1, c + 1 : c + 2], (32, 128))
                    both = jnp.where(upper, a, b)
                    value = jnp.where(shift == u, both, value)
                    for n, (here, edge_u) in enumerate(beyond):
                        if u == edge_u:
                            edges[n] = jnp.where(here & (row == EDGE_ROW[v] + o), both[:16], edges[n])
                band_ref[(v * 3 + o) * 32 : (v * 3 + o) * 32 + 32, columns_of] = value.astype(BF16)
        for n in range(2):
            band_ref[288 + 16 * n : 304 + 16 * n, columns_of] = edges[n].astype(BF16)


PHASE_ORDER = ((1, 0), (0, 1), (3, 0), (1, 1), (2, 0), (3, 1), (2, 1), (0, 0))


def head(i, j, weight_ref, bias_ref, band_ref, tile_ref, sums_ref, sides_ref, edges_ref, got_sides_ref, got_edges_ref, got_corners_ref, phase_ref, load, down, border_sems, send_phase, meanwhile):
    band(weight_ref, band_ref)
    load[0].wait()
    lane = lax.broadcasted_iota(jnp.int32, (32, 128), 1)
    tall = lax.broadcasted_iota(jnp.int32, (32, 128), 0)
    to_right = jnp.zeros((32, 128), F32)
    to_left = jnp.zeros((32, 128), F32)
    for k in range(8):
        if k == 3:
            load[1].wait()
        window = tile_ref[:, k * 32 : k * 32 + 64, :].reshape(1024, 256)
        count = 320 if k in (0, 7) else 288
        value = jnp.dot(band_ref[:count], window, preferred_element_type=F32)
        sums_ref[k] = value[:288].reshape(9, 32, 256)
        if k == 0:
            edges_ref[0] = value[288:304]
        if k == 7:
            edges_ref[1] = value[304:320]
        for o in range(3):
            to_right = jnp.where(lane == 3 * k + o, value[o * 32 : o * 32 + 32, 255:256], to_right)
            to_left = jnp.where(lane == 3 * k + o, value[192 + o * 32 : 224 + o * 32, 0:1], to_left)
    sides_ref[0] = to_right
    sides_ref[1] = to_left
    down()
    send_sems, recv_sems = border_sems
    copies = []
    for slot, step in enumerate((1, -1)):
        copies.append((sides_ref.at[slot], got_sides_ref.at[slot], i, (j + step + 16) % 16))
    for edge, down_step in enumerate((-1, 1)):
        row = (i + down_step + 8) % 8
        copies.append((edges_ref.at[edge], got_edges_ref.at[edge], row, j))
        for side, step in enumerate((1, -1)):
            corner = edges_ref.at[edge, pl.ds(0, 8), pl.ds(128 * (1 - side), 128)]
            copies.append((corner, got_corners_ref.at[edge * 2 + side], row, (j + step + 16) % 16))
    copies = [
        pltpu.make_async_remote_copy(
            src_ref=source, dst_ref=target, send_sem=send_sems.at[n], recv_sem=recv_sems.at[n],
            device_id=row * 16 + col, device_id_type=LOGICAL,
        )
        for n, (source, target, row, col) in enumerate(copies)
    ]
    for copy in copies:
        copy.start()
    meanwhile()
    for copy in copies:
        copy.wait()
    below, above = i < 7, i > 0
    left, right = j > 0, j < 15
    wide = lax.broadcasted_iota(jnp.int32, (32, 256), 1)
    row = lax.broadcasted_iota(jnp.int32, (8, 256), 0)
    for edge, (k, rows, here) in enumerate(((7, pl.ds(24, 8), (row == 7) & below), (0, pl.ds(0, 8), (row == 0) & above))):
        for v in range(3):
            for o in range(3):
                beyond = got_edges_ref[edge, pl.ds(EDGE_ROW[v] + o, 1), :]
                sums_ref[k, v * 3 + o, rows, :] += jnp.where(here, beyond, 0.0)
    for side, there in enumerate((left, right)):
        column = got_sides_ref[side]
        for edge, (k, x, inside) in enumerate(((7, 31, below), (0, 0, above))):
            corners = got_corners_ref[edge * 2 + side]
            for o in range(3):
                y = 127 * (1 - side)
                corner = corners[EDGE_ROW[2 * side] + o : EDGE_ROW[2 * side] + o + 1, y : y + 1]
                here = (lane == 3 * k + o) & (tall == x) & inside
                column = column + jnp.where(here, corner, 0.0)
        got_sides_ref[side] = jnp.where(there, column, 0.0)

    turn = 1 - 2 * (j % 2)
    for o in range(3):

        def block(k):
            index = 3 * k + o
            before = pltpu.roll(got_sides_ref[0], (128 - index) % 128, 1)
            after = pltpu.roll(got_sides_ref[1], 127 - index, 1)
            first = pltpu.roll(sums_ref[k, o], 1, 1)
            last = pltpu.roll(sums_ref[k, 6 + o], 255, 1)
            first = jnp.where(wide == 0, jnp.concatenate([before, before], 1), first)
            last = jnp.where(wide == 255, jnp.concatenate([after, after], 1), last)
            value = encode(jnp.tanh(first + last + (sums_ref[k, 3 + o] + bias_ref[o])))
            phase_ref[o, 2 * k] = value[:16]
            phase_ref[o, 2 * k + 1] = value[16:]
            send_phase(o, 2 * k)
            send_phase(o, 2 * k + 1)

        for x_step, z_step in PHASE_ORDER:
            block(((j // 8 + z_step) % 2) * 4 + (j // 2 + turn * x_step) % 4)


def spectral_kernel(
    weight_ref, bias_ref, wave_ref, travel_ref, pairs_ref, turns_ref, features_ref,
    forward_hbm, lanes_hbm, back_hbm, twist_x_hbm, twist_y_ref,
    high_ref, low_ref,
    forward_ref, lanes_ref, back_ref, twist_x_ref,
    tile_ref, band_ref, sums_ref, sides_ref, edges_ref, got_sides_ref, got_edges_ref, got_corners_ref, phase_ref, got_phase_ref,
    packets_ref, spread_in_ref, filtered_ref, returned_ref, cos_ref, sin_ref, re_ref, im_ref, hi_ref, lo_ref, half_ref, field_hi_ref, field_lo_ref,
    tile_sem, table_sems, border_send, border_recv, send_sems, recv_sems, local_sems, group_sems,
):
    colors = 3
    i, j = lax.axis_index("row"), lax.axis_index("col")
    me = i * 16 + j
    load = [
        pltpu.make_async_copy(features_ref.at[:, pl.ds(128 * n, 128), :], tile_ref.at[:, pl.ds(16 + 128 * n, 128), :], tile_sem.at[n])
        for n in range(2)
    ]
    for part in load:
        part.start()
    down = enter(i, j)
    tables_in = []
    for n, (source, target) in enumerate(((forward_hbm, forward_ref), (lanes_hbm, lanes_ref), (back_hbm, back_ref), (twist_x_hbm, twist_x_ref))):
        tables_in.append(pltpu.make_async_copy(source, target, table_sems.at[n]))
        tables_in[n].start()
    tile_ref[:, 0:16, :] = jnp.zeros((16, 16, 256), BF16)
    tile_ref[:, 272:288, :] = jnp.zeros((16, 16, 256), BF16)

    def each(body):
        def step(o, carry):
            body(o)
            return carry

        lax.fori_loop(0, colors, step, 0)

    def send_phase(o, peer):
        n = 2 + o

        @pl.when(peer == j)
        def _():
            pltpu.make_async_copy(phase_ref.at[o, peer], got_phase_ref.at[o, j], local_sems.at[n]).start()

        @pl.when(peer != j)
        def _():
            pltpu.make_async_remote_copy(
                src_ref=phase_ref.at[o, peer], dst_ref=got_phase_ref.at[o, j], send_sem=send_sems.at[n], recv_sem=recv_sems.at[n],
                device_id=i * 16 + peer, device_id_type=LOGICAL,
            ).start()

    head(
        i, j, weight_ref, bias_ref, band_ref, tile_ref, sums_ref, sides_ref, edges_ref, got_sides_ref, got_edges_ref, got_corners_ref, phase_ref,
        load, down, (border_send, border_recv), send_phase,
        lambda: each(lambda o: transfer(o, me, wave_ref[o], travel_ref[0], cos_ref, sin_ref)),
    )

    by_pair = packets_ref.reshape(64, 2, colors, 8, 128)

    def forward(o):
        wait_all(got_phase_ref.at[o], send_sems.at[2 + o], recv_sems.at[2 + o], local_sems.at[2 + o])
        rows_forward(o, got_phase_ref, forward_ref, twist_y_ref, by_pair, half_ref, field_hi_ref, field_lo_ref)

    tables_in[0].wait()
    each(forward)

    def groups(body):
        def step(c, carry):
            body(c)
            return carry

        lax.fori_loop(0, 8, step, 0)

    groups(lambda c: send_group(c, me, packets_ref, spread_in_ref, send_sems.at[0], group_sems.at[c], local_sems.at[0]))

    def wait_group(c, landing, local_sem, sem):
        @pl.when(c == 0)
        def _():
            wait_for(landing.at[0], local_sem)
            wait_for(landing.at[pl.ds(0, 15)], sem)

        @pl.when(c != 0)
        def _():
            wait_for(landing.at[pl.ds(0, 16)], sem)

    def arrive(c):
        wait_group(c, spread_in_ref, local_sems.at[0], group_sems.at[c])
        for o in range(colors):
            columns_in((me - c + 8) % 8, o, spread_in_ref, pairs_ref, turns_ref, re_ref, im_ref)

    def leave(c):
        for o in range(colors):
            columns_out((me + c) % 8, o, pairs_ref, re_ref, im_ref, filtered_ref)
        send_group(c, me, filtered_ref, returned_ref, send_sems.at[1], group_sems.at[8 + c], local_sems.at[1])

    groups(arrive)
    for table in tables_in[1:]:
        table.wait()
    for o in range(colors):
        columns(o, lanes_ref, back_ref, twist_x_ref, cos_ref, sin_ref, re_ref, im_ref, hi_ref.at[o], lo_ref.at[o])
    groups(leave)
    wait_for(packets_ref.at[pl.ds(0, 127)], send_sems.at[0])

    def finish(c):
        wait_group(c, returned_ref, local_sems.at[1], group_sems.at[8 + c])
        for m in range(16):
            d = (me - c + 8 * m + 8) % 128
            high_ref[d], low_ref[d] = split(decode(returned_ref[d]))

    groups(finish)
    wait_for(filtered_ref.at[pl.ds(0, 127)], send_sems.at[1])


def rows_inverse_kernel(hi_ref, lo_ref, matrix_ref, twist_ref, out_ref, value_ref, result_ref, sems):
    colors = result_ref.shape[0]
    by_pair = [ref.reshape(64, 2, colors, 8, 128) for ref in (hi_ref, lo_ref)]

    for o in range(colors):
        rows_inverse(o, *by_pair, matrix_ref, twist_ref, result_ref, value_ref.at[o])
        pltpu.make_async_copy(result_ref.at[o], out_ref.at[o], sems.at[o]).start()
    for o in range(colors):
        pltpu.make_async_copy(result_ref.at[o], out_ref.at[o], sems.at[o]).wait()


def per_device(features, conv_weight, bias, wave, travel):
    table = tables()
    colors = 3
    names = ("forward_y", "lanes", "lanes_back", "twist_x", "twist_y")
    args = [jnp.asarray(table[k]) for k in names]
    smem = pl.BlockSpec(memory_space=pltpu.SMEM)
    vmem = pl.BlockSpec(memory_space=pltpu.VMEM)
    exchange = pltpu.VMEM((128, colors, 8, 128), BF16)
    high, low = pl.pallas_call(
        spectral_kernel,
        in_specs=[vmem] + [smem] * 5 + [pl.BlockSpec(memory_space=pl.ANY)] * 5 + [vmem],
        out_specs=[vmem] * 2,
        out_shape=[pltpu.VMEM((128, colors, 8, 128), BF16)] * 2,
        scratch_shapes=[
            *(pltpu.VMEM(a.shape, a.dtype) for a in args[:4]),
            pltpu.VMEM((16, 288, 256), BF16),
            pltpu.VMEM((320, 1024), BF16),
            pltpu.VMEM((8, 9, 32, 256), F32),
            pltpu.VMEM((2, 32, 128), F32),
            pltpu.VMEM((2, 16, 256), F32),
            pltpu.VMEM((2, 32, 128), F32),
            pltpu.VMEM((2, 16, 256), F32),
            pltpu.VMEM((4, 8, 128), F32),
            pltpu.VMEM((colors, 16, 16, 256), BF16),
            pltpu.VMEM((colors, 16, 16, 256), BF16),
            exchange, exchange, exchange, exchange,
            pltpu.VMEM((colors, 64, 8, 128), F32),
            pltpu.VMEM((colors, 64, 8, 128), F32),
            pltpu.VMEM((colors, 64, 8, 128), F32),
            pltpu.VMEM((colors, 64, 8, 128), F32),
            pltpu.VMEM((colors, 64, 8, 256), BF16),
            pltpu.VMEM((colors, 64, 8, 256), BF16),
            pltpu.VMEM((2, 256, 128), F32),
            pltpu.VMEM((512, 256), BF16),
            pltpu.VMEM((512, 256), BF16),
            pltpu.SemaphoreType.DMA((2,)),
            pltpu.SemaphoreType.DMA((4,)),
            pltpu.SemaphoreType.DMA((8,)),
            pltpu.SemaphoreType.DMA((8,)),
            pltpu.SemaphoreType.DMA((5,)),
            pltpu.SemaphoreType.DMA((5,)),
            pltpu.SemaphoreType.DMA((5,)),
            pltpu.SemaphoreType.DMA((16,)),
        ],
        compiler_params=pltpu.CompilerParams(collective_id=0, has_side_effects=True, vmem_limit_bytes=VMEM_LIMIT),
        name="spectral",
    )(conv_weight.transpose(0, 2, 3, 1), bias, wave, travel, jnp.asarray(table["pairs"]), jnp.asarray(table["turns"]), features, *args)
    return pl.pallas_call(
        rows_inverse_kernel,
        in_specs=[vmem] * 4,
        out_specs=pl.BlockSpec(memory_space=pl.ANY),
        out_shape=jax.ShapeDtypeStruct((colors, 2, 16, 4096), BF16),
        scratch_shapes=[
            pltpu.VMEM((colors, 256, 512), F32),
            pltpu.VMEM((colors, 2, 16, 4096), BF16),
            pltpu.SemaphoreType.DMA((colors,)),
        ],
        compiler_params=pltpu.CompilerParams(vmem_limit_bytes=16 * 1024 * 1024),
        name="rows_inverse",
    )(high, low, args[0], args[4])


def solution(mesh):
    in_specs = (P(None, "row", "col"), P(), P(), P(), P())
    out_specs = P(None, None, ("row", "col"), None)
    return jax.shard_map(
        per_device, mesh=mesh, in_specs=in_specs, out_specs=out_specs, check_vma=False
    )
```
